128 devices in a mesh: mer: 16 (over x, z), box: 8 (over y, core).
Axes of the slice: x: 4, y: 4, z: 4, core: 2. Of those that a mesh axis runs over, the one named last changes fastest.
Arguments:
- annulus: float32 [25, 512, 2048], P(None, 'box', 'mer'), may hold values from -6 to 6
- annulus_prev: float32 [25, 512, 2048], P(None, 'box', 'mer'), may hold values from -6 to 6
- derivative: float32 [25, 25], replicated, may hold values from -1.25 to 1.25
- radial_modulus: float32 [25, 2048], P(None, 'mer'), may hold values from 0.5 to 2
- shear_modulus: float32 [25, 2048], P(None, 'mer'), may hold values from 0.5 to 2
- node_mass: float32 [25, 2048], P(None, 'mer'), may hold values from 1 to 4
- element_modes: int32 [2048], P('mer'), may hold values from 1 to 256
- upper_rows: int32 [4096], P('mer'), may hold values from 0 to 3199
- lower_rows: int32 [4096], P('mer'), may hold values from 0 to 3199
- coupling_rows: int32 [32768], P('mer'), may hold values from 0 to 3199
- coupling_target: int32 [32768, 1], P('mer'), may hold values from 0 to 127; in each aligned block of 2048 rows (0 to 2047, 2048 to 4095, ...) at most 32 rows name the same one
- box_field: float32 [131072], P(('mer', 'box')), may hold values from -6 to 6
- box_prev: float32 [131072], P(('mer', 'box')), may hold values from -6 to 6
- box_angle: float32 [131072], P(('mer', 'box')), may hold values from -3.140625 to 3.140625
- box_spring: float32 [131072], P(('mer', 'box')), may hold values from 0.5 to 2
- box_mass: float32 [131072], P(('mer', 'box')), may hold values from 1 to 4
- box_weight: float32 [131072], P(('mer', 'box')), may hold values from 0.05 to 0.5
- box_slot: int32 [131072], P(('mer', 'box')), may hold values from 0 to 511, as said below
Outputs:
- annulus_out: float32 [25, 512, 2048], P(None, 'box', 'mer')
- box_out: float32 [131072], P(('mer', 'box'))
The draws below stay inside these ranges and needn't reach their ends.
Inputs may be any that keep to these rules, and one draw needn't show every extreme that they name: `lower_rows`: part rows, paired with the previous part's upper rows. `coupling_target`: among the 2048 rows of one part no box part is named more than 32 times, and some box part exactly 32 times. `box_slot`: slot p * 16 + i of the node's box part: the p-th coupling row that part i sends there; slots that no row fills hold zeros. Among the 1024 nodes of one box part, exactly 64 read slots of each meridional part i.
All inputs are finite; a program needn't handle non-finite values.
Results may differ from the reference program's by a relative error of at most 0.0003.
Values sent between devices are 32-bit elements; how exact they have to be, the bound alone decides.
A program may use at most 128 MiB of HBM per device.

```python
import math
import jax
import jax.numpy as jnp
import numpy as np
from jax import lax

NODES = 25
MODES = 256
E_DEV = 128
SHB = 256
CPL = 2048
BN_DEV = 1024
STEPS = 2
ELEMS = 2048
CAP = 32
SLOTS = 512
BOXN = 131072
N_MER = 16
DEVICES = 128


def draw_box_slot(key, part):
    first = jax.random.fold_in(key, 11)
    second = jax.random.fold_in(key, 23)
    base = jnp.arange(BN_DEV, dtype=jnp.int32) % N_MER
    source = jax.vmap(lambda single: jax.random.permutation(single, base))(jax.random.split(first, DEVICES))
    places = jax.random.randint(second, (DEVICES, BN_DEV), 0, CAP, dtype=jnp.int32)
    return (places * N_MER + source).reshape(-1).astype(jnp.int32)


def touch_ends(array, key, least, top_value):
    dims = array.shape
    spot = [jax.random.randint(jax.random.fold_in(key, axis), (), 0, dims[axis]) for axis in range(len(dims))]
    array = array.at[tuple(spot)].set(least)
    longest = dims.index(max(dims))
    spot[longest] = (spot[longest] + 1) % dims[longest]
    return array.at[tuple(spot)].set(top_value)


def block_levels(own_key, dims, pieces, least, high):
    gain = 1.0
    for dim, blocks in pieces:
        steps = jax.random.uniform(jax.random.fold_in(jax.random.fold_in(own_key, 6), dim), (blocks,), jnp.float32, least / len(pieces), high / len(pieces))
        gain = gain * jnp.repeat(jnp.exp(steps), dims[dim] // blocks).reshape((-1,) + (1,) * (len(dims) - 1 - dim))
    return gain


def shared_out(own_key, own, number, rows, count, top, bound, lean):
    ranking = jax.random.permutation(own_key, count)
    heavy_load, common = portions_of(count, rows * top, bound, lean, True), portions_of(count, rows * top, bound, lean, False)
    places = jnp.arange(count)

    def named(lengths, turn):
        used = int((lengths > 0).sum())
        fixed = max(1, used // 4)
        shifted = fixed + (places - fixed + turn * (used - fixed)) % max(1, count - fixed)
        return jnp.zeros((count,), jnp.int32).at[ranking[jnp.where(places < fixed, places, shifted)]].set(jnp.asarray(lengths, jnp.int32))

    lengths = jnp.where(number % 4 == 0, named(heavy_load, number // 4), named(common, number - number // 4 - 1))
    mixed = jax.random.permutation(jax.random.fold_in(own, 3), count)
    giver, receiver = mixed[0:count // 2 * 2:2], mixed[1:count // 2 * 2:2]
    room = jnp.minimum(lengths[giver] - 1, bound - lengths[receiver]) // 2
    room = jnp.where((giver == ranking[0]) | (receiver == ranking[0]) | (lengths[receiver] == 0), 0, jnp.maximum(room, 0))
    shifted = jax.random.randint(jax.random.fold_in(own, 4), (count // 2,), 0, 1 << 20) % (room + 1)
    lengths = lengths.at[giver].add(-shifted).at[receiver].add(shifted)
    labels = jnp.searchsorted(jnp.cumsum(lengths), jnp.arange(rows * top), side="right").astype(jnp.int32)
    table = labels.reshape(top, rows).T
    table = table[jax.random.permutation(jax.random.fold_in(own, 1), rows)]
    turn = jax.random.randint(jax.random.fold_in(own, 2), (rows, 1), 0, top)
    return jnp.take_along_axis(table, (jnp.arange(top)[None, :] + turn) % top, axis=1)


def portions_of(amount, total, limit, lean, full):
    weights = [(1 << 20) // math.isqrt(grade ** lean) + 1 for grade in range(1, amount + 1)]
    largest = limit if full else min(limit, max(-(-total // amount), total * weights[0] // sum(weights)))
    least = 1 if total - largest >= amount - 1 else 0
    given, spare = [largest] + [least] * (amount - 1), total - largest - least * (amount - 1)
    while spare > 0:
        movable = [i for i in range(1, amount) if given[i] < largest] or [i for i in range(1, amount) if given[i] < limit]
        mass, left = sum([weights[i] for i in movable]), spare
        for i in movable:
            extra = min(limit - given[i], max(1, left * weights[i] // mass), spare)
            given[i] = given[i] + extra
            spare = spare - extra
    return np.array(given)


def gaussian(rng, dims, width, most, cuts=(), kind=jnp.bfloat16):
    entries = jax.random.normal(rng, dims, jnp.float32) * width
    if len(cuts) > 0:
        entries = block_levels(rng, dims, cuts, -0.22, 0.18) * entries
    return jnp.clip(entries, min=-most, max=most).astype(kind)


def setup_inputs(seed: int = 0) -> dict:
    keys = jax.random.split(jax.random.key(seed), 19)
    annulus = gaussian(keys[0], (NODES, 2 * MODES, ELEMS), 1.0, 6.0, ((1, 8), (2, 16)), jnp.float32)
    annulus_prev = gaussian(keys[1], (NODES, 2 * MODES, ELEMS), 1.0, 6.0, ((1, 8), (2, 16)), jnp.float32)
    derivative = gaussian(keys[2], (NODES, NODES), NODES ** -0.5, 1.25, (), jnp.float32)
    radial_modulus = jnp.clip(jnp.exp(math.log(2.0) - 1.3862944 * jax.random.uniform(keys[3], (NODES, ELEMS), jnp.float32) ** block_levels(keys[3], (NODES, ELEMS), ((1, 16),), -0.2, 0.2)), 0.5, 2.0)
    shear_modulus = jnp.clip(jnp.exp(math.log(2.0) - 1.3862944 * jax.random.uniform(keys[4], (NODES, ELEMS), jnp.float32) ** block_levels(keys[4], (NODES, ELEMS), ((1, 16),), -0.2, 0.2)), 0.5, 2.0)
    node_mass = jnp.clip(jnp.exp(math.log(4.0) - 1.3862944 * jax.random.uniform(keys[5], (NODES, ELEMS), jnp.float32) ** block_levels(keys[5], (NODES, ELEMS), ((1, 16),), -0.2, 0.2)), 1.0, 4.0)
    element_modes = touch_ends(jax.random.randint(keys[6], (ELEMS,), 1, MODES + 1), jax.random.fold_in(keys[6], 1), 1, MODES).astype(jnp.int32)
    upper_rows = touch_ends(jax.random.randint(keys[7], (N_MER * SHB,), 0, NODES * E_DEV), jax.random.fold_in(keys[7], 1), 0, (NODES * E_DEV) - 1).astype(jnp.int32)
    lower_rows = touch_ends(jax.random.randint(keys[8], (N_MER * SHB,), 0, NODES * E_DEV), jax.random.fold_in(keys[8], 1), 0, (NODES * E_DEV) - 1).astype(jnp.int32)
    coupling_rows = touch_ends(jax.random.randint(keys[9], (N_MER * CPL,), 0, NODES * E_DEV), jax.random.fold_in(keys[9], 1), 0, (NODES * E_DEV) - 1).astype(jnp.int32)
    coupling_target_keys = jax.random.split(jax.random.fold_in(keys[10], 1), (N_MER * CPL) // CPL)
    coupling_target_turns = jax.random.permutation(jax.random.fold_in(keys[10], 3), (N_MER * CPL) // CPL)
    coupling_target = jax.vmap(lambda own, number: shared_out(jax.random.fold_in(keys[10], 2), own, number, CPL, DEVICES, 1, CAP, 2))(coupling_target_keys, coupling_target_turns).reshape((N_MER * CPL, 1))
    box_field = gaussian(keys[11], (BOXN,), 1.0, 6.0, ((0, 128),), jnp.float32)
    box_prev = gaussian(keys[12], (BOXN,), 1.0, 6.0, ((0, 128),), jnp.float32)
    box_angle = jnp.clip(jax.random.uniform(keys[13], (BOXN,), jnp.float32, -3.140625, 3.140625), -3.140625, 3.140625)
    box_spring = jnp.clip(jnp.exp(math.log(2.0) - 1.3862944 * jax.random.uniform(keys[14], (BOXN,), jnp.float32) ** block_levels(keys[14], (BOXN,), ((0, 128),), -0.2, 0.2)), 0.5, 2.0)
    box_mass = jnp.clip(jnp.exp(math.log(4.0) - 1.3862944 * jax.random.uniform(keys[15], (BOXN,), jnp.float32) ** block_levels(keys[15], (BOXN,), ((0, 128),), -0.2, 0.2)), 1.0, 4.0)
    box_weight = jnp.clip(jnp.exp(math.log(0.5) - 2.3025851 * jax.random.uniform(keys[16], (BOXN,), jnp.float32) ** block_levels(keys[16], (BOXN,), ((0, 128),), -0.2, 0.2)), 0.05, 0.5)
    box_slot = draw_box_slot(jax.random.fold_in(keys[18], 71), 0)
    return dict(annulus=annulus, annulus_prev=annulus_prev, derivative=derivative, radial_modulus=radial_modulus, shear_modulus=shear_modulus, node_mass=node_mass, element_modes=element_modes, upper_rows=upper_rows, lower_rows=lower_rows, coupling_rows=coupling_rows, coupling_target=coupling_target, box_field=box_field, box_prev=box_prev, box_angle=box_angle, box_spring=box_spring, box_mass=box_mass, box_weight=box_weight, box_slot=box_slot)


step_scale = 0.25


def azimuth_basis(angles):
    column = jnp.arange(2 * MODES, dtype=jnp.int32)
    order = (column % MODES).astype(jnp.float32)
    phase = angles[:, None] * order[None, :]
    return jnp.where(column[None, :] < MODES, jnp.cos(phase), jnp.sin(phase))


def annulus_force(values, derivative, radial_modulus, shear_modulus, wavenum):
    node_count, column_count, element_count = values.shape
    flat = values.reshape(node_count, column_count * element_count)
    gradient = jnp.dot(derivative, flat, precision=lax.Precision.HIGHEST)
    gradient = gradient.reshape(node_count, column_count, element_count)
    flux = (radial_modulus[:, None, :] * gradient).reshape(node_count, column_count * element_count)
    backward = jnp.dot(derivative.T, flux, precision=lax.Precision.HIGHEST)
    backward = backward.reshape(node_count, column_count, element_count)
    return -backward - shear_modulus[:, None, :] * wavenum[None, :, None] * values


def box_part(packed):
    coefficients, slot_ids, angles, springs, weights, positions = packed
    harmonic = azimuth_basis(angles)
    sample = jnp.sum(coefficients[slot_ids] * harmonic, axis=1)
    pull = springs * (sample - positions)
    reaction = jax.ops.segment_sum((-weights * pull)[:, None] * harmonic, slot_ids, num_segments=SLOTS)
    return pull, reaction


def reference(annulus, annulus_prev, derivative, radial_modulus, shear_modulus, node_mass, element_modes, upper_rows, lower_rows, coupling_rows, coupling_target, box_field, box_prev, box_angle, box_spring, box_mass, box_weight, box_slot):
    column = jnp.arange(2 * MODES, dtype=jnp.int32)
    order = (column % MODES).astype(jnp.float32)
    wavenum = (2.0 * order / MODES) ** 2
    live_mask = ((column % MODES)[:, None] < element_modes[None, :]).astype(jnp.float32)
    part_index = jnp.arange(N_MER, dtype=jnp.int32)[:, None]
    upper_part = upper_rows.reshape(N_MER, SHB)
    lower_part = lower_rows.reshape(N_MER, SHB)
    upper_node = upper_part // E_DEV
    upper_element = part_index * E_DEV + upper_part % E_DEV
    lower_node = lower_part // E_DEV
    lower_element = part_index * E_DEV + lower_part % E_DEV
    coupled = coupling_rows.reshape(N_MER, CPL)
    coupled_node = coupled // E_DEV
    coupled_element = part_index * E_DEV + coupled % E_DEV
    target = coupling_target[:, 0].reshape(N_MER, CPL)
    target_hot = (target[:, :, None] == jnp.arange(DEVICES, dtype=jnp.int32)[None, None, :]).astype(jnp.int32)
    position = jnp.sum((jnp.cumsum(target_hot, axis=1) - target_hot) * target_hot, axis=2)
    global_slot = (target * SLOTS + position * N_MER + part_index).reshape(-1).astype(jnp.int32)
    slot_parts = box_slot.reshape(DEVICES, BN_DEV)
    angle_parts = box_angle.reshape(DEVICES, BN_DEV)
    spring_parts = box_spring.reshape(DEVICES, BN_DEV)
    weight_parts = box_weight.reshape(DEVICES, BN_DEV)
    current = annulus
    previous = annulus_prev
    box_now = box_field
    box_before = box_prev
    for step_index in range(STEPS):
        force = annulus_force(current, derivative, radial_modulus, shear_modulus, wavenum)
        lower_values = force[lower_node, :, lower_element]
        upper_values = force[upper_node, :, upper_element]
        empty_rows = jnp.zeros((1, SHB, 2 * MODES), jnp.float32)
        from_below = jnp.concatenate([empty_rows, upper_values[:-1]], axis=0)
        from_above = jnp.concatenate([lower_values[1:], empty_rows], axis=0)
        force = force.at[lower_node, :, lower_element].add(from_below)
        force = force.at[upper_node, :, upper_element].add(from_above)
        sent_rows = current[coupled_node, :, coupled_element].reshape(N_MER * CPL, 2 * MODES)
        table = jnp.zeros((DEVICES * SLOTS, 2 * MODES), jnp.float32).at[global_slot].set(sent_rows)
        table = table.reshape(DEVICES, SLOTS, 2 * MODES)
        pull, reaction = lax.map(box_part, (table, slot_parts, angle_parts, spring_parts, weight_parts, box_now.reshape(DEVICES, BN_DEV)))
        returned = reaction.reshape(DEVICES * SLOTS, 2 * MODES)[global_slot].reshape(N_MER, CPL, 2 * MODES)
        force = force.at[coupled_node, :, coupled_element].add(returned)
        annulus_next = 2.0 * current - previous + step_scale * live_mask[None, :, :] * force / node_mass[:, None, :]
        box_next = 2.0 * box_now - box_before + step_scale * pull.reshape(-1) / box_mass
        previous = current
        current = annulus_next
        box_before = box_now
        box_now = box_next
    return current, box_now
```

```python
import functools

import jax
import jax.numpy as jnp
from jax import lax
from jax.experimental import pallas as pl
from jax.experimental.pallas import tpu as pltpu
from jax.sharding import PartitionSpec as P

F32 = jnp.float32
BF16 = jnp.bfloat16
I32 = jnp.int32
MESH = pl.DeviceIdType.MESH

MER, BOX = 16, 8
MODES = 256
NODES, COLS, ELEMS = 25, 64, 128
PAIRS = 13
GROUPS = 32
ALL_GROUPS = 36
ROWS = 64
STEP_SCALE = 0.25


def iota(shape, dim):
    return lax.broadcasted_iota(I32, shape, dim)


def hot(mask):
    return jnp.where(mask, 1.0, 0.0).astype(BF16)


def dot(a, b):
    return jnp.dot(a, b, preferred_element_type=F32)


def dot_nt(a, b):
    return lax.dot_general(a, b, (((1,), (1,)), ((), ())), preferred_element_type=F32)


def split2(x):
    hi = x.astype(BF16)
    return hi, (x - hi.astype(F32)).astype(BF16)


def split3(x):
    hi = x.astype(BF16)
    rest = x - hi.astype(F32)
    mid = rest.astype(BF16)
    return hi, mid, (rest - mid.astype(F32)).astype(BF16)


def take_lanes(x, index):
    return jnp.take_along_axis(x, index, axis=1, mode="promise_in_bounds")


def sincos(x):
    k = jnp.floor(x * 0.6366197723675814 + 0.5)
    r = x - k * 1.5703125
    r = r - k * 4.837512969970703125e-4
    r = r - k * 7.54978995489188216e-8
    z = r * r
    s = ((-1.9515295891e-4 * z + 8.3321608736e-3) * z - 1.6666654611e-1) * z * r + r
    c = ((2.443315711809948e-5 * z - 1.388731625493765e-3) * z + 4.166664568298827e-2) * z * z
    c = c - 0.5 * z + 1.0
    q = k.astype(I32)
    odd = (q & 1) == 1
    sine = jnp.where(odd, c, s)
    cosine = jnp.where(odd, s, c)
    sine = jnp.where((q & 2) == 2, -sine, sine)
    cosine = jnp.where(((q + 1) & 2) == 2, -cosine, cosine)
    return sine, cosine


def setup_kernel(
    slot_ref, angle_ref, spring_ref, mass_ref, weight_ref, now_ref, before_ref,
    rows_ref, target_ref, lower_ref, upper_ref,
    send_ref, dest_ref, node_ref, elem_ref, fields,
):
    tri = hot(iota((128, 128), 0) < iota((128, 128), 1))
    slot = slot_ref[...]
    part = slot & (MER - 1)
    sources = [
        angle_ref[...], (slot >> 4).astype(F32), spring_ref[...], mass_ref[...],
        weight_ref[...], now_ref[...], before_ref[...], jnp.zeros((8, 128), F32),
    ]
    for r in range(8):
        for f in range(8):
            fields[r, f : f + 1, :] = sources[f][r : r + 1, :]
    base = jnp.zeros((MER, 1), F32)
    total = jnp.zeros((24, 1024), F32)
    for r in range(8):
        mine = part[r : r + 1, :]
        member = jnp.where(iota((MER, 128), 0) == mine, 1.0, 0.0)
        rank = dot(member.astype(BF16), tri) + base
        place = jnp.sum(member * rank, axis=0, keepdims=True).astype(I32)
        base = base + jnp.sum(member, axis=1, keepdims=True)
        dest = mine * 64 + place
        dest_ref[r : r + 1, :] = dest
        order = hot(iota((1024, 128), 0) == dest)
        pieces = jnp.concatenate(split3(fields[r]), axis=0)
        total = total + dot_nt(pieces, order)
    sorted_fields = total[0:8] + (total[8:16] + total[16:24])
    for m in range(8):
        send_ref[m] = sorted_fields[:, m * 128 : (m + 1) * 128]

    rows = rows_ref[...]
    target = target_ref[...]
    reader = (target & (BOX - 1)) * MER + (target >> 3)
    node1 = ((rows >> 7) + 1).astype(F32)
    elem = (rows & 127).astype(F32)
    count = jnp.zeros((128, 1), F32)
    table = jnp.zeros((64, 128), F32)
    for r in range(16):
        mine = reader[r : r + 1, :]
        member = jnp.where(iota((128, 128), 0) == mine, 1.0, 0.0)
        rank = dot(member.astype(BF16), tri) + count
        place = jnp.sum(member * rank, axis=0, keepdims=True).astype(I32)
        count = count + jnp.sum(member, axis=1, keepdims=True)
        lane = (mine & 3) * 32 + place
        group = iota((GROUPS, 128), 0) == (mine >> 2)
        values = jnp.concatenate(
            [
                jnp.where(group, jnp.broadcast_to(node1[r : r + 1, :], (GROUPS, 128)), 0.0),
                jnp.where(group, jnp.broadcast_to(elem[r : r + 1, :], (GROUPS, 128)), 0.0),
            ],
            axis=0,
        ).astype(BF16)
        table = table + dot_nt(values, hot(iota((128, 128), 0) == lane))
    node_ref[0:GROUPS, :] = table[0:GROUPS].astype(I32) - 1
    elem_ref[0:GROUPS, :] = table[GROUPS : 2 * GROUPS].astype(I32)
    for k, ref in enumerate((lower_ref, upper_ref)):
        edge = ref[...]
        node_ref[GROUPS + 2 * k : GROUPS + 2 * k + 2, :] = edge >> 7
        elem_ref[GROUPS + 2 * k : GROUPS + 2 * k + 2, :] = edge & 127


def halves(even, odd, half):
    low = jnp.where(half == 0, even, pltpu.roll(even, 64, 1))
    high = jnp.where(half == 1, odd, pltpu.roll(odd, 64, 1))
    return jnp.where(iota((8, 128), 1) < 64, low, high)


def greet(partners):
    barrier = pltpu.get_barrier_semaphore()
    for device in partners:
        pl.semaphore_signal(barrier, inc=1, device_id=device, device_id_type=MESH)
    pl.semaphore_wait(barrier, len(partners))


def distribute_kernel(
    send_ref, own_ref, angle_ref, place_ref, received, share, shared,
    send_sem, recv_sem, share_send, share_recv,
):
    i = lax.axis_index("mer")
    j = lax.axis_index("box")
    mer_peers = [lax.rem(i + o, MER) for o in range(1, MER)]
    box_peers = [lax.rem(j + o, BOX) for o in range(1, BOX)]
    greet([(q, j) for q in mer_peers] + [(i, q) for q in box_peers])
    copies = []
    for o, q in enumerate(mer_peers):
        copy = pltpu.make_async_remote_copy(
            src_ref=send_ref.at[q // 2],
            dst_ref=received.at[i],
            send_sem=send_sem.at[o],
            recv_sem=recv_sem.at[o],
            device_id=(q, j),
            device_id_type=MESH,
        )
        copy.start()
        copies.append(copy)
    received[i] = send_ref[i // 2]
    for copy in copies:
        copy.wait()
    half = lax.rem(i, 2)
    fields = []
    for f in range(7):
        even = jnp.concatenate([received[2 * r, f : f + 1, :] for r in range(8)], axis=0)
        odd = jnp.concatenate([received[2 * r + 1, f : f + 1, :] for r in range(8)], axis=0)
        fields.append(halves(even, odd, half))
    share[0] = fields[0]
    share[1] = fields[1]
    copies = []
    for o, q in enumerate(box_peers):
        copy = pltpu.make_async_remote_copy(
            src_ref=share,
            dst_ref=shared.at[j],
            send_sem=share_send.at[o],
            recv_sem=share_recv.at[o],
            device_id=(i, q),
            device_id_type=MESH,
        )
        copy.start()
        copies.append(copy)
    for f in range(5):
        own_ref[f] = fields[f + 2]
    shared[j] = share[...]
    for copy in copies:
        copy.wait()
    for b in range(BOX):
        angle_ref[b * 8 : (b + 1) * 8, :] = shared[b, 0]
        place_ref[b * 8 : (b + 1) * 8, :] = shared[b, 1].astype(I32)


def harmonics(j, angle_ref, harmonic_ref):
    sub = iota((8, 128), 0).astype(F32)
    first = (lax.rem(j, 4) * 64).astype(F32)
    is_sine = j >= 4

    def body(row, carry):
        angle = jnp.broadcast_to(angle_ref[pl.ds(row, 1), :], (8, 128))
        base_sin, base_cos = sincos(angle * (sub + first))
        step_sin, step_cos = sincos(angle * (sub * 8.0))
        a = jnp.where(is_sine, base_sin, base_cos)
        b = jnp.where(is_sine, -base_cos, base_sin)
        for t in range(8):
            harmonic_ref[row, t * 8 : (t + 1) * 8, :] = (
                a * step_cos[t : t + 1, :] - b * step_sin[t : t + 1, :]
            )
        return carry

    lax.fori_loop(0, ROWS, body, 0)


def gather_rows(values_ref, node, elem, groups):
    index = jnp.broadcast_to(elem, (8, 128))
    node = jnp.broadcast_to(node, (8, 128))
    acc = [jnp.zeros((8, 128), F32) for _ in range(8)]
    for a in range(NODES):
        mask = node == a
        for c in range(8):
            taken = take_lanes(values_ref[a * 64 + c * 8 : a * 64 + c * 8 + 8, :], index)
            acc[c] = jnp.where(mask, taken, acc[c])
    return acc


def fill_table(values_ref, node_ref, elem_ref, table_ref):
    def body(g, carry):
        acc = gather_rows(values_ref, node_ref[pl.ds(g, 1), :], elem_ref[pl.ds(g, 1), :], 1)
        for c in range(8):
            table_ref[g, c * 8 : (c + 1) * 8, :] = acc[c]
        return carry

    lax.fori_loop(0, GROUPS, body, 0)


def node_lane(place, odd):
    return place + (iota((1, 128), 1) >> 6) * 32 + odd * 64


def sample_nodes(table_ref, place_ref, harmonic_ref, partial_ref):
    def body(g, carry):
        for odd in range(2):
            row = 2 * g + odd
            index = jnp.broadcast_to(node_lane(place_ref[pl.ds(row, 1), :], odd), (8, 128))
            acc = jnp.zeros((8, 128), F32)
            for c in range(8):
                taken = take_lanes(table_ref[g, c * 8 : (c + 1) * 8, :], index)
                acc = acc + taken * harmonic_ref[row, c * 8 : (c + 1) * 8, :]
            partial_ref[pl.ds(row, 1), :] = jnp.sum(acc, axis=0, keepdims=True)
        return carry

    lax.fori_loop(0, GROUPS, body, 0)


def compute_force(j, values_ref, deriv_ref, deriv_t_ref, radial_ref, shear_ref, force_ref):
    deriv = deriv_ref[...]
    deriv_t = deriv_t_ref[...]
    radial = radial_ref[...]
    shear = shear_ref[...]
    first = lax.rem(j, 4) * 64

    def body(k, carry):
        x = jnp.concatenate(
            [values_ref[pl.ds(k * 8 + c, NODES, stride=64), :] for c in range(8)], axis=1
        )
        gradient = jnp.dot(deriv, x, precision=lax.Precision.HIGHEST, preferred_element_type=F32)
        flux = gradient * jnp.concatenate([radial] * 8, axis=1)
        back = jnp.dot(deriv_t, flux, precision=lax.Precision.HIGHEST, preferred_element_type=F32)
        for c in range(8):
            wave = (first + k * 8 + c).astype(F32) * (2.0 / MODES)
            lanes = slice(c * 128, (c + 1) * 128)
            force_ref[pl.ds(k * 8 + c, NODES, stride=64), :] = (
                -back[:, lanes] - shear * (wave * wave) * x[:, lanes]
            )
        return carry

    lax.fori_loop(0, 8, body, 0)


def edge_forces(force_ref, node_ref, elem_ref, edge_ref):
    def body(g, carry):
        acc = gather_rows(
            force_ref, node_ref[pl.ds(GROUPS + g, 1), :], elem_ref[pl.ds(GROUPS + g, 1), :], 1
        )
        for c in range(8):
            edge_ref[g, c * 8 : (c + 1) * 8, :] = acc[c]
        return carry

    lax.fori_loop(0, 4, body, 0)


def front(j, values_ref, node_ref, elem_ref, place_ref, harmonic_ref, table_ref,
          deriv_ref, deriv_t_ref, radial_ref, shear_ref, partial_ref, force_ref, edge_ref):
    fill_table(values_ref, node_ref, elem_ref, table_ref)
    sample_nodes(table_ref, place_ref, harmonic_ref, partial_ref)
    compute_force(j, values_ref, deriv_ref, deriv_t_ref, radial_ref, shear_ref, force_ref)
    edge_forces(force_ref, node_ref, elem_ref, edge_ref)


def slot_reactions(drive_ref, harmonic_ref, place_ref, edge_ref, high_ref, low_ref):
    def body(g, carry):
        pieces, hots = [], []
        for odd in range(2):
            row = 2 * g + odd
            x = harmonic_ref[row] * drive_ref[pl.ds(row, 1), :]
            pieces.append(split2(x))
            lane = node_lane(place_ref[pl.ds(row, 1), :], odd)
            hots.append(hot(iota((128, 128), 0) == lane))
        left = jnp.concatenate([pieces[0][0], pieces[1][0], pieces[0][1], pieces[1][1]], axis=1)
        right = jnp.concatenate(hots + hots, axis=1)
        high, low = split2(dot_nt(left, right))
        high_ref[g] = high
        low_ref[g] = low
        return carry

    lax.fori_loop(0, GROUPS, body, 0)
    for g in range(4):
        high, low = split2(edge_ref[g])
        high_ref[GROUPS + g] = high
        low_ref[GROUPS + g] = low


def scatter_slots(node_ref, elem_ref, high_ref, low_ref, left_ref, sum_ref):
    sum_ref[...] = jnp.zeros_like(sum_ref)

    def body(t, carry):
        hots = []
        for h in range(2):
            g = 2 * t + h
            node = node_ref[pl.ds(g, 1), :]
            lane = (node & 1) * 128 + elem_ref[pl.ds(g, 1), :]
            hots.append(hot(iota((256, 128), 0) == lane))
            pair = node >> 1
            high = high_ref[g]
            low = low_ref[g]
            for a in range(PAIRS):
                mask = jnp.broadcast_to(hot(pair == a), (COLS, 128))
                left_ref[a * 64 : (a + 1) * 64, h * 128 : (h + 1) * 128] = high * mask
                left_ref[a * 64 : (a + 1) * 64, 256 + h * 128 : 384 + h * 128] = low * mask
        right = jnp.concatenate(hots + hots, axis=1)
        sum_ref[...] += dot_nt(left_ref[...], right)
        return carry

    lax.fori_loop(0, ALL_GROUPS // 2, body, 0)


def advance(j, now_ref, before_ref, force_ref, sum_ref, mass_ref, modes_ref, next_ref):
    order = lax.rem(j, 4) * 64 + iota((COLS, 128), 0)
    live = jnp.where(order < modes_ref[...], STEP_SCALE, 0.0)
    for a in range(NODES):
        rows = slice(a * 64, (a + 1) * 64)
        pair = a // 2
        lanes = slice((a % 2) * 128, (a % 2) * 128 + 128)
        total = force_ref[rows, :] + sum_ref[pair * 64 : (pair + 1) * 64, lanes]
        next_ref[rows, :] = (
            2.0 * now_ref[rows, :] - before_ref[rows, :] + live * total / mass_ref[a : a + 1, :]
        )


def first_kernel(
    angle_ref, place_ref, now_ref, node_ref, elem_ref, deriv_ref, deriv_t_ref, radial_ref,
    shear_ref, harmonic_ref, partial_ref, force_ref, edge_ref, table_ref,
):
    j = lax.axis_index("box")
    harmonics(j, angle_ref, harmonic_ref)
    front(j, now_ref, node_ref, elem_ref, place_ref, harmonic_ref, table_ref, deriv_ref,
          deriv_t_ref, radial_ref, shear_ref, partial_ref, force_ref, edge_ref)


def middle_kernel(
    drive_ref, edge_in_ref, harmonic_ref, place_ref, now_ref, before_ref, force_in_ref,
    node_ref, elem_ref, deriv_ref, deriv_t_ref, radial_ref, shear_ref, mass_ref, modes_ref,
    next_ref, partial_ref, force_ref, edge_ref,
    table_ref, high_ref, low_ref, left_ref, sum_ref,
):
    j = lax.axis_index("box")
    slot_reactions(drive_ref, harmonic_ref, place_ref, edge_in_ref, high_ref, low_ref)
    scatter_slots(node_ref, elem_ref, high_ref, low_ref, left_ref, sum_ref)
    advance(j, now_ref, before_ref, force_in_ref, sum_ref, mass_ref, modes_ref, next_ref)
    front(j, next_ref, node_ref, elem_ref, place_ref, harmonic_ref, table_ref, deriv_ref,
          deriv_t_ref, radial_ref, shear_ref, partial_ref, force_ref, edge_ref)


def last_kernel(
    drive_ref, edge_in_ref, harmonic_ref, place_ref, now_ref, before_ref, force_in_ref,
    node_ref, elem_ref, mass_ref, modes_ref, box_ref, dest_ref,
    next_ref, box_out_ref, high_ref, low_ref, left_ref, sum_ref,
):
    j = lax.axis_index("box")
    slot_reactions(drive_ref, harmonic_ref, place_ref, edge_in_ref, high_ref, low_ref)
    scatter_slots(node_ref, elem_ref, high_ref, low_ref, left_ref, sum_ref)
    advance(j, now_ref, before_ref, force_in_ref, sum_ref, mass_ref, modes_ref, next_ref)
    box = box_ref[...]
    line = jnp.concatenate([box[m : m + 1, :] for m in range(8)], axis=1)
    pieces = jnp.concatenate([piece.astype(F32) for piece in split3(line)], axis=0).astype(BF16)
    for r in range(8):
        out = dot(pieces, hot(iota((1024, 128), 0) == dest_ref[r : r + 1, :]))
        box_out_ref[r : r + 1, :] = out[0:1] + (out[1:2] + out[2:3])


def exchange_kernel(
    last, partial_ref, spring_ref, mass_ref, weight_ref, now_ref, before_ref, edge_ref,
    drive_ref, next_ref, edge_out_ref,
    sums, drive, drives, edges, ways, returned,
    sum_send, sum_recv, drive_send, drive_recv, edge_send, edge_recv, way_send, way_recv,
):
    i = lax.axis_index("mer")
    j = lax.axis_index("box")
    above = lax.rem(i + 1, MER)
    below = lax.rem(i + MER - 1, MER)
    mer_peers = [lax.rem(i + o, MER) for o in range(1, MER)]
    box_peers = [lax.rem(j + o, BOX) for o in range(1, BOX)]
    met = mer_peers if last else [above, below]
    greet([(q, j) for q in met] + [(i, q) for q in box_peers])
    copies = []
    for o, q in enumerate(box_peers):
        copy = pltpu.make_async_remote_copy(
            src_ref=partial_ref.at[pl.ds(pl.multiple_of(q * 8, 8), 8), :],
            dst_ref=sums.at[o],
            send_sem=sum_send.at[o],
            recv_sem=sum_recv.at[o],
            device_id=(i, q),
            device_id_type=MESH,
        )
        copy.start()
        copies.append(copy)
    up = pltpu.make_async_remote_copy(
        src_ref=edge_ref.at[2:4], dst_ref=edges.at[0:2],
        send_sem=edge_send.at[0], recv_sem=edge_recv.at[0],
        device_id=(above, j), device_id_type=MESH,
    )
    down = pltpu.make_async_remote_copy(
        src_ref=edge_ref.at[0:2], dst_ref=edges.at[2:4],
        send_sem=edge_send.at[1], recv_sem=edge_recv.at[1],
        device_id=(below, j), device_id_type=MESH,
    )
    up.start()
    down.start()
    sample = partial_ref[pl.ds(pl.multiple_of(j * 8, 8), 8), :]
    for copy in copies:
        copy.wait()
    for o in range(BOX - 1):
        sample = sample + sums[o]
    now = now_ref[...]
    pull = spring_ref[...] * (sample - now)
    drive[...] = -weight_ref[...] * pull
    copies = []
    for o, q in enumerate(box_peers):
        copy = pltpu.make_async_remote_copy(
            src_ref=drive,
            dst_ref=drives.at[j],
            send_sem=drive_send.at[o],
            recv_sem=drive_recv.at[o],
            device_id=(i, q),
            device_id_type=MESH,
        )
        copy.start()
        copies.append(copy)
    after = 2.0 * now - before_ref[...] + STEP_SCALE * pull / mass_ref[...]
    if last:
        for m in range(8):
            ways[m] = jnp.broadcast_to(after[m : m + 1, :], (8, 128))
        for o, q in enumerate(mer_peers):
            copy = pltpu.make_async_remote_copy(
                src_ref=ways.at[q // 2],
                dst_ref=returned.at[i],
                send_sem=way_send.at[o],
                recv_sem=way_recv.at[o],
                device_id=(q, j),
                device_id_type=MESH,
            )
            copy.start()
            copies.append(copy)
        returned[i] = ways[i // 2]
    else:
        next_ref[...] = after
    drives[j] = drive[...]
    up.wait()
    down.wait()
    for g in range(4):
        ghost = (i == 0) if g < 2 else (i == MER - 1)
        edge_out_ref[g] = jnp.where(ghost, 0.0, edges[g])
    for copy in copies:
        copy.wait()
    if last:
        even = jnp.concatenate([returned[2 * r, 0:1, :] for r in range(8)], axis=0)
        odd = jnp.concatenate([returned[2 * r + 1, 0:1, :] for r in range(8)], axis=0)
        next_ref[...] = halves(even, odd, lax.rem(i, 2))
    for b in range(BOX):
        drive_ref[b * 8 : (b + 1) * 8, :] = drives[b]


def shape(*dims, dtype=F32):
    return jax.ShapeDtypeStruct(dims, dtype)


def call(kernel, outs, scratch, name, collective=None):
    params = dict(vmem_limit_bytes=48 << 20)
    if collective is not None:
        params.update(collective_id=collective, has_side_effects=True)
    return pl.pallas_call(
        kernel,
        out_shape=outs,
        scratch_shapes=scratch,
        compiler_params=pltpu.CompilerParams(**params),
        name=name,
    )


def dma(count):
    return pltpu.SemaphoreType.DMA((count,))


def exchange(last):
    return call(
        functools.partial(exchange_kernel, last),
        [shape(ROWS, 128), shape(8, 128), shape(4, COLS, 128)],
        [
            pltpu.VMEM((7, 8, 128), F32), pltpu.VMEM((8, 128), F32), pltpu.VMEM((8, 8, 128), F32),
            pltpu.VMEM((4, COLS, 128), F32), pltpu.VMEM((8, 8, 128), F32),
            pltpu.VMEM((MER, 8, 128), F32),
            dma(7), dma(7), dma(7), dma(7), dma(2), dma(2), dma(15), dma(15),
        ],
        "exchange_last" if last else "exchange",
        2 if last else 1,
    )


BACK_SCRATCH = [
    pltpu.VMEM((ALL_GROUPS, COLS, 128), BF16), pltpu.VMEM((ALL_GROUPS, COLS, 128), BF16),
    pltpu.VMEM((PAIRS * COLS, 512), BF16), pltpu.VMEM((PAIRS * COLS, 256), F32),
]


def per_device(
    annulus, annulus_prev, derivative, radial_modulus, shear_modulus, node_mass, element_modes,
    upper_rows, lower_rows, coupling_rows, coupling_target, box_field, box_prev, box_angle,
    box_spring, box_mass, box_weight, box_slot,
):
    flat = NODES * COLS
    now = annulus.reshape(flat, ELEMS)
    before = annulus_prev.reshape(flat, ELEMS)
    modes = element_modes.reshape(1, ELEMS)
    deriv_t = derivative.T

    send, dest, node, elem = call(
        setup_kernel,
        [shape(8, 8, 128), shape(8, 128, dtype=I32), shape(ALL_GROUPS, 128, dtype=I32),
         shape(ALL_GROUPS, 128, dtype=I32)],
        [pltpu.VMEM((8, 8, 128), F32)],
        "setup",
    )(
        *(x.reshape(8, 128) for x in (
            box_slot, box_angle, box_spring, box_mass, box_weight, box_field, box_prev)),
        coupling_rows.reshape(16, 128), coupling_target.reshape(16, 128),
        lower_rows.reshape(2, 128), upper_rows.reshape(2, 128),
    )
    own, angle, place = call(
        distribute_kernel,
        [shape(5, 8, 128), shape(ROWS, 128), shape(ROWS, 128, dtype=I32)],
        [
            pltpu.VMEM((MER, 8, 128), F32), pltpu.VMEM((2, 8, 128), F32),
            pltpu.VMEM((BOX, 2, 8, 128), F32), dma(15), dma(15), dma(7), dma(7),
        ],
        "distribute",
        0,
    )(send)
    spring, mass, weight, box_now, box_before = (own[k] for k in range(5))
    table = pltpu.VMEM((GROUPS, COLS, 128), F32)
    harmonic, partial, force, edge = call(
        first_kernel,
        [shape(ROWS, COLS, 128), shape(ROWS, 128), shape(flat, ELEMS), shape(4, COLS, 128)],
        [table],
        "first",
    )(angle, place, now, node, elem, derivative, deriv_t, radial_modulus, shear_modulus)
    drive, box_next, edge = exchange(False)(
        partial, spring, mass, weight, box_now, box_before, edge)
    later, partial, force, edge = call(
        middle_kernel,
        [shape(flat, ELEMS), shape(ROWS, 128), shape(flat, ELEMS), shape(4, COLS, 128)],
        [table] + BACK_SCRATCH,
        "middle",
    )(drive, edge, harmonic, place, now, before, force, node, elem, derivative, deriv_t,
      radial_modulus, shear_modulus, node_mass, modes)
    drive, box_back, edge = exchange(True)(
        partial, spring, mass, weight, box_next, box_now, edge)
    final, box_out = call(
        last_kernel, [shape(flat, ELEMS), shape(8, 128)], BACK_SCRATCH, "last"
    )(drive, edge, harmonic, place, later, now, force, node, elem, node_mass, modes, box_back, dest)
    return final.reshape(NODES, COLS, ELEMS), box_out.reshape(1024)


def solution(mesh):
    mer_box = P(("mer", "box"))
    in_specs = (
        P(None, "box", "mer"), P(None, "box", "mer"), P(),
        P(None, "mer"), P(None, "mer"), P(None, "mer"),
        P("mer"), P("mer"), P("mer"), P("mer"), P("mer", None),
        mer_box, mer_box, mer_box, mer_box, mer_box, mer_box, mer_box,
    )
    return jax.shard_map(
        per_device, mesh=mesh, in_specs=in_specs,
        out_specs=(P(None, "box", "mer"), mer_box), check_vma=False,
    )
```

```python
import jax
import jax.numpy as jnp
from jax import lax
from jax.experimental import pallas as pl
from jax.experimental.pallas import tpu as pltpu
from jax.sharding import PartitionSpec as P

F32 = jnp.float32
BF16 = jnp.bfloat16
I32 = jnp.int32
MESH = pl.DeviceIdType.MESH

MER, BOX = 16, 8
MODES = 256
NODES, COLS, ELEMS = 25, 64, 128
PAIRS = 13
GROUPS = 32
ALL_GROUPS = 36
ROWS = 64
STEP_SCALE = 0.25


def iota(shape, dim):
    return lax.broadcasted_iota(I32, shape, dim)


def hot(mask):
    return jnp.where(mask, 1.0, 0.0).astype(BF16)


def dot(a, b):
    return jnp.dot(a, b, preferred_element_type=F32)


def dot_nt(a, b):
    return lax.dot_general(a, b, (((1,), (1,)), ((), ())), preferred_element_type=F32)


def split2(x):
    hi = x.astype(BF16)
    return hi, (x - hi.astype(F32)).astype(BF16)


def split3(x):
    hi = x.astype(BF16)
    rest = x - hi.astype(F32)
    mid = rest.astype(BF16)
    return hi, mid, (rest - mid.astype(F32)).astype(BF16)


def take_lanes(x, index):
    return jnp.take_along_axis(x, index, axis=1, mode="promise_in_bounds")


def sincos(x):
    k = jnp.floor(x * 0.6366197723675814 + 0.5)
    r = x - k * 1.5703125
    r = r - k * 4.837512969970703125e-4
    r = r - k * 7.54978995489188216e-8
    z = r * r
    s = ((-1.9515295891e-4 * z + 8.3321608736e-3) * z - 1.6666654611e-1) * z * r + r
    c = ((2.443315711809948e-5 * z - 1.388731625493765e-3) * z + 4.166664568298827e-2) * z * z
    c = c - 0.5 * z + 1.0
    q = k.astype(I32)
    odd = (q & 1) == 1
    sine = jnp.where(odd, c, s)
    cosine = jnp.where(odd, s, c)
    sine = jnp.where((q & 2) == 2, -sine, sine)
    cosine = jnp.where(((q + 1) & 2) == 2, -cosine, cosine)
    return sine, cosine


def before_lane():
    return hot(iota((128, 128), 0) < iota((128, 128), 1))


def order_nodes(sources, dest_ref, send_ref, fields):
    tri = before_lane()
    part = sources[1] & (MER - 1)
    values = [sources[0], (sources[1] >> 4).astype(F32)] + list(sources[2:])
    for r in range(8):
        for f in range(7):
            fields[r, f : f + 1, :] = values[f][r : r + 1, :]
        fields[r, 7:8, :] = jnp.zeros((1, 128), F32)
    base = jnp.zeros((MER, 1), F32)
    total = jnp.zeros((24, 1024), F32)
    for r in range(8):
        mine = part[r : r + 1, :]
        member = jnp.where(iota((MER, 128), 0) == mine, 1.0, 0.0)
        rank = dot(member.astype(BF16), tri) + base
        place = jnp.sum(member * rank, axis=0, keepdims=True).astype(I32)
        base = base + jnp.sum(member, axis=1, keepdims=True)
        dest = mine * 64 + place
        dest_ref[r : r + 1, :] = dest
        order = hot(iota((1024, 128), 0) == dest)
        pieces = jnp.concatenate(split3(fields[r]), axis=0)
        total = total + dot_nt(pieces, order)
    sorted_fields = total[0:8] + (total[8:16] + total[16:24])
    for m in range(8):
        send_ref[m] = sorted_fields[:, m * 128 : (m + 1) * 128]


def slot_table(rows, target, edges, node_ref, elem_ref):
    tri = before_lane()
    reader = (target & (BOX - 1)) * MER + (target >> 3)
    node1 = ((rows >> 7) + 1).astype(F32)
    elem = (rows & 127).astype(F32)
    count = jnp.zeros((128, 1), F32)
    table = jnp.zeros((64, 128), F32)
    for r in range(16):
        mine = reader[r : r + 1, :]
        member = jnp.where(iota((128, 128), 0) == mine, 1.0, 0.0)
        rank = dot(member.astype(BF16), tri) + count
        place = jnp.sum(member * rank, axis=0, keepdims=True).astype(I32)
        count = count + jnp.sum(member, axis=1, keepdims=True)
        lane = (mine & 3) * 32 + place
        group = iota((GROUPS, 128), 0) == (mine >> 2)
        values = jnp.concatenate(
            [
                jnp.where(group, jnp.broadcast_to(node1[r : r + 1, :], (GROUPS, 128)), 0.0),
                jnp.where(group, jnp.broadcast_to(elem[r : r + 1, :], (GROUPS, 128)), 0.0),
            ],
            axis=0,
        ).astype(BF16)
        table = table + dot_nt(values, hot(iota((128, 128), 0) == lane))
    node_ref[0:GROUPS, :] = table[0:GROUPS].astype(I32) - 1
    elem_ref[0:GROUPS, :] = table[GROUPS : 2 * GROUPS].astype(I32)
    for k, edge in enumerate(edges):
        node_ref[GROUPS + 2 * k : GROUPS + 2 * k + 2, :] = edge >> 7
        elem_ref[GROUPS + 2 * k : GROUPS + 2 * k + 2, :] = edge & 127


def halves(even, odd, half):
    low = jnp.where(half == 0, even, pltpu.roll(even, 64, 1))
    high = jnp.where(half == 1, odd, pltpu.roll(odd, 64, 1))
    return jnp.where(iota((8, 128), 1) < 64, low, high)


def harmonics(j, angles, block, harmonic_ref):
    sub = iota((8, 128), 0).astype(F32)
    first = (lax.rem(j, 4) * 64).astype(F32)
    is_sine = j >= 4
    for r in range(8):
        angle = jnp.broadcast_to(angles[r : r + 1, :], (8, 128))
        base_sin, base_cos = sincos(angle * (sub + first))
        step_sin, step_cos = sincos(angle * (sub * 8.0))
        a = jnp.where(is_sine, base_sin, base_cos)
        b = jnp.where(is_sine, -base_cos, base_sin)
        for t in range(8):
            harmonic_ref[block * 8 + r, t * 8 : (t + 1) * 8, :] = (
                a * step_cos[t : t + 1, :] - b * step_sin[t : t + 1, :]
            )


def gather_rows(values_ref, node, elem, groups):
    index = jnp.broadcast_to(elem, (8, 128))
    node = jnp.broadcast_to(node, (8, 128))
    acc = [jnp.zeros((8, 128), F32) for _ in range(8)]
    for a in range(NODES):
        mask = node == a
        for c in range(8):
            taken = take_lanes(values_ref[a * 64 + c * 8 : a * 64 + c * 8 + 8, :], index)
            acc[c] = jnp.where(mask, taken, acc[c])
    return acc


def fill_table(values_ref, node_ref, elem_ref, table_ref):
    def body(g, carry):
        acc = gather_rows(values_ref, node_ref[pl.ds(g, 1), :], elem_ref[pl.ds(g, 1), :], 1)
        for c in range(8):
            table_ref[g, c * 8 : (c + 1) * 8, :] = acc[c]
        return carry

    lax.fori_loop(0, GROUPS, body, 0)


def node_lane(place, odd):
    return place + (iota((1, 128), 1) >> 6) * 32 + odd * 64


def sample_nodes(table_ref, places, block, harmonic_ref):
    rows = []
    for r in range(8):
        index = jnp.broadcast_to(node_lane(places[r : r + 1, :], r % 2), (8, 128))
        group = block * 4 + r // 2
        acc = jnp.zeros((8, 128), F32)
        for c in range(8):
            taken = take_lanes(table_ref[group, c * 8 : (c + 1) * 8, :], index)
            acc = acc + taken * harmonic_ref[block * 8 + r, c * 8 : (c + 1) * 8, :]
        rows.append(jnp.sum(acc, axis=0, keepdims=True))
    return jnp.concatenate(rows, axis=0)


def compute_force(j, values_ref, deriv_ref, radial_ref, shear_ref, force_ref):
    deriv = deriv_ref[...]
    radial = radial_ref[...]
    shear = shear_ref[...]
    first = lax.rem(j, 4) * 64

    def body(k, carry):
        x = jnp.concatenate(
            [values_ref[pl.ds(k * 8 + c, NODES, stride=64), :] for c in range(8)], axis=1
        )
        gradient = jnp.dot(deriv, x, precision=lax.Precision.HIGHEST, preferred_element_type=F32)
        flux = gradient * jnp.concatenate([radial] * 8, axis=1)
        back = lax.dot_general(
            deriv, flux, (((0,), (0,)), ((), ())),
            precision=lax.Precision.HIGHEST, preferred_element_type=F32,
        )
        for c in range(8):
            wave = (first + k * 8 + c).astype(F32) * (2.0 / MODES)
            lanes = slice(c * 128, (c + 1) * 128)
            force_ref[pl.ds(k * 8 + c, NODES, stride=64), :] = (
                -back[:, lanes] - shear * (wave * wave) * x[:, lanes]
            )
        return carry

    lax.fori_loop(0, 8, body, 0)


def edge_forces(force_ref, node_ref, elem_ref, edge_ref):
    def body(g, carry):
        acc = gather_rows(
            force_ref, node_ref[pl.ds(GROUPS + g, 1), :], elem_ref[pl.ds(GROUPS + g, 1), :], 1
        )
        for c in range(8):
            edge_ref[g, c * 8 : (c + 1) * 8, :] = acc[c]
        return carry

    lax.fori_loop(0, 4, body, 0)


def slot_reactions(drives, places, block, harmonic_ref, high_ref, low_ref):
    for k in range(4):
        pieces, hots = [], []
        for odd in range(2):
            r = 2 * k + odd
            x = harmonic_ref[block * 8 + r] * drives[r : r + 1, :]
            pieces.append(split2(x))
            lane = node_lane(places[r : r + 1, :], odd)
            hots.append(hot(iota((128, 128), 0) == lane))
        left = jnp.concatenate([pieces[0][0], pieces[1][0], pieces[0][1], pieces[1][1]], axis=1)
        right = jnp.concatenate(hots + hots, axis=1)
        high, low = split2(dot_nt(left, right))
        high_ref[block * 4 + k] = high
        low_ref[block * 4 + k] = low


def scatter_slots(first, node_ref, elem_ref, high_ref, low_ref, left_ref, sum_ref):
    def body(t, carry):
        hots = []
        for h in range(2):
            g = 2 * t + h
            node = node_ref[pl.ds(g, 1), :]
            lane = (node & 1) * 128 + elem_ref[pl.ds(g, 1), :]
            hots.append(hot(iota((256, 128), 0) == lane))
            pair = node >> 1
            high = high_ref[g]
            low = low_ref[g]
            for a in range(PAIRS):
                mask = jnp.broadcast_to(hot(pair == a), (COLS, 128))
                left_ref[a * 64 : (a + 1) * 64, h * 128 : (h + 1) * 128] = high * mask
                left_ref[a * 64 : (a + 1) * 64, 256 + h * 128 : 384 + h * 128] = low * mask
        right = jnp.concatenate(hots + hots, axis=1)
        sum_ref[...] += dot_nt(left_ref[...], right)
        return carry

    lax.fori_loop(first, first + 2, body, 0)


def advance(j, now_ref, before_ref, force_ref, sum_ref, mass_ref, modes_ref, next_ref):
    order = lax.rem(j, 4) * 64 + iota((COLS, 128), 0)
    live = jnp.where(order < modes_ref[...], STEP_SCALE, 0.0)
    for a in range(NODES):
        rows = slice(a * 64, (a + 1) * 64)
        pair = a // 2
        lanes = slice((a % 2) * 128, (a % 2) * 128 + 128)
        total = force_ref[rows, :] + sum_ref[pair * 64 : (pair + 1) * 64, lanes]
        next_ref[rows, :] = (
            2.0 * now_ref[rows, :] - before_ref[rows, :] + live * total / mass_ref[a : a + 1, :]
        )


INPUTS = 18


def whole_kernel(*refs):
    hbm = refs[:INPUTS]
    out_ref, box_out_ref = refs[INPUTS : INPUTS + 2]
    vmem = refs[INPUTS + 2 : 2 * INPUTS + 2]
    (
        fields, dest_ref, send_ref, node_ref, elem_ref, received, share, shared, harmonic_ref,
        table_ref, force_ref, next_ref, last_ref, high_ref, low_ref, left_ref, sum_ref,
        edge_ref, edges, partial, sums, drive, drives, ways, returned, box_last,
        load_sem, send_sem, recv_sem, share_send, share_recv, edge_send, edge_recv,
        sum_send, sum_recv, drive_send, drive_recv, way_send, way_recv, out_sem,
    ) = refs[2 * INPUTS + 2 :]
    (
        angle_ref, slot_ref, spring_ref, mass_ref, weight_ref, now_ref, before_ref,
        rows_ref, target_ref, lower_ref, upper_ref, value_ref, old_ref, deriv_ref,
        radial_ref, shear_ref, node_mass_ref, modes_ref,
    ) = vmem
    i = lax.axis_index("mer")
    j = lax.axis_index("box")
    above = lax.rem(i + 1, MER)
    below = lax.rem(i + MER - 1, MER)

    loads = [pltpu.make_async_copy(hbm[k], vmem[k], load_sem.at[k]) for k in range(INPUTS)]
    for load in loads:
        load.start()
    barrier = pltpu.get_barrier_semaphore()
    for o in range(1, MER):
        pl.semaphore_signal(
            barrier, inc=1, device_id=(lax.rem(i + o, MER), j), device_id_type=MESH)
    for o in range(1, BOX):
        pl.semaphore_signal(
            barrier, inc=1, device_id=(i, lax.rem(j + o, BOX)), device_id_type=MESH)

    def way(source, target, send, recv, device):
        return pltpu.make_async_remote_copy(
            src_ref=source, dst_ref=target, send_sem=send, recv_sem=recv,
            device_id=device, device_id_type=MESH)

    def to_part(o):
        q = lax.rem(i + o, MER)
        return way(send_ref.at[lax.div(q, 2)], received.at[i], send_sem.at[o], recv_sem.at[o], (q, j))

    def to_share(o):
        q = lax.rem(j + o, BOX)
        return way(share, shared.at[j], share_send.at[o], share_recv.at[o], (i, q))

    def to_sum(step, o):
        q = lax.rem(j + BOX - o, BOX)
        return way(partial.at[step, q], sums.at[step, o],
                   sum_send.at[step, o], sum_recv.at[step, o], (i, q))

    def to_drive(step, o):
        q = lax.rem(j + o, BOX)
        return way(drive.at[step], drives.at[step, j],
                   drive_send.at[step, o], drive_recv.at[step, o], (i, q))

    def to_back(o):
        q = lax.rem(i + o, MER)
        return way(ways.at[lax.div(q, 2)], returned.at[i], way_send.at[o], way_recv.at[o], (q, j))

    def to_edges(step):
        return (
            way(edge_ref.at[step, 2:4], edges.at[step, 0:2],
                edge_send.at[step, 0], edge_recv.at[step, 0], (above, j)),
            way(edge_ref.at[step, 0:2], edges.at[step, 2:4],
                edge_send.at[step, 1], edge_recv.at[step, 1], (below, j)),
        )

    def repeat(first, last, work):
        def body(o, carry):
            work(o)
            return carry

        lax.fori_loop(first, last, body, 0)

    for load in loads[:7]:
        load.wait()
    order_nodes([ref[...] for ref in vmem[:7]], dest_ref, send_ref, fields)
    pl.semaphore_wait(barrier, MER + BOX - 2)
    repeat(1, MER, lambda o: to_part(o).start())
    received[i] = send_ref[lax.div(i, 2)]
    for load in loads[7:]:
        load.wait()
    slot_table(rows_ref[...], target_ref[...], (lower_ref[...], upper_ref[...]), node_ref, elem_ref)
    fill_table(value_ref, node_ref, elem_ref, table_ref)

    repeat(1, MER, lambda o: to_part(o).wait_recv())
    half = lax.rem(i, 2)
    own = []
    for f in range(7):
        even = jnp.concatenate([received[2 * r, f : f + 1, :] for r in range(8)], axis=0)
        odd = jnp.concatenate([received[2 * r + 1, f : f + 1, :] for r in range(8)], axis=0)
        own.append(halves(even, odd, half))
    share[0] = own[0]
    share[1] = own[1]
    repeat(1, BOX, lambda o: to_share(o).start())
    shared[j] = share[...]
    spring, mass, weight, box_now, box_before = own[2:]

    def forces(step, ref):
        compute_force(j, ref, deriv_ref, radial_ref, shear_ref, force_ref)
        edge_forces(force_ref, node_ref, elem_ref, edge_ref.at[step])
        for copy in to_edges(step):
            copy.start()

    def sample_block(step, block):
        partial[step, block] = sample_nodes(
            table_ref, shared[block, 1].astype(I32), block, harmonic_ref)

    def pulls(step, now):
        sample = partial[step, j]
        for o in range(1, BOX):
            to_sum(step, o).wait_recv()
            sample = sample + sums[step, o]
        pull = spring * (sample - now)
        drive[step] = -weight * pull
        repeat(1, BOX, lambda o: to_drive(step, o).start())
        drives[step, j] = drive[step]
        return pull

    def react(step, block):
        slot_reactions(drives[step, block], shared[block, 1].astype(I32), block,
                       harmonic_ref, high_ref, low_ref)
        scatter_slots(block * 2, node_ref, elem_ref, high_ref, low_ref, left_ref, sum_ref)

    def reactions(step):
        sum_ref[...] = jnp.zeros_like(sum_ref)
        react(step, j)

        def work(o):
            to_drive(step, o).wait_recv()
            react(step, lax.rem(j + BOX - o, BOX))

        repeat(1, BOX, work)
        for copy in to_edges(step):
            copy.wait_recv()
        for g in range(4):
            ghost = (i == 0) if g < 2 else (i == MER - 1)
            high, low = split2(jnp.where(ghost, 0.0, edges[step, g]))
            high_ref[GROUPS + g] = high
            low_ref[GROUPS + g] = low
        scatter_slots(GROUPS // 2, node_ref, elem_ref, high_ref, low_ref, left_ref, sum_ref)

    forces(0, value_ref)

    def enter(block):
        harmonics(j, shared[block, 0], block, harmonic_ref)
        sample_block(0, block)

    enter(j)

    def enter_peer(o):
        to_share(o).wait_recv()
        enter(lax.rem(j + BOX - o, BOX))
        to_sum(0, o).start()

    repeat(1, BOX, enter_peer)
    pull = pulls(0, box_now)
    box_next = 2.0 * box_now - box_before + STEP_SCALE * pull / mass
    reactions(0)
    advance(j, value_ref, old_ref, force_ref, sum_ref, node_mass_ref, modes_ref, next_ref)

    fill_table(next_ref, node_ref, elem_ref, table_ref)

    def sample_peer(o):
        sample_block(1, lax.rem(j + BOX - o, BOX))
        to_sum(1, o).start()

    repeat(1, BOX, sample_peer)
    sample_block(1, j)
    forces(1, next_ref)
    pull = pulls(1, box_next)
    box_after = 2.0 * box_next - box_now + STEP_SCALE * pull / mass
    for m in range(8):
        ways[m] = jnp.broadcast_to(box_after[m : m + 1, :], (8, 128))
    repeat(1, MER, lambda o: to_back(o).start())
    returned[i] = ways[lax.div(i, 2)]
    reactions(1)
    advance(j, next_ref, value_ref, force_ref, sum_ref, node_mass_ref, modes_ref, last_ref)
    result = pltpu.make_async_copy(last_ref, out_ref, out_sem.at[0])
    result.start()

    repeat(1, MER, lambda o: to_back(o).wait_recv())
    even = jnp.concatenate([returned[2 * r, 0:1, :] for r in range(8)], axis=0)
    odd = jnp.concatenate([returned[2 * r + 1, 0:1, :] for r in range(8)], axis=0)
    box = halves(even, odd, half)
    line = jnp.concatenate([box[m : m + 1, :] for m in range(8)], axis=1)
    pieces = jnp.concatenate([piece.astype(F32) for piece in split3(line)], axis=0).astype(BF16)
    for r in range(8):
        out = dot(pieces, hot(iota((1024, 128), 0) == dest_ref[r : r + 1, :]))
        box_last[r : r + 1, :] = out[0:1] + (out[1:2] + out[2:3])
    box_result = pltpu.make_async_copy(box_last, box_out_ref, out_sem.at[1])
    box_result.start()

    def sent(o):
        to_share(o).wait_send()
        for step in range(2):
            to_sum(step, o).wait_send()
            to_drive(step, o).wait_send()

    repeat(1, BOX, sent)

    def sent_far(o):
        to_part(o).wait_send()
        to_back(o).wait_send()

    repeat(1, MER, sent_far)
    for step in range(2):
        for copy in to_edges(step):
            copy.wait_send()
    result.wait()
    box_result.wait()


def per_device(
    annulus, annulus_prev, derivative, radial_modulus, shear_modulus, node_mass, element_modes,
    upper_rows, lower_rows, coupling_rows, coupling_target, box_field, box_prev, box_angle,
    box_spring, box_mass, box_weight, box_slot,
):
    flat = NODES * COLS
    args = [
        x.reshape(8, 128)
        for x in (box_angle, box_slot, box_spring, box_mass, box_weight, box_field, box_prev)
    ] + [
        coupling_rows.reshape(16, 128), coupling_target.reshape(16, 128),
        lower_rows.reshape(2, 128), upper_rows.reshape(2, 128),
        annulus.reshape(flat, ELEMS), annulus_prev.reshape(flat, ELEMS), derivative,
        radial_modulus, shear_modulus, node_mass, element_modes.reshape(1, ELEMS),
    ]
    vmem = pltpu.VMEM
    scratch = [vmem(x.shape, x.dtype) for x in args] + [
        vmem((8, 8, 128), F32),
        vmem((8, 128), I32),
        vmem((8, 8, 128), F32),
        vmem((ALL_GROUPS, 128), I32),
        vmem((ALL_GROUPS, 128), I32),
        vmem((MER, 8, 128), F32),
        vmem((2, 8, 128), F32),
        vmem((BOX, 2, 8, 128), F32),
        vmem((ROWS, COLS, 128), F32),
        vmem((GROUPS, COLS, 128), F32),
        vmem((flat, ELEMS), F32),
        vmem((flat, ELEMS), F32),
        vmem((flat, ELEMS), F32),
        vmem((ALL_GROUPS, COLS, 128), BF16),
        vmem((ALL_GROUPS, COLS, 128), BF16),
        vmem((PAIRS * COLS, 512), BF16),
        vmem((PAIRS * COLS, 256), F32),
        vmem((2, 4, COLS, 128), F32),
        vmem((2, 4, COLS, 128), F32),
        vmem((2, BOX, 8, 128), F32),
        vmem((2, BOX, 8, 128), F32),
        vmem((2, 8, 128), F32),
        vmem((2, BOX, 8, 128), F32),
        vmem((8, 8, 128), F32),
        vmem((MER, 8, 128), F32),
        vmem((8, 128), F32),
    ]
    dma = pltpu.SemaphoreType.DMA
    scratch += [dma((INPUTS,))] + [dma((MER,))] * 2 + [dma((BOX,))] * 2 + [dma((2, 2))] * 2
    scratch += [dma((2, BOX))] * 4 + [dma((MER,))] * 2 + [dma((2,))]
    any_space = pl.BlockSpec(memory_space=pl.ANY)
    final, box_out = pl.pallas_call(
        whole_kernel,
        out_shape=[jax.ShapeDtypeStruct((flat, ELEMS), F32), jax.ShapeDtypeStruct((8, 128), F32)],
        in_specs=[any_space] * INPUTS,
        out_specs=[any_space] * 2,
        scratch_shapes=scratch,
        compiler_params=pltpu.CompilerParams(
            vmem_limit_bytes=56 << 20, collective_id=0, has_side_effects=True),
        name="coupled_steps",
    )(*args)
    return final.reshape(NODES, COLS, ELEMS), box_out.reshape(1024)


def solution(mesh):
    mer_box = P(("mer", "box"))
    in_specs = (
        P(None, "box", "mer"), P(None, "box", "mer"), P(),
        P(None, "mer"), P(None, "mer"), P(None, "mer"),
        P("mer"), P("mer"), P("mer"), P("mer"), P("mer", None),
        mer_box, mer_box, mer_box, mer_box, mer_box, mer_box, mer_box,
    )
    return jax.shard_map(
        per_device, mesh=mesh, in_specs=in_specs,
        out_specs=(P(None, "box", "mer"), mer_box), check_vma=False,
    )
```

```python
import jax
import jax.numpy as jnp
from jax import lax
from jax.experimental import pallas as pl
from jax.experimental.pallas import tpu as pltpu
from jax.sharding import PartitionSpec as P

F32 = jnp.float32
BF16 = jnp.bfloat16
I32 = jnp.int32
MESH = pl.DeviceIdType.MESH

MER, BOX = 16, 8
MODES = 256
NODES, COLS, ELEMS = 25, 64, 128
PAIRS = 13
GROUPS = 32
ALL_GROUPS = 36
ROWS = 64
STEP_SCALE = 0.25


def iota(shape, dim):
    return lax.broadcasted_iota(I32, shape, dim)


def hot(mask):
    return jnp.where(mask, 1.0, 0.0).astype(BF16)


def dot(a, b):
    return jnp.dot(a, b, preferred_element_type=F32)


def dot_nt(a, b):
    return lax.dot_general(a, b, (((1,), (1,)), ((), ())), preferred_element_type=F32)


def split2(x):
    hi = x.astype(BF16)
    return hi, (x - hi.astype(F32)).astype(BF16)


def split3(x):
    hi = x.astype(BF16)
    rest = x - hi.astype(F32)
    mid = rest.astype(BF16)
    return hi, mid, (rest - mid.astype(F32)).astype(BF16)


def take_lanes(x, index):
    return jnp.take_along_axis(x, index, axis=1, mode="promise_in_bounds")


def sincos(x):
    k = jnp.floor(x * 0.6366197723675814 + 0.5)
    r = x - k * 1.5703125
    r = r - k * 4.837512969970703125e-4
    r = r - k * 7.54978995489188216e-8
    z = r * r
    s = ((-1.9515295891e-4 * z + 8.3321608736e-3) * z - 1.6666654611e-1) * z * r + r
    c = ((2.443315711809948e-5 * z - 1.388731625493765e-3) * z + 4.166664568298827e-2) * z * z
    c = c - 0.5 * z + 1.0
    q = k.astype(I32)
    odd = (q & 1) == 1
    sine = jnp.where(odd, c, s)
    cosine = jnp.where(odd, s, c)
    sine = jnp.where((q & 2) == 2, -sine, sine)
    cosine = jnp.where(((q + 1) & 2) == 2, -cosine, cosine)
    return sine, cosine


def before_lane():
    return hot(iota((128, 128), 0) < iota((128, 128), 1))


def order_nodes(sources, dest_ref, send_ref, fields):
    tri = before_lane()
    part = sources[1] & (MER - 1)
    values = [sources[0], (sources[1] >> 4).astype(F32)] + list(sources[2:])
    for r in range(8):
        for f in range(7):
            fields[r, f : f + 1, :] = values[f][r : r + 1, :]
        fields[r, 7:8, :] = jnp.zeros((1, 128), F32)
    base = jnp.zeros((MER, 1), F32)
    total = jnp.zeros((24, 1024), F32)
    for r in range(8):
        mine = part[r : r + 1, :]
        member = jnp.where(iota((MER, 128), 0) == mine, 1.0, 0.0)
        rank = dot(member.astype(BF16), tri) + base
        place = jnp.sum(member * rank, axis=0, keepdims=True).astype(I32)
        base = base + jnp.sum(member, axis=1, keepdims=True)
        dest = mine * 64 + place
        dest_ref[r : r + 1, :] = dest
        order = hot(iota((1024, 128), 0) == dest)
        pieces = jnp.concatenate(split3(fields[r]), axis=0)
        total = total + dot_nt(pieces, order)
    sorted_fields = total[0:8] + (total[8:16] + total[16:24])
    for m in range(8):
        send_ref[m] = sorted_fields[:, m * 128 : (m + 1) * 128]


def slot_table(rows, target, edges, node_ref, elem_ref):
    tri = before_lane()
    reader = (target & (BOX - 1)) * MER + (target >> 3)
    node1 = ((rows >> 7) + 1).astype(F32)
    elem = (rows & 127).astype(F32)
    count = jnp.zeros((128, 1), F32)
    table = jnp.zeros((64, 128), F32)
    for r in range(16):
        mine = reader[r : r + 1, :]
        member = jnp.where(iota((128, 128), 0) == mine, 1.0, 0.0)
        rank = dot(member.astype(BF16), tri) + count
        place = jnp.sum(member * rank, axis=0, keepdims=True).astype(I32)
        count = count + jnp.sum(member, axis=1, keepdims=True)
        lane = (mine & 3) * 32 + place
        group = iota((GROUPS, 128), 0) == (mine >> 2)
        values = jnp.concatenate(
            [
                jnp.where(group, jnp.broadcast_to(node1[r : r + 1, :], (GROUPS, 128)), 0.0),
                jnp.where(group, jnp.broadcast_to(elem[r : r + 1, :], (GROUPS, 128)), 0.0),
            ],
            axis=0,
        ).astype(BF16)
        table = table + dot_nt(values, hot(iota((128, 128), 0) == lane))
    node_ref[0:GROUPS, :] = table[0:GROUPS].astype(I32) - 1
    elem_ref[0:GROUPS, :] = table[GROUPS : 2 * GROUPS].astype(I32)
    for k, edge in enumerate(edges):
        node_ref[GROUPS + 2 * k : GROUPS + 2 * k + 2, :] = edge >> 7
        elem_ref[GROUPS + 2 * k : GROUPS + 2 * k + 2, :] = edge & 127


def halves(even, odd, half):
    low = jnp.where(half == 0, even, pltpu.roll(even, 64, 1))
    high = jnp.where(half == 1, odd, pltpu.roll(odd, 64, 1))
    return jnp.where(iota((8, 128), 1) < 64, low, high)


def harmonics(j, angles, block, harmonic_ref):
    sub = iota((8, 128), 0).astype(F32)
    first = (lax.rem(j, 4) * 64).astype(F32)
    is_sine = j >= 4
    for r in range(8):
        angle = jnp.broadcast_to(angles[r : r + 1, :], (8, 128))
        base_sin, base_cos = sincos(angle * (sub + first))
        step_sin, step_cos = sincos(angle * (sub * 8.0))
        a = jnp.where(is_sine, base_sin, base_cos)
        b = jnp.where(is_sine, -base_cos, base_sin)
        for t in range(8):
            harmonic_ref[block * 8 + r, t * 8 : (t + 1) * 8, :] = (
                a * step_cos[t : t + 1, :] - b * step_sin[t : t + 1, :]
            )


def gather_rows(values_ref, node, elem):
    index = jnp.broadcast_to(elem, (8, 128))
    node = jnp.broadcast_to(node, (8, 128))
    acc = [jnp.zeros((8, 128), F32) for _ in range(8)]
    for a in range(NODES):
        mask = node == a
        for c in range(8):
            taken = take_lanes(values_ref[a * 64 + c * 8 : a * 64 + c * 8 + 8, :], index)
            acc[c] = jnp.where(mask, taken, acc[c])
    return acc


MATRIX_GROUPS, LANE_GROUPS = 6, 2


def keep_pieces(values, a, pieces_ref):
    rows = slice((a // 2) * 64, (a // 2) * 64 + 64)
    lane = (a % 2) * 128
    high, low = split2(values)
    pieces_ref[rows, lane : lane + 128] = high
    pieces_ref[rows, 256 + lane : 384 + lane] = low


def slot_hots(node_ref, elem_ref, hot_ref):
    def body(g, carry):
        lane = (node_ref[pl.ds(g, 1), :] & 1) * 128 + elem_ref[pl.ds(g, 1), :]
        hot_ref[g] = hot(iota((256, 128), 0) == lane)
        return carry

    lax.fori_loop(0, ALL_GROUPS, body, 0)


def fill_table(values_ref, pieces_ref, hot_ref, node_ref, elem_ref, table_ref):
    def body(t, carry):
        first = t * (MATRIX_GROUPS + LANE_GROUPS)
        right = jnp.concatenate([hot_ref[first + k] for k in range(MATRIX_GROUPS)], axis=1)
        out = dot(pieces_ref[...], jnp.concatenate([right, right], axis=0))
        for k in range(LANE_GROUPS):
            g = first + MATRIX_GROUPS + k
            acc = gather_rows(values_ref, node_ref[pl.ds(g, 1), :], elem_ref[pl.ds(g, 1), :])
            for c in range(8):
                table_ref[g, c * 8 : (c + 1) * 8, :] = acc[c]
        for k in range(MATRIX_GROUPS):
            g = first + k
            pair = node_ref[pl.ds(g, 1), :] >> 1
            acc = jnp.zeros((COLS, 128), F32)
            for a in range(PAIRS):
                acc = jnp.where(
                    pair == a, out[a * 64 : (a + 1) * 64, k * 128 : (k + 1) * 128], acc)
            table_ref[g] = acc
        return carry

    lax.fori_loop(0, GROUPS // (MATRIX_GROUPS + LANE_GROUPS), body, 0)


def node_lane(place, odd):
    return place + (iota((1, 128), 1) >> 6) * 32 + odd * 64


def sample_nodes(table_ref, places, block, harmonic_ref):
    rows = []
    for r in range(8):
        index = jnp.broadcast_to(node_lane(places[r : r + 1, :], r % 2), (8, 128))
        group = block * 4 + r // 2
        acc = jnp.zeros((8, 128), F32)
        for c in range(8):
            taken = take_lanes(table_ref[group, c * 8 : (c + 1) * 8, :], index)
            acc = acc + taken * harmonic_ref[block * 8 + r, c * 8 : (c + 1) * 8, :]
        rows.append(jnp.sum(acc, axis=0, keepdims=True))
    return jnp.concatenate(rows, axis=0)


def small_stack(matrix):
    high, low = split2(matrix)
    return jnp.concatenate([high, high, low], axis=1)


def compute_force(j, values_ref, deriv_ref, radial_ref, shear_ref, force_ref):
    deriv = deriv_ref[...]
    stack = small_stack(deriv[0:32, 0:32])
    stack_t = small_stack(deriv.T[0:32, 0:32])
    radial = jnp.concatenate([radial_ref[...], jnp.zeros((7, 128), F32)], axis=0)
    radial = jnp.concatenate([radial] * 16, axis=1)
    shear = shear_ref[...]
    first = lax.rem(j, 4) * 64

    def times(left, x):
        high, low = split2(x)
        return dot(left, jnp.concatenate([high, low, high], axis=0))

    def body(k, carry):
        x = jnp.concatenate(
            [values_ref[pl.ds(k * 16 + c, 32, stride=64), :] for c in range(16)], axis=1
        )
        back = times(stack_t, times(stack, x) * radial)
        for c in range(16):
            wave = (first + k * 16 + c).astype(F32) * (2.0 / MODES)
            lanes = slice(c * 128, (c + 1) * 128)
            force_ref[pl.ds(k * 16 + c, NODES, stride=64), :] = (
                -back[0:NODES, lanes] - shear * (wave * wave) * x[0:NODES, lanes]
            )
        return carry

    lax.fori_loop(0, 4, body, 0)


def edge_forces(force_ref, node_ref, elem_ref, edge_ref):
    def body(g, carry):
        acc = gather_rows(
            force_ref, node_ref[pl.ds(GROUPS + g, 1), :], elem_ref[pl.ds(GROUPS + g, 1), :]
        )
        for c in range(8):
            edge_ref[g, c * 8 : (c + 1) * 8, :] = acc[c]
        return carry

    lax.fori_loop(0, 4, body, 0)


def slot_reactions(drives, places, block, harmonic_ref, high_ref, low_ref):
    for k in range(4):
        pieces, hots = [], []
        for odd in range(2):
            r = 2 * k + odd
            x = harmonic_ref[block * 8 + r] * drives[r : r + 1, :]
            pieces.append(split2(x))
            lane = node_lane(places[r : r + 1, :], odd)
            hots.append(hot(iota((128, 128), 0) == lane))
        left = jnp.concatenate([pieces[0][0], pieces[1][0], pieces[0][1], pieces[1][1]], axis=1)
        right = jnp.concatenate(hots + hots, axis=1)
        high, low = split2(dot_nt(left, right))
        high_ref[block * 4 + k] = high
        low_ref[block * 4 + k] = low


def scatter_slots(first, node_ref, hot_ref, high_ref, low_ref, left_ref, sum_ref):
    rights = []
    for h in range(4):
        pair = node_ref[pl.ds(first + h, 1), :] >> 1
        high = high_ref[first + h]
        low = low_ref[first + h]
        for a in range(PAIRS):
            mask = jnp.broadcast_to(hot(pair == a), (COLS, 128))
            rows = slice(a * 64, (a + 1) * 64)
            left_ref[rows, h * 128 : (h + 1) * 128] = high * mask
            left_ref[rows, 512 + h * 128 : 640 + h * 128] = low * mask
        rights.append(hot_ref[first + h])
    sum_ref[...] += dot_nt(left_ref[...], jnp.concatenate(rights + rights, axis=1))


def advance(j, now_ref, before_ref, force_ref, sum_ref, mass_ref, modes_ref, next_ref,
            pieces_ref=None):
    order = lax.rem(j, 4) * 64 + iota((COLS, 128), 0)
    live = jnp.where(order < modes_ref[...], STEP_SCALE, 0.0)
    for a in range(NODES):
        rows = slice(a * 64, (a + 1) * 64)
        pair = a // 2
        lanes = slice((a % 2) * 128, (a % 2) * 128 + 128)
        total = force_ref[rows, :] + sum_ref[pair * 64 : (pair + 1) * 64, lanes]
        after = 2.0 * now_ref[rows, :] - before_ref[rows, :] + live * total / mass_ref[a : a + 1, :]
        next_ref[rows, :] = after
        if pieces_ref is not None:
            keep_pieces(after, a, pieces_ref)


INPUTS = 18
VALUES = 11
PADDED = 32 * COLS


def whole_kernel(*refs):
    hbm = refs[:INPUTS]
    out_ref, box_out_ref = refs[INPUTS : INPUTS + 2]
    vmem = refs[INPUTS + 2 : 2 * INPUTS + 2]
    (
        fields, dest_ref, send_ref, node_ref, elem_ref, received, share, shared, harmonic_ref,
        table_ref, force_ref, next_ref, last_ref, high_ref, low_ref, left_ref, sum_ref,
        edge_ref, edges, partial, sums, drive, drives, ways, returned, box_last,
        pieces_ref, hot_ref, square_ref,
        load_sem, send_sem, recv_sem, share_send, share_recv, edge_send, edge_recv,
        sum_send, sum_recv, drive_send, drive_recv, way_send, way_recv, out_sem,
    ) = refs[2 * INPUTS + 2 :]
    (
        angle_ref, slot_ref, spring_ref, mass_ref, weight_ref, now_ref, before_ref,
        rows_ref, target_ref, lower_ref, upper_ref, value_ref, old_ref, deriv_ref,
        radial_ref, shear_ref, node_mass_ref, modes_ref,
    ) = vmem
    i = lax.axis_index("mer")
    j = lax.axis_index("box")
    above = lax.rem(i + 1, MER)
    below = lax.rem(i + MER - 1, MER)

    def landing(k):
        if k == VALUES:
            return value_ref.at[0 : NODES * COLS]
        return vmem[k]

    loads = [pltpu.make_async_copy(hbm[k], landing(k), load_sem.at[k]) for k in range(INPUTS)]
    for load in loads:
        load.start()
    barrier = pltpu.get_barrier_semaphore()
    for o in range(1, MER):
        pl.semaphore_signal(
            barrier, inc=1, device_id=(lax.rem(i + o, MER), j), device_id_type=MESH)
    for o in range(1, BOX):
        pl.semaphore_signal(
            barrier, inc=1, device_id=(i, lax.rem(j + o, BOX)), device_id_type=MESH)

    def way(source, target, send, recv, device):
        return pltpu.make_async_remote_copy(
            src_ref=source, dst_ref=target, send_sem=send, recv_sem=recv,
            device_id=device, device_id_type=MESH)

    def to_part(o):
        q = lax.rem(i + o, MER)
        return way(send_ref.at[lax.div(q, 2)], received.at[i], send_sem.at[o], recv_sem.at[o], (q, j))

    def to_share(o):
        q = lax.rem(j + o, BOX)
        return way(share, shared.at[j], share_send.at[o], share_recv.at[o], (i, q))

    def to_sum(step, o):
        q = lax.rem(j + BOX - o, BOX)
        return way(partial.at[step, q], sums.at[step, o],
                   sum_send.at[step, o], sum_recv.at[step, o], (i, q))

    def to_drive(step, o):
        q = lax.rem(j + o, BOX)
        return way(drive.at[step], drives.at[step, j],
                   drive_send.at[step, o], drive_recv.at[step, o], (i, q))

    def to_back(o):
        q = lax.rem(i + o, MER)
        return way(ways.at[lax.div(q, 2)], returned.at[i], way_send.at[o], way_recv.at[o], (q, j))

    def to_edges(step):
        return (
            way(edge_ref.at[step, 2:4], edges.at[step, 0:2],
                edge_send.at[step, 0], edge_recv.at[step, 0], (above, j)),
            way(edge_ref.at[step, 0:2], edges.at[step, 2:4],
                edge_send.at[step, 1], edge_recv.at[step, 1], (below, j)),
        )

    def repeat(first, last, work):
        def body(o, carry):
            work(o)
            return carry

        lax.fori_loop(first, last, body, 0)

    for load in loads[:7]:
        load.wait()
    order_nodes([ref[...] for ref in vmem[:7]], dest_ref, send_ref, fields)
    pl.semaphore_wait(barrier, MER + BOX - 2)
    repeat(1, MER, lambda o: to_part(o).start())
    received[i] = send_ref[lax.div(i, 2)]
    for load in loads[7:]:
        load.wait()
    slot_table(rows_ref[...], target_ref[...], (lower_ref[...], upper_ref[...]), node_ref, elem_ref)
    slot_hots(node_ref, elem_ref, hot_ref)
    square_ref[...] = jnp.zeros_like(square_ref)
    square_ref[0:NODES, 0:NODES] = deriv_ref[...]
    for ref in (value_ref, next_ref):
        ref[NODES * COLS : PADDED, :] = jnp.zeros((PADDED - NODES * COLS, ELEMS), F32)
    for a in range(NODES):
        keep_pieces(value_ref[a * COLS : (a + 1) * COLS, :], a, pieces_ref)
    for lane in (128, 384):
        pieces_ref[(PAIRS - 1) * COLS : PAIRS * COLS, lane : lane + 128] = jnp.zeros(
            (COLS, 128), BF16)
    fill_table(value_ref, pieces_ref, hot_ref, node_ref, elem_ref, table_ref)

    repeat(1, MER, lambda o: to_part(o).wait_recv())
    half = lax.rem(i, 2)
    own = []
    for f in range(7):
        even = jnp.concatenate([received[2 * r, f : f + 1, :] for r in range(8)], axis=0)
        odd = jnp.concatenate([received[2 * r + 1, f : f + 1, :] for r in range(8)], axis=0)
        own.append(halves(even, odd, half))
    share[0] = own[0]
    share[1] = own[1]
    repeat(1, BOX, lambda o: to_share(o).start())
    shared[j] = share[...]
    spring, mass, weight, box_now, box_before = own[2:]

    def forces(step, ref):
        compute_force(j, ref, square_ref, radial_ref, shear_ref, force_ref)
        edge_forces(force_ref, node_ref, elem_ref, edge_ref.at[step])
        for copy in to_edges(step):
            copy.start()

    def sample_block(step, block):
        partial[step, block] = sample_nodes(
            table_ref, shared[block, 1].astype(I32), block, harmonic_ref)

    def pulls(step, now):
        sample = partial[step, j]
        for o in range(1, BOX):
            to_sum(step, o).wait_recv()
            sample = sample + sums[step, o]
        pull = spring * (sample - now)
        drive[step] = -weight * pull
        repeat(1, BOX, lambda o: to_drive(step, o).start())
        drives[step, j] = drive[step]
        return pull

    def react(step, block):
        slot_reactions(drives[step, block], shared[block, 1].astype(I32), block,
                       harmonic_ref, high_ref, low_ref)
        scatter_slots(block * 4, node_ref, hot_ref, high_ref, low_ref, left_ref, sum_ref)

    def reactions(step):
        sum_ref[...] = jnp.zeros_like(sum_ref)
        react(step, j)

        def work(o):
            to_drive(step, o).wait_recv()
            react(step, lax.rem(j + BOX - o, BOX))

        repeat(1, BOX, work)
        for copy in to_edges(step):
            copy.wait_recv()
        for g in range(4):
            ghost = (i == 0) if g < 2 else (i == MER - 1)
            high, low = split2(jnp.where(ghost, 0.0, edges[step, g]))
            high_ref[GROUPS + g] = high
            low_ref[GROUPS + g] = low
        scatter_slots(GROUPS, node_ref, hot_ref, high_ref, low_ref, left_ref, sum_ref)

    forces(0, value_ref)

    def enter(block):
        harmonics(j, shared[block, 0], block, harmonic_ref)
        sample_block(0, block)

    enter(j)

    def enter_peer(o):
        to_share(o).wait_recv()
        enter(lax.rem(j + BOX - o, BOX))
        to_sum(0, o).start()

    repeat(1, BOX, enter_peer)
    pull = pulls(0, box_now)
    box_next = 2.0 * box_now - box_before + STEP_SCALE * pull / mass
    reactions(0)
    advance(j, value_ref, old_ref, force_ref, sum_ref, node_mass_ref, modes_ref, next_ref,
            pieces_ref)

    fill_table(next_ref, pieces_ref, hot_ref, node_ref, elem_ref, table_ref)

    def sample_peer(o):
        sample_block(1, lax.rem(j + BOX - o, BOX))
        to_sum(1, o).start()

    repeat(1, BOX, sample_peer)
    sample_block(1, j)
    forces(1, next_ref)
    pull = pulls(1, box_next)
    box_after = 2.0 * box_next - box_now + STEP_SCALE * pull / mass
    for m in range(8):
        ways[m] = jnp.broadcast_to(box_after[m : m + 1, :], (8, 128))
    repeat(1, MER, lambda o: to_back(o).start())
    returned[i] = ways[lax.div(i, 2)]
    reactions(1)
    advance(j, next_ref, value_ref, force_ref, sum_ref, node_mass_ref, modes_ref, last_ref)
    result = pltpu.make_async_copy(last_ref, out_ref, out_sem.at[0])
    result.start()

    repeat(1, MER, lambda o: to_back(o).wait_recv())
    even = jnp.concatenate([returned[2 * r, 0:1, :] for r in range(8)], axis=0)
    odd = jnp.concatenate([returned[2 * r + 1, 0:1, :] for r in range(8)], axis=0)
    box = halves(even, odd, half)
    line = jnp.concatenate([box[m : m + 1, :] for m in range(8)], axis=1)
    pieces = jnp.concatenate([piece.astype(F32) for piece in split3(line)], axis=0).astype(BF16)
    for r in range(8):
        out = dot(pieces, hot(iota((1024, 128), 0) == dest_ref[r : r + 1, :]))
        box_last[r : r + 1, :] = out[0:1] + (out[1:2] + out[2:3])
    box_result = pltpu.make_async_copy(box_last, box_out_ref, out_sem.at[1])
    box_result.start()

    def sent(o):
        to_share(o).wait_send()
        for step in range(2):
            to_sum(step, o).wait_send()
            to_drive(step, o).wait_send()

    repeat(1, BOX, sent)

    def sent_far(o):
        to_part(o).wait_send()
        to_back(o).wait_send()

    repeat(1, MER, sent_far)
    for step in range(2):
        for copy in to_edges(step):
            copy.wait_send()
    result.wait()
    box_result.wait()


PIECES = 8


def hand_over_kernel(final_ref, box_ref, out_ref, box_out_ref, sem):
    rows = NODES * COLS // PIECES
    copies = [
        pltpu.make_async_copy(
            final_ref.at[k * rows : (k + 1) * rows], out_ref.at[k * rows : (k + 1) * rows],
            sem.at[k])
        for k in range(PIECES)
    ]
    copies.append(pltpu.make_async_copy(box_ref, box_out_ref, sem.at[PIECES]))
    for copy in copies:
        copy.start()
    for copy in copies:
        copy.wait()


def per_device(
    annulus, annulus_prev, derivative, radial_modulus, shear_modulus, node_mass, element_modes,
    upper_rows, lower_rows, coupling_rows, coupling_target, box_field, box_prev, box_angle,
    box_spring, box_mass, box_weight, box_slot,
):
    flat = NODES * COLS
    args = [
        x.reshape(8, 128)
        for x in (box_angle, box_slot, box_spring, box_mass, box_weight, box_field, box_prev)
    ] + [
        coupling_rows.reshape(16, 128), coupling_target.reshape(16, 128),
        lower_rows.reshape(2, 128), upper_rows.reshape(2, 128),
        annulus.reshape(flat, ELEMS), annulus_prev.reshape(flat, ELEMS), derivative,
        radial_modulus, shear_modulus, node_mass, element_modes.reshape(1, ELEMS),
    ]
    vmem = pltpu.VMEM
    scratch = [vmem(x.shape, x.dtype) for x in args]
    scratch[VALUES] = vmem((PADDED, ELEMS), F32)
    scratch += [
        vmem((8, 8, 128), F32),
        vmem((8, 128), I32),
        vmem((8, 8, 128), F32),
        vmem((ALL_GROUPS, 128), I32),
        vmem((ALL_GROUPS, 128), I32),
        vmem((MER, 8, 128), F32),
        vmem((2, 8, 128), F32),
        vmem((BOX, 2, 8, 128), F32),
        vmem((ROWS, COLS, 128), F32),
        vmem((GROUPS, COLS, 128), F32),
        vmem((flat, ELEMS), F32),
        vmem((PADDED, ELEMS), F32),
        vmem((flat, ELEMS), F32),
        vmem((ALL_GROUPS, COLS, 128), BF16),
        vmem((ALL_GROUPS, COLS, 128), BF16),
        vmem((PAIRS * COLS, 1024), BF16),
        vmem((PAIRS * COLS, 256), F32),
        vmem((2, 4, COLS, 128), F32),
        vmem((2, 4, COLS, 128), F32),
        vmem((2, BOX, 8, 128), F32),
        vmem((2, BOX, 8, 128), F32),
        vmem((2, 8, 128), F32),
        vmem((2, BOX, 8, 128), F32),
        vmem((8, 8, 128), F32),
        vmem((MER, 8, 128), F32),
        vmem((8, 128), F32),
        vmem((PAIRS * COLS, 512), BF16),
        vmem((ALL_GROUPS, 256, 128), BF16),
        vmem((128, 128), F32),
    ]
    dma = pltpu.SemaphoreType.DMA
    scratch += [dma((INPUTS,))] + [dma((MER,))] * 2 + [dma((BOX,))] * 2 + [dma((2, 2))] * 2
    scratch += [dma((2, BOX))] * 4 + [dma((MER,))] * 2 + [dma((2,))]
    any_space = pl.BlockSpec(memory_space=pl.ANY)
    final, box_out = pl.pallas_call(
        whole_kernel,
        out_shape=[jax.ShapeDtypeStruct((flat, ELEMS), F32), jax.ShapeDtypeStruct((8, 128), F32)],
        in_specs=[any_space] * INPUTS,
        out_specs=[any_space] * 2,
        scratch_shapes=scratch,
        compiler_params=pltpu.CompilerParams(
            vmem_limit_bytes=56 << 20, collective_id=0, has_side_effects=True),
        name="coupled_steps",
    )(*args)
    final, box_out = pl.pallas_call(
        hand_over_kernel,
        out_shape=[jax.ShapeDtypeStruct((flat, ELEMS), F32), jax.ShapeDtypeStruct((8, 128), F32)],
        in_specs=[any_space] * 2,
        out_specs=[any_space] * 2,
        scratch_shapes=[dma((PIECES + 1,))],
        name="hand_over",
    )(final, box_out)
    return final.reshape(NODES, COLS, ELEMS), box_out.reshape(1024)


def solution(mesh):
    mer_box = P(("mer", "box"))
    in_specs = (
        P(None, "box", "mer"), P(None, "box", "mer"), P(),
        P(None, "mer"), P(None, "mer"), P(None, "mer"),
        P("mer"), P("mer"), P("mer"), P("mer"), P("mer", None),
        mer_box, mer_box, mer_box, mer_box, mer_box, mer_box, mer_box,
    )
    return jax.shard_map(
        per_device, mesh=mesh, in_specs=in_specs,
        out_specs=(P(None, "box", "mer"), mer_box), check_vma=False,
    )
```

```python
import jax
import jax.numpy as jnp
from jax import lax
from jax.experimental import pallas as pl
from jax.experimental.pallas import tpu as pltpu
from jax.sharding import PartitionSpec as P

F32 = jnp.float32
BF16 = jnp.bfloat16
I32 = jnp.int32
MESH = pl.DeviceIdType.MESH

MER, BOX = 16, 8
MODES = 256
NODES, COLS, ELEMS = 25, 64, 128
PAIRS = 13
GROUPS = 16
ALL_GROUPS = 20
CHUNKS = 32
ROWS = 64
STEP_SCALE = 0.25


def iota(shape, dim):
    return lax.broadcasted_iota(I32, shape, dim)


def hot(mask):
    return jnp.where(mask, 1.0, 0.0).astype(BF16)


def dot(a, b):
    return jnp.dot(a, b, preferred_element_type=F32)


def dot_nt(a, b):
    return lax.dot_general(a, b, (((1,), (1,)), ((), ())), preferred_element_type=F32)


def split2(x):
    hi = x.astype(BF16)
    return hi, (x - hi.astype(F32)).astype(BF16)


def split3(x):
    hi = x.astype(BF16)
    rest = x - hi.astype(F32)
    mid = rest.astype(BF16)
    return hi, mid, (rest - mid.astype(F32)).astype(BF16)


def take_lanes(x, index):
    return jnp.take_along_axis(x, index, axis=1, mode="promise_in_bounds")


def sincos(x):
    k = jnp.floor(x * 0.6366197723675814 + 0.5)
    r = x - k * 1.5703125
    r = r - k * 4.837512969970703125e-4
    r = r - k * 7.54978995489188216e-8
    z = r * r
    s = ((-1.9515295891e-4 * z + 8.3321608736e-3) * z - 1.6666654611e-1) * z * r + r
    c = ((2.443315711809948e-5 * z - 1.388731625493765e-3) * z + 4.166664568298827e-2) * z * z
    c = c - 0.5 * z + 1.0
    q = k.astype(I32)
    odd = (q & 1) == 1
    sine = jnp.where(odd, c, s)
    cosine = jnp.where(odd, s, c)
    sine = jnp.where((q & 2) == 2, -sine, sine)
    cosine = jnp.where(((q + 1) & 2) == 2, -cosine, cosine)
    return sine, cosine


def before_lane():
    return hot(iota((128, 128), 0) < iota((128, 128), 1))


def order_nodes(sources, dest_ref, send_ref, fields):
    tri = before_lane()
    part = sources[1] & (MER - 1)
    values = [sources[0], (sources[1] >> 4).astype(F32)] + list(sources[2:])
    for r in range(8):
        for f in range(7):
            fields[r, f : f + 1, :] = values[f][r : r + 1, :]
        fields[r, 7:8, :] = jnp.zeros((1, 128), F32)
    base = jnp.zeros((MER, 1), F32)
    total = jnp.zeros((24, 1024), F32)
    for r in range(8):
        mine = part[r : r + 1, :]
        member = jnp.where(iota((MER, 128), 0) == mine, 1.0, 0.0)
        rank = dot(member.astype(BF16), tri) + base
        place = jnp.sum(member * rank, axis=0, keepdims=True).astype(I32)
        base = base + jnp.sum(member, axis=1, keepdims=True)
        dest = mine * 64 + place
        dest_ref[r : r + 1, :] = dest
        order = hot(iota((1024, 128), 0) == dest)
        pieces = jnp.concatenate(split3(fields[r]), axis=0)
        total = total + dot_nt(pieces, order)
    sorted_fields = total[0:8] + (total[8:16] + total[16:24])
    for m in range(8):
        send_ref[m] = sorted_fields[:, m * 128 : (m + 1) * 128]


def pick_rows(shape, source):
    return hot(iota(shape, 1) == source(iota(shape, 0)))


def row_table(rows, target, edges, node_ref, elem_ref, start_ref, count_ref, meta_ref, shift_ref):
    tri = before_lane()
    reader = (target & (BOX - 1)) * MER + (target >> 3)
    node = (rows >> 7).astype(F32)
    elem = (rows & 127).astype(F32)
    readers = iota((128, 128), 0)
    seen = jnp.zeros((128, 128), F32)
    for r in range(16):
        seen = seen + jnp.where(readers == reader[r : r + 1, :], 1.0, 0.0)
    count = jnp.sum(seen, axis=1, keepdims=True)
    wide = jnp.broadcast_to(count, (128, 128)).astype(BF16)
    below = hot(iota((128, 128), 1) < iota((128, 128), 0))
    start = dot(below, wide)
    base = start
    table = jnp.zeros((2 * GROUPS, 128), F32)
    for r in range(16):
        mine = reader[r : r + 1, :]
        member = jnp.where(readers == mine, 1.0, 0.0)
        rank = dot(member.astype(BF16), tri) + base
        place = jnp.sum(member * rank, axis=0, keepdims=True).astype(I32)
        base = base + jnp.sum(member, axis=1, keepdims=True)
        group = iota((GROUPS, 128), 0) == (place >> 7)
        values = jnp.concatenate(
            [
                jnp.where(group, jnp.broadcast_to(node[r : r + 1, :], (GROUPS, 128)), 0.0),
                jnp.where(group, jnp.broadcast_to(elem[r : r + 1, :], (GROUPS, 128)), 0.0),
            ],
            axis=0,
        ).astype(BF16)
        table = table + dot_nt(values, hot(readers == (place & 127)))
    node_ref[0:GROUPS, :] = table[0:GROUPS].astype(I32)
    elem_ref[0:GROUPS, :] = table[GROUPS : 2 * GROUPS].astype(I32)
    for k, edge in enumerate(edges):
        node_ref[GROUPS + 2 * k : GROUPS + 2 * k + 2, :] = edge >> 7
        elem_ref[GROUPS + 2 * k : GROUPS + 2 * k + 2, :] = edge & 127

    high = jnp.floor(start * (1.0 / 16.0))
    parts = [high.astype(BF16), (start - 16.0 * high).astype(BF16)]
    same_half = (iota((128, 128), 0) & 1) == (iota((128, 128), 1) >> 6)

    def halved(x):
        return jnp.where(same_half, x.astype(F32), 0.0).astype(BF16)

    def joined(left, right):
        return (16.0 * dot(left, right[0]) + dot(left, right[1])).astype(I32)

    own = hot((iota((ROWS, 128), 1) >> 1) == iota((ROWS, 128), 0))
    first = joined(pick_rows((ROWS, 128), lambda row: (row >> 1) * 4), parts) >> 7
    start_ref[...] = joined(own, [halved(part) for part in parts]) - 128 * first
    count_ref[...] = dot(own, halved(wide)).astype(I32)
    group = joined(pick_rows((CHUNKS, 128), lambda chunk: chunk * 4), parts) >> 7
    after = joined(pick_rows((CHUNKS, 128), lambda chunk: (chunk + 1) * 4), parts) >> 7
    shift_ref[...] = after - group
    meta_ref[0:CHUNKS, :] = group
    last = jnp.sum(jnp.where(group <= iota((CHUNKS, 128), 1), 1, 0), axis=0, keepdims=True) - 1
    meta_ref[CHUNKS : CHUNKS + 8, :] = jnp.broadcast_to(last, (8, 128))


def halves(even, odd, half):
    low = jnp.where(half == 0, even, pltpu.roll(even, 64, 1))
    high = jnp.where(half == 1, odd, pltpu.roll(odd, 64, 1))
    return jnp.where(iota((8, 128), 1) < 64, low, high)


def harmonics(j, angles, filled, block, harmonic_ref):
    sub = iota((8, 128), 0).astype(F32)
    first = (lax.rem(j, 4) * 64).astype(F32)
    is_sine = j >= 4
    for r in range(8):
        angle = jnp.broadcast_to(angles[r : r + 1, :], (8, 128))
        base_sin, base_cos = sincos(angle * (sub + first))
        step_sin, step_cos = sincos(angle * (sub * 8.0))
        keep = jnp.broadcast_to(filled[r : r + 1, :], (8, 128)) > 0
        a = jnp.where(keep, jnp.where(is_sine, base_sin, base_cos), 0.0)
        b = jnp.where(keep, jnp.where(is_sine, -base_cos, base_sin), 0.0)
        for t in range(8):
            harmonic_ref[block * 8 + r, t * 8 : (t + 1) * 8, :] = (
                a * step_cos[t : t + 1, :] - b * step_sin[t : t + 1, :]
            )


def gather_rows(values_ref, node, elem):
    index = jnp.broadcast_to(elem, (8, 128))
    node = jnp.broadcast_to(node, (8, 128))
    acc = [jnp.zeros((8, 128), F32) for _ in range(8)]
    for a in range(NODES):
        mask = node == a
        for c in range(8):
            taken = take_lanes(values_ref[a * 64 + c * 8 : a * 64 + c * 8 + 8, :], index)
            acc[c] = jnp.where(mask, taken, acc[c])
    return acc


MATRIX_GROUPS, LANE_GROUPS = 6, 2


def keep_pieces(values, a, pieces_ref):
    rows = slice((a // 2) * 64, (a // 2) * 64 + 64)
    lane = (a % 2) * 128
    high, low = split2(values)
    pieces_ref[rows, lane : lane + 128] = high
    pieces_ref[rows, 256 + lane : 384 + lane] = low


def slot_hots(node_ref, elem_ref, hot_ref):
    def body(g, carry):
        lane = (node_ref[pl.ds(g, 1), :] & 1) * 128 + elem_ref[pl.ds(g, 1), :]
        hot_ref[g] = hot(iota((256, 128), 0) == lane)
        return carry

    lax.fori_loop(0, ALL_GROUPS, body, 0)


def fill_table(values_ref, pieces_ref, hot_ref, node_ref, elem_ref, table_ref):
    def body(t, carry):
        first = t * (MATRIX_GROUPS + LANE_GROUPS)
        right = jnp.concatenate([hot_ref[first + k] for k in range(MATRIX_GROUPS)], axis=1)
        out = dot(pieces_ref[...], jnp.concatenate([right, right], axis=0))
        for k in range(LANE_GROUPS):
            g = first + MATRIX_GROUPS + k
            acc = gather_rows(values_ref, node_ref[pl.ds(g, 1), :], elem_ref[pl.ds(g, 1), :])
            for c in range(8):
                table_ref[g, c * 8 : (c + 1) * 8, :] = acc[c]
        for k in range(MATRIX_GROUPS):
            g = first + k
            pair = node_ref[pl.ds(g, 1), :] >> 1
            acc = jnp.zeros((COLS, 128), F32)
            for a in range(PAIRS):
                acc = jnp.where(
                    pair == a, out[a * 64 : (a + 1) * 64, k * 128 : (k + 1) * 128], acc)
            table_ref[g] = acc
        return carry

    lax.fori_loop(0, GROUPS // (MATRIX_GROUPS + LANE_GROUPS), body, 0)


def sample_nodes(table_ref, local_ref, meta_ref, block, harmonic_ref):
    rows = []
    for r in range(8):
        row = block * 8 + r
        group = lax.clamp(0, meta_ref[block * 4 + r // 2, 0], GROUPS)
        local = jnp.broadcast_to(local_ref[pl.ds(row, 1), :], (8, 128))
        index = local & 127
        second = local > 127
        acc = jnp.zeros((8, 128), F32)
        for c in range(8):
            columns = slice(c * 8, (c + 1) * 8)
            taken = jnp.where(
                second,
                take_lanes(table_ref[group + 1, columns, :], index),
                take_lanes(table_ref[group, columns, :], index),
            )
            acc = acc + taken * harmonic_ref[row, columns, :]
        rows.append(jnp.sum(acc, axis=0, keepdims=True))
    return jnp.concatenate(rows, axis=0)


def small_stack(matrix):
    high, low = split2(matrix)
    return jnp.concatenate([high, high, low], axis=1)


def compute_force(j, values_ref, deriv_ref, radial_ref, shear_ref, force_ref):
    deriv = deriv_ref[...]
    stack = small_stack(deriv[0:32, 0:32])
    stack_t = small_stack(deriv.T[0:32, 0:32])
    radial = jnp.concatenate([radial_ref[...], jnp.zeros((7, 128), F32)], axis=0)
    radial = jnp.concatenate([radial] * 16, axis=1)
    shear = shear_ref[...]
    first = lax.rem(j, 4) * 64

    def times(left, x):
        high, low = split2(x)
        return dot(left, jnp.concatenate([high, low, high], axis=0))

    def body(k, carry):
        x = jnp.concatenate(
            [values_ref[pl.ds(k * 16 + c, 32, stride=64), :] for c in range(16)], axis=1
        )
        back = times(stack_t, times(stack, x) * radial)
        for c in range(16):
            wave = (first + k * 16 + c).astype(F32) * (2.0 / MODES)
            lanes = slice(c * 128, (c + 1) * 128)
            force_ref[pl.ds(k * 16 + c, NODES, stride=64), :] = (
                -back[0:NODES, lanes] - shear * (wave * wave) * x[0:NODES, lanes]
            )
        return carry

    lax.fori_loop(0, 4, body, 0)


def edge_forces(force_ref, node_ref, elem_ref, edge_ref):
    def body(g, carry):
        acc = gather_rows(
            force_ref, node_ref[pl.ds(GROUPS + g, 1), :], elem_ref[pl.ds(GROUPS + g, 1), :]
        )
        for c in range(8):
            edge_ref[g, c * 8 : (c + 1) * 8, :] = acc[c]
        return carry

    lax.fori_loop(0, 4, body, 0)


def row_reactions(drives, block, carry, local_ref, shift_ref, harmonic_ref, high_ref, low_ref):
    for k in range(4):
        chunk = block * 4 + k
        pieces, hots = [], []
        for odd in range(2):
            r = 2 * k + odd
            pieces.append(split2(harmonic_ref[block * 8 + r] * drives[r : r + 1, :]))
            hots.append(hot(iota((256, 128), 0) == local_ref[pl.ds(block * 8 + r, 1), :]))
        left = jnp.concatenate(
            [
                jnp.concatenate([pieces[0][p], pieces[1][p]], axis=1) for p in range(2)
            ],
            axis=0,
        )
        out = dot_nt(left, jnp.concatenate(hots, axis=1))
        out = out[0:COLS] + out[COLS : 2 * COLS]
        here = carry[0] + out[:, 0:128]
        there = carry[1] + out[:, 128:256]
        high, low = split2(here)
        high_ref[chunk] = high
        low_ref[chunk] = low
        moved = jnp.broadcast_to(shift_ref[pl.ds(chunk, 1), :], (COLS, 128)) > 0
        carry = (jnp.where(moved, there, here), jnp.where(moved, 0.0, there))
    return carry


def scatter_rows(sources, first, node_ref, hot_ref, high_ref, low_ref, left_ref, sum_ref):
    rights = []
    for h in range(4):
        pair = node_ref[pl.ds(first + h, 1), :] >> 1
        high = high_ref[sources[h]]
        low = low_ref[sources[h]]
        for a in range(PAIRS):
            mask = jnp.broadcast_to(hot(pair == a), (COLS, 128))
            rows = slice(a * 64, (a + 1) * 64)
            left_ref[rows, h * 128 : (h + 1) * 128] = high * mask
            left_ref[rows, 512 + h * 128 : 640 + h * 128] = low * mask
        rights.append(hot_ref[first + h])
    sum_ref[...] += dot_nt(left_ref[...], jnp.concatenate(rights + rights, axis=1))


def advance(j, now_ref, before_ref, force_ref, sum_ref, mass_ref, modes_ref, next_ref,
            pieces_ref=None):
    order = lax.rem(j, 4) * 64 + iota((COLS, 128), 0)
    live = jnp.where(order < modes_ref[...], STEP_SCALE, 0.0)
    for a in range(NODES):
        rows = slice(a * 64, (a + 1) * 64)
        pair = a // 2
        lanes = slice((a % 2) * 128, (a % 2) * 128 + 128)
        total = force_ref[rows, :] + sum_ref[pair * 64 : (pair + 1) * 64, lanes]
        after = 2.0 * now_ref[rows, :] - before_ref[rows, :] + live * total / mass_ref[a : a + 1, :]
        next_ref[rows, :] = after
        if pieces_ref is not None:
            keep_pieces(after, a, pieces_ref)


INPUTS = 18
VALUES = 11
PADDED = 32 * COLS


def whole_kernel(*refs):
    hbm = refs[:INPUTS]
    out_ref, box_out_ref = refs[INPUTS : INPUTS + 2]
    vmem = refs[INPUTS + 2 : 2 * INPUTS + 2]
    (
        fields, dest_ref, send_ref, node_ref, elem_ref, received, share, shared, harmonic_ref,
        table_ref, force_ref, next_ref, last_ref, high_ref, low_ref, left_ref, sum_ref,
        edge_ref, edges, partial, sums, drive, drives, ways, returned, box_last,
        pieces_ref, hot_ref, square_ref, start_ref, count_ref, meta_ref, shift_ref, local_ref,
        meta_smem, meta_sem,
        load_sem, send_sem, recv_sem, share_send, share_recv, edge_send, edge_recv,
        sum_send, sum_recv, drive_send, drive_recv, way_send, way_recv, out_sem,
    ) = refs[2 * INPUTS + 2 :]
    (
        angle_ref, slot_ref, spring_ref, mass_ref, weight_ref, now_ref, before_ref,
        rows_ref, target_ref, lower_ref, upper_ref, value_ref, old_ref, deriv_ref,
        radial_ref, shear_ref, node_mass_ref, modes_ref,
    ) = vmem
    i = lax.axis_index("mer")
    j = lax.axis_index("box")
    above = lax.rem(i + 1, MER)
    below = lax.rem(i + MER - 1, MER)

    def landing(k):
        if k == VALUES:
            return value_ref.at[0 : NODES * COLS]
        return vmem[k]

    loads = [pltpu.make_async_copy(hbm[k], landing(k), load_sem.at[k]) for k in range(INPUTS)]
    for load in loads:
        load.start()
    barrier = pltpu.get_barrier_semaphore()
    for o in range(1, MER):
        pl.semaphore_signal(
            barrier, inc=1, device_id=(lax.rem(i + o, MER), j), device_id_type=MESH)
    for o in range(1, BOX):
        pl.semaphore_signal(
            barrier, inc=1, device_id=(i, lax.rem(j + o, BOX)), device_id_type=MESH)

    def way(source, target, send, recv, device):
        return pltpu.make_async_remote_copy(
            src_ref=source, dst_ref=target, send_sem=send, recv_sem=recv,
            device_id=device, device_id_type=MESH)

    def to_part(o):
        q = lax.rem(i + o, MER)
        return way(send_ref.at[lax.div(q, 2)], received.at[i], send_sem.at[o], recv_sem.at[o], (q, j))

    def to_share(o):
        q = lax.rem(j + o, BOX)
        return way(share, shared.at[j], share_send.at[o], share_recv.at[o], (i, q))

    def to_sum(step, o):
        q = lax.rem(j + BOX - o, BOX)
        return way(partial.at[step, q], sums.at[step, o],
                   sum_send.at[step, o], sum_recv.at[step, o], (i, q))

    def to_drive(step, o):
        q = lax.rem(j + o, BOX)
        return way(drive.at[step], drives.at[step, j],
                   drive_send.at[step, o], drive_recv.at[step, o], (i, q))

    def to_back(o):
        q = lax.rem(i + o, MER)
        return way(ways.at[lax.div(q, 2)], returned.at[i], way_send.at[o], way_recv.at[o], (q, j))

    def to_edges(step):
        return (
            way(edge_ref.at[step, 2:4], edges.at[step, 0:2],
                edge_send.at[step, 0], edge_recv.at[step, 0], (above, j)),
            way(edge_ref.at[step, 0:2], edges.at[step, 2:4],
                edge_send.at[step, 1], edge_recv.at[step, 1], (below, j)),
        )

    def repeat(first, last, work):
        def body(o, carry):
            work(o)
            return carry

        lax.fori_loop(first, last, body, 0)

    for load in loads[:7]:
        load.wait()
    order_nodes([ref[...] for ref in vmem[:7]], dest_ref, send_ref, fields)
    pl.semaphore_wait(barrier, MER + BOX - 2)
    repeat(1, MER, lambda o: to_part(o).start())
    received[i] = send_ref[lax.div(i, 2)]
    for load in loads[7:]:
        load.wait()
    row_table(rows_ref[...], target_ref[...], (lower_ref[...], upper_ref[...]), node_ref, elem_ref,
              start_ref, count_ref, meta_ref, shift_ref)
    meta = pltpu.make_async_copy(meta_ref, meta_smem, meta_sem.at[0])
    meta.start()
    slot_hots(node_ref, elem_ref, hot_ref)
    square_ref[...] = jnp.zeros_like(square_ref)
    square_ref[0:NODES, 0:NODES] = deriv_ref[...]
    for ref in (value_ref, next_ref):
        ref[NODES * COLS : PADDED, :] = jnp.zeros((PADDED - NODES * COLS, ELEMS), F32)
    for a in range(NODES):
        keep_pieces(value_ref[a * COLS : (a + 1) * COLS, :], a, pieces_ref)
    for lane in (128, 384):
        pieces_ref[(PAIRS - 1) * COLS : PAIRS * COLS, lane : lane + 128] = jnp.zeros(
            (COLS, 128), BF16)
    table_ref[GROUPS : GROUPS + 2] = jnp.zeros((2, COLS, 128), F32)
    meta.wait()

    repeat(1, MER, lambda o: to_part(o).wait_recv())
    half = lax.rem(i, 2)
    own = []
    for f in range(7):
        even = jnp.concatenate([received[2 * r, f : f + 1, :] for r in range(8)], axis=0)
        odd = jnp.concatenate([received[2 * r + 1, f : f + 1, :] for r in range(8)], axis=0)
        own.append(halves(even, odd, half))
    share[0] = own[0]
    share[1] = own[1]
    repeat(1, BOX, lambda o: to_share(o).start())
    shared[j] = share[...]
    spring, mass, weight, box_now, box_before = own[2:]

    def forces(step, ref):
        compute_force(j, ref, square_ref, radial_ref, shear_ref, force_ref)
        edge_forces(force_ref, node_ref, elem_ref, edge_ref.at[step])
        for copy in to_edges(step):
            copy.start()

    def sample_block(step, block):
        partial[step, block] = sample_nodes(table_ref, local_ref, meta_smem, block, harmonic_ref)

    def pulls(step, now):
        sample = partial[step, j]
        for o in range(1, BOX):
            to_sum(step, o).wait_recv()
            sample = sample + sums[step, o]
        pull = spring * (sample - now)
        drive[step] = -weight * pull
        repeat(1, BOX, lambda o: to_drive(step, o).start())
        drives[step, j] = drive[step]
        return pull

    def reactions(step):
        sum_ref[...] = jnp.zeros_like(sum_ref)

        def work(block, carry):
            @pl.when(block != j)
            def _():
                to_drive(step, lax.rem(j + BOX - block, BOX)).wait_recv()

            return row_reactions(drives[step, block], block, carry, local_ref, shift_ref,
                                 harmonic_ref, high_ref, low_ref)

        nothing = jnp.zeros((COLS, 128), F32)
        lax.fori_loop(0, BOX, work, (nothing, nothing))

        def scatter(t, carry):
            sources = [
                lax.clamp(0, meta_smem[CHUNKS, t * 4 + h], CHUNKS - 1) for h in range(4)
            ]
            scatter_rows(sources, t * 4, node_ref, hot_ref, high_ref, low_ref, left_ref, sum_ref)
            return carry

        lax.fori_loop(0, GROUPS // 4, scatter, 0)
        for copy in to_edges(step):
            copy.wait_recv()
        for g in range(4):
            ghost = (i == 0) if g < 2 else (i == MER - 1)
            high, low = split2(jnp.where(ghost, 0.0, edges[step, g]))
            high_ref[CHUNKS + g] = high
            low_ref[CHUNKS + g] = low
        scatter_rows([CHUNKS + h for h in range(4)], GROUPS, node_ref, hot_ref, high_ref,
                     low_ref, left_ref, sum_ref)

    fill_table(value_ref, pieces_ref, hot_ref, node_ref, elem_ref, table_ref)

    def enter(block):
        rows = pl.ds(pl.multiple_of(block * 8, 8), 8)
        places = shared[block, 1].astype(I32)
        filled = jnp.where(places < count_ref[rows, :], 1, 0)
        local_ref[rows, :] = jnp.where(filled > 0, start_ref[rows, :] + places, 0)
        harmonics(j, shared[block, 0], filled, block, harmonic_ref)
        sample_block(0, block)

    enter(j)

    def enter_peer(o):
        to_share(o).wait_recv()
        enter(lax.rem(j + BOX - o, BOX))
        to_sum(0, o).start()

    repeat(1, BOX, enter_peer)
    pull = pulls(0, box_now)
    forces(0, value_ref)
    box_next = 2.0 * box_now - box_before + STEP_SCALE * pull / mass
    reactions(0)
    advance(j, value_ref, old_ref, force_ref, sum_ref, node_mass_ref, modes_ref, next_ref,
            pieces_ref)

    fill_table(next_ref, pieces_ref, hot_ref, node_ref, elem_ref, table_ref)

    def sample_peer(o):
        sample_block(1, lax.rem(j + BOX - o, BOX))
        to_sum(1, o).start()

    repeat(1, BOX, sample_peer)
    sample_block(1, j)
    pull = pulls(1, box_next)
    box_after = 2.0 * box_next - box_now + STEP_SCALE * pull / mass
    for m in range(8):
        ways[m] = jnp.broadcast_to(box_after[m : m + 1, :], (8, 128))
    repeat(1, MER, lambda o: to_back(o).start())
    returned[i] = ways[lax.div(i, 2)]
    forces(1, next_ref)
    reactions(1)
    advance(j, next_ref, value_ref, force_ref, sum_ref, node_mass_ref, modes_ref, last_ref)
    result = pltpu.make_async_copy(last_ref, out_ref, out_sem.at[0])
    result.start()

    repeat(1, MER, lambda o: to_back(o).wait_recv())
    even = jnp.concatenate([returned[2 * r, 0:1, :] for r in range(8)], axis=0)
    odd = jnp.concatenate([returned[2 * r + 1, 0:1, :] for r in range(8)], axis=0)
    box = halves(even, odd, half)
    line = jnp.concatenate([box[m : m + 1, :] for m in range(8)], axis=1)
    pieces = jnp.concatenate([piece.astype(F32) for piece in split3(line)], axis=0).astype(BF16)
    for r in range(8):
        out = dot(pieces, hot(iota((1024, 128), 0) == dest_ref[r : r + 1, :]))
        box_last[r : r + 1, :] = out[0:1] + (out[1:2] + out[2:3])
    box_result = pltpu.make_async_copy(box_last, box_out_ref, out_sem.at[1])
    box_result.start()

    def sent(o):
        to_share(o).wait_send()
        for step in range(2):
            to_sum(step, o).wait_send()
            to_drive(step, o).wait_send()

    repeat(1, BOX, sent)

    def sent_far(o):
        to_part(o).wait_send()
        to_back(o).wait_send()

    repeat(1, MER, sent_far)
    for step in range(2):
        for copy in to_edges(step):
            copy.wait_send()
    result.wait()
    box_result.wait()


def hand_over_kernel(final_ref, box_ref, out_ref, box_out_ref, final, box, sem):
    half = NODES * COLS // 2
    parts = [
        (final_ref.at[k * half : (k + 1) * half], final.at[k * half : (k + 1) * half],
         out_ref.at[k * half : (k + 1) * half])
        for k in range(2)
    ] + [(box_ref, box, box_out_ref)]
    copies = [
        (pltpu.make_async_copy(source, middle, sem.at[0, k]),
         pltpu.make_async_copy(middle, target, sem.at[1, k]))
        for k, (source, middle, target) in enumerate(parts)
    ]
    for first, second in copies:
        first.start()
    for first, second in copies:
        first.wait()
        second.start()
    for first, second in copies:
        second.wait()


def per_device(
    annulus, annulus_prev, derivative, radial_modulus, shear_modulus, node_mass, element_modes,
    upper_rows, lower_rows, coupling_rows, coupling_target, box_field, box_prev, box_angle,
    box_spring, box_mass, box_weight, box_slot,
):
    flat = NODES * COLS
    args = [
        x.reshape(8, 128)
        for x in (box_angle, box_slot, box_spring, box_mass, box_weight, box_field, box_prev)
    ] + [
        coupling_rows.reshape(16, 128), coupling_target.reshape(16, 128),
        lower_rows.reshape(2, 128), upper_rows.reshape(2, 128),
        annulus.reshape(flat, ELEMS), annulus_prev.reshape(flat, ELEMS), derivative,
        radial_modulus, shear_modulus, node_mass, element_modes.reshape(1, ELEMS),
    ]
    vmem = pltpu.VMEM
    scratch = [vmem(x.shape, x.dtype) for x in args]
    scratch[VALUES] = vmem((PADDED, ELEMS), F32)
    scratch += [
        vmem((8, 8, 128), F32),
        vmem((8, 128), I32),
        vmem((8, 8, 128), F32),
        vmem((ALL_GROUPS, 128), I32),
        vmem((ALL_GROUPS, 128), I32),
        vmem((MER, 8, 128), F32),
        vmem((2, 8, 128), F32),
        vmem((BOX, 2, 8, 128), F32),
        vmem((ROWS, COLS, 128), F32),
        vmem((GROUPS + 2, COLS, 128), F32),
        vmem((flat, ELEMS), F32),
        vmem((PADDED, ELEMS), F32),
        vmem((flat, ELEMS), F32),
        vmem((CHUNKS + 4, COLS, 128), BF16),
        vmem((CHUNKS + 4, COLS, 128), BF16),
        vmem((PAIRS * COLS, 1024), BF16),
        vmem((PAIRS * COLS, 256), F32),
        vmem((2, 4, COLS, 128), F32),
        vmem((2, 4, COLS, 128), F32),
        vmem((2, BOX, 8, 128), F32),
        vmem((2, BOX, 8, 128), F32),
        vmem((2, 8, 128), F32),
        vmem((2, BOX, 8, 128), F32),
        vmem((8, 8, 128), F32),
        vmem((MER, 8, 128), F32),
        vmem((8, 128), F32),
        vmem((PAIRS * COLS, 512), BF16),
        vmem((ALL_GROUPS, 256, 128), BF16),
        vmem((128, 128), F32),
        vmem((ROWS, 128), I32),
        vmem((ROWS, 128), I32),
        vmem((CHUNKS + 8, 128), I32),
        vmem((CHUNKS, 128), I32),
        vmem((ROWS, 128), I32),
        pltpu.SMEM((CHUNKS + 8, 128), I32),
        pltpu.SemaphoreType.DMA((1,)),
    ]
    dma = pltpu.SemaphoreType.DMA
    scratch += [dma((INPUTS,))] + [dma((MER,))] * 2 + [dma((BOX,))] * 2 + [dma((2, 2))] * 2
    scratch += [dma((2, BOX))] * 4 + [dma((MER,))] * 2 + [dma((2,))]
    any_space = pl.BlockSpec(memory_space=pl.ANY)
    final, box_out = pl.pallas_call(
        whole_kernel,
        out_shape=[jax.ShapeDtypeStruct((flat, ELEMS), F32), jax.ShapeDtypeStruct((8, 128), F32)],
        in_specs=[any_space] * INPUTS,
        out_specs=[any_space] * 2,
        scratch_shapes=scratch,
        compiler_params=pltpu.CompilerParams(
            vmem_limit_bytes=56 << 20, collective_id=0, has_side_effects=True),
        name="coupled_steps",
    )(*args)
    final, box_out = pl.pallas_call(
        hand_over_kernel,
        out_shape=[jax.ShapeDtypeStruct((flat, ELEMS), F32), jax.ShapeDtypeStruct((8, 128), F32)],
        in_specs=[any_space] * 2,
        out_specs=[any_space] * 2,
        scratch_shapes=[vmem((flat, ELEMS), F32), vmem((8, 128), F32), dma((2, 3))],
        compiler_params=pltpu.CompilerParams(vmem_limit_bytes=60 << 20),
        name="hand_over",
    )(final, box_out)
    return final.reshape(NODES, COLS, ELEMS), box_out.reshape(1024)


def solution(mesh):
    mer_box = P(("mer", "box"))
    in_specs = (
        P(None, "box", "mer"), P(None, "box", "mer"), P(),
        P(None, "mer"), P(None, "mer"), P(None, "mer"),
        P("mer"), P("mer"), P("mer"), P("mer"), P("mer", None),
        mer_box, mer_box, mer_box, mer_box, mer_box, mer_box, mer_box,
    )
    return jax.shard_map(
        per_device, mesh=mesh, in_specs=in_specs,
        out_specs=(P(None, "box", "mer"), mer_box), check_vma=False,
    )
```

```python
import jax
import jax.numpy as jnp
from jax import lax
from jax.experimental import pallas as pl
from jax.experimental.pallas import tpu as pltpu
from jax.sharding import PartitionSpec as P

F32 = jnp.float32
BF16 = jnp.bfloat16
I32 = jnp.int32
MESH = pl.DeviceIdType.MESH

MER, BOX = 16, 8
MODES = 256
NODES, COLS, ELEMS = 25, 64, 128
PAIRS = 13
GROUPS = 16
ALL_GROUPS = 20
CHUNKS = 32
ROWS = 64
STEP_SCALE = 0.25


def iota(shape, dim):
    return lax.broadcasted_iota(I32, shape, dim)


def hot(mask):
    return jnp.where(mask, 1.0, 0.0).astype(BF16)


def dot(a, b):
    return jnp.dot(a, b, preferred_element_type=F32)


def dot_nt(a, b):
    return lax.dot_general(a, b, (((1,), (1,)), ((), ())), preferred_element_type=F32)


def split2(x):
    hi = x.astype(BF16)
    return hi, (x - hi.astype(F32)).astype(BF16)


def split3(x):
    hi = x.astype(BF16)
    rest = x - hi.astype(F32)
    mid = rest.astype(BF16)
    return hi, mid, (rest - mid.astype(F32)).astype(BF16)


def take_lanes(x, index):
    return jnp.take_along_axis(x, index, axis=1, mode="promise_in_bounds")


def sincos(x):
    k = jnp.floor(x * 0.6366197723675814 + 0.5)
    r = x - k * 1.5703125
    r = r - k * 4.837512969970703125e-4
    r = r - k * 7.54978995489188216e-8
    z = r * r
    s = ((-1.9515295891e-4 * z + 8.3321608736e-3) * z - 1.6666654611e-1) * z * r + r
    c = ((2.443315711809948e-5 * z - 1.388731625493765e-3) * z + 4.166664568298827e-2) * z * z
    c = c - 0.5 * z + 1.0
    q = k.astype(I32)
    odd = (q & 1) == 1
    sine = jnp.where(odd, c, s)
    cosine = jnp.where(odd, s, c)
    sine = jnp.where((q & 2) == 2, -sine, sine)
    cosine = jnp.where(((q + 1) & 2) == 2, -cosine, cosine)
    return sine, cosine


def before_lane():
    return hot(iota((128, 128), 0) < iota((128, 128), 1))


def order_nodes(sources, dest_ref, send_ref, fields):
    tri = before_lane()
    part = sources[1] & (MER - 1)
    values = [sources[0], (sources[1] >> 4).astype(F32)] + list(sources[2:])
    for r in range(8):
        for f in range(7):
            fields[r, f : f + 1, :] = values[f][r : r + 1, :]
        fields[r, 7:8, :] = jnp.zeros((1, 128), F32)
    base = jnp.zeros((MER, 1), F32)
    total = jnp.zeros((24, 1024), F32)
    for r in range(8):
        mine = part[r : r + 1, :]
        member = jnp.where(iota((MER, 128), 0) == mine, 1.0, 0.0)
        rank = dot(member.astype(BF16), tri) + base
        place = jnp.sum(member * rank, axis=0, keepdims=True).astype(I32)
        base = base + jnp.sum(member, axis=1, keepdims=True)
        dest = mine * 64 + place
        dest_ref[r : r + 1, :] = dest
        order = hot(iota((1024, 128), 0) == dest)
        pieces = jnp.concatenate(split3(fields[r]), axis=0)
        total = total + dot_nt(pieces, order)
    sorted_fields = total[0:8] + (total[8:16] + total[16:24])
    for m in range(8):
        send_ref[m] = sorted_fields[:, m * 128 : (m + 1) * 128]


def pick_rows(shape, source):
    return hot(iota(shape, 1) == source(iota(shape, 0)))


def order_hots(dest_ref, order_ref):
    def body(r, carry):
        order_ref[r] = hot(iota((1024, 128), 0) == dest_ref[pl.ds(r, 1), :])
        return carry

    lax.fori_loop(0, 8, body, 0)


def row_table(rows, target, edges, node_ref, elem_ref, start_ref, count_ref, meta_ref, shift_ref):
    tri = before_lane()
    reader = (target & (BOX - 1)) * MER + (target >> 3)
    node = (rows >> 7).astype(F32)
    elem = (rows & 127).astype(F32)
    readers = iota((128, 128), 0)
    seen = jnp.zeros((128, 128), F32)
    for r in range(16):
        seen = seen + jnp.where(readers == reader[r : r + 1, :], 1.0, 0.0)
    count = jnp.sum(seen, axis=1, keepdims=True)
    wide = jnp.broadcast_to(count, (128, 128)).astype(BF16)
    below = hot(iota((128, 128), 1) < iota((128, 128), 0))
    start = dot(below, wide)
    base = start
    table = jnp.zeros((2 * GROUPS, 128), F32)
    for r in range(16):
        mine = reader[r : r + 1, :]
        member = jnp.where(readers == mine, 1.0, 0.0)
        rank = dot(member.astype(BF16), tri) + base
        place = jnp.sum(member * rank, axis=0, keepdims=True).astype(I32)
        base = base + jnp.sum(member, axis=1, keepdims=True)
        group = iota((GROUPS, 128), 0) == (place >> 7)
        values = jnp.concatenate(
            [
                jnp.where(group, jnp.broadcast_to(node[r : r + 1, :], (GROUPS, 128)), 0.0),
                jnp.where(group, jnp.broadcast_to(elem[r : r + 1, :], (GROUPS, 128)), 0.0),
            ],
            axis=0,
        ).astype(BF16)
        table = table + dot_nt(values, hot(readers == (place & 127)))
    node_ref[0:GROUPS, :] = table[0:GROUPS].astype(I32)
    elem_ref[0:GROUPS, :] = table[GROUPS : 2 * GROUPS].astype(I32)
    for k, edge in enumerate(edges):
        node_ref[GROUPS + 2 * k : GROUPS + 2 * k + 2, :] = edge >> 7
        elem_ref[GROUPS + 2 * k : GROUPS + 2 * k + 2, :] = edge & 127

    high = jnp.floor(start * (1.0 / 16.0))
    parts = [high.astype(BF16), (start - 16.0 * high).astype(BF16)]
    same_half = (iota((128, 128), 0) & 1) == (iota((128, 128), 1) >> 6)

    def halved(x):
        return jnp.where(same_half, x.astype(F32), 0.0).astype(BF16)

    def joined(left, right):
        return (16.0 * dot(left, right[0]) + dot(left, right[1])).astype(I32)

    own = hot((iota((ROWS, 128), 1) >> 1) == iota((ROWS, 128), 0))
    first = joined(pick_rows((ROWS, 128), lambda row: (row >> 1) * 4), parts) >> 7
    start_ref[...] = joined(own, [halved(part) for part in parts]) - 128 * first
    count_ref[...] = dot(own, halved(wide)).astype(I32)
    group = joined(pick_rows((CHUNKS, 128), lambda chunk: chunk * 4), parts) >> 7
    after = joined(pick_rows((CHUNKS, 128), lambda chunk: (chunk + 1) * 4), parts) >> 7
    shift_ref[...] = after - group
    meta_ref[0:CHUNKS, :] = group
    last = jnp.sum(jnp.where(group <= iota((CHUNKS, 128), 1), 1, 0), axis=0, keepdims=True) - 1
    meta_ref[CHUNKS : CHUNKS + 8, :] = jnp.broadcast_to(last, (8, 128))


def halves(even, odd, half):
    low = jnp.where(half == 0, even, pltpu.roll(even, 64, 1))
    high = jnp.where(half == 1, odd, pltpu.roll(odd, 64, 1))
    return jnp.where(iota((8, 128), 1) < 64, low, high)


def harmonics(j, angles, filled, block, harmonic_ref):
    sub = iota((8, 128), 0).astype(F32)
    first = (lax.rem(j, 4) * 64).astype(F32)
    is_sine = j >= 4
    for r in range(8):
        angle = jnp.broadcast_to(angles[r : r + 1, :], (8, 128))
        base_sin, base_cos = sincos(angle * (sub + first))
        step_sin, step_cos = sincos(angle * (sub * 8.0))
        keep = jnp.broadcast_to(filled[r : r + 1, :], (8, 128)) > 0
        a = jnp.where(keep, jnp.where(is_sine, base_sin, base_cos), 0.0)
        b = jnp.where(keep, jnp.where(is_sine, -base_cos, base_sin), 0.0)
        for t in range(8):
            harmonic_ref[block * 8 + r, t * 8 : (t + 1) * 8, :] = (
                a * step_cos[t : t + 1, :] - b * step_sin[t : t + 1, :]
            )


def gather_rows(values_ref, node, elem):
    index = jnp.broadcast_to(elem, (8, 128))
    node = jnp.broadcast_to(node, (8, 128))
    acc = [jnp.zeros((8, 128), F32) for _ in range(8)]
    for a in range(NODES):
        mask = node == a
        for c in range(8):
            taken = take_lanes(values_ref[a * 64 + c * 8 : a * 64 + c * 8 + 8, :], index)
            acc[c] = jnp.where(mask, taken, acc[c])
    return acc


MATRIX_GROUPS, LANE_GROUPS = 6, 2


def keep_pieces(values, a, pieces_ref):
    rows = slice((a // 2) * 64, (a // 2) * 64 + 64)
    lane = (a % 2) * 128
    high, low = split2(values)
    pieces_ref[rows, lane : lane + 128] = high
    pieces_ref[rows, 256 + lane : 384 + lane] = low


def slot_hots(node_ref, elem_ref, hot_ref):
    def body(g, carry):
        lane = (node_ref[pl.ds(g, 1), :] & 1) * 128 + elem_ref[pl.ds(g, 1), :]
        hot_ref[:, pl.ds(pl.multiple_of(g * 128, 128), 128)] = hot(iota((256, 128), 0) == lane)
        return carry

    lax.fori_loop(0, ALL_GROUPS, body, 0)


def fill_table(values_ref, pieces_ref, hot_ref, node_ref, elem_ref, table_ref):
    for t in range(GROUPS // (MATRIX_GROUPS + LANE_GROUPS)):
        first = t * (MATRIX_GROUPS + LANE_GROUPS)
        right = hot_ref[:, first * 128 : (first + MATRIX_GROUPS) * 128]
        out = dot(pieces_ref[...], jnp.concatenate([right, right], axis=0))
        for k in range(LANE_GROUPS):
            g = first + MATRIX_GROUPS + k
            acc = gather_rows(values_ref, node_ref[g : g + 1, :], elem_ref[g : g + 1, :])
            for c in range(8):
                table_ref[g, c * 8 : (c + 1) * 8, :] = acc[c]
        for k in range(MATRIX_GROUPS):
            g = first + k
            pair = node_ref[g : g + 1, :] >> 1
            acc = jnp.zeros((COLS, 128), F32)
            for a in range(PAIRS):
                acc = jnp.where(
                    pair == a, out[a * 64 : (a + 1) * 64, k * 128 : (k + 1) * 128], acc)
            table_ref[g] = acc


def sample_nodes(table_ref, local_ref, meta_ref, block, harmonic_ref):
    rows = []
    for r in range(8):
        row = block * 8 + r
        group = lax.clamp(0, meta_ref[block * 4 + r // 2, 0], GROUPS)
        local = jnp.broadcast_to(local_ref[pl.ds(row, 1), :], (8, 128))
        index = local & 127
        second = local > 127
        acc = jnp.zeros((8, 128), F32)
        for c in range(8):
            columns = slice(c * 8, (c + 1) * 8)
            taken = jnp.where(
                second,
                take_lanes(table_ref[group + 1, columns, :], index),
                take_lanes(table_ref[group, columns, :], index),
            )
            acc = acc + taken * harmonic_ref[row, columns, :]
        rows.append(jnp.sum(acc, axis=0, keepdims=True))
    return jnp.concatenate(rows, axis=0)


def small_stack(matrix):
    high, low = split2(matrix)
    return jnp.concatenate([high, high, low], axis=1)


def compute_force(j, values_ref, deriv_ref, radial_ref, shear_ref, force_ref):
    deriv = deriv_ref[...]
    stack = small_stack(deriv[0:32, 0:32])
    stack_t = small_stack(deriv.T[0:32, 0:32])
    radial = jnp.concatenate([radial_ref[...], jnp.zeros((7, 128), F32)], axis=0)
    radial = jnp.concatenate([radial] * 16, axis=1)
    shear = shear_ref[...]
    first = lax.rem(j, 4) * 64

    def times(left, x):
        high, low = split2(x)
        return dot(left, jnp.concatenate([high, low, high], axis=0))

    def body(k, carry):
        x = jnp.concatenate(
            [values_ref[pl.ds(k * 16 + c, 32, stride=64), :] for c in range(16)], axis=1
        )
        back = times(stack_t, times(stack, x) * radial)
        for c in range(16):
            wave = (first + k * 16 + c).astype(F32) * (2.0 / MODES)
            lanes = slice(c * 128, (c + 1) * 128)
            force_ref[pl.ds(k * 16 + c, NODES, stride=64), :] = (
                -back[0:NODES, lanes] - shear * (wave * wave) * x[0:NODES, lanes]
            )
        return carry

    lax.fori_loop(0, 4, body, 0)


def edge_forces(force_ref, node_ref, elem_ref, edge_ref):
    def body(g, carry):
        acc = gather_rows(
            force_ref, node_ref[pl.ds(GROUPS + g, 1), :], elem_ref[pl.ds(GROUPS + g, 1), :]
        )
        for c in range(8):
            edge_ref[g, c * 8 : (c + 1) * 8, :] = acc[c]
        return carry

    lax.fori_loop(0, 4, body, 0)


def chunk_hots(local_ref, near_ref):
    def body(chunk, carry):
        for odd in range(2):
            near_ref[chunk, :, odd * 128 : (odd + 1) * 128] = hot(
                iota((256, 128), 0) == local_ref[pl.ds(chunk * 2 + odd, 1), :])
        return carry

    lax.fori_loop(0, CHUNKS, body, 0)


def row_reactions(drives, block, carry, near_ref, shift_ref, harmonic_ref, high_ref, low_ref):
    for k in range(4):
        chunk = block * 4 + k
        pieces = [
            split2(harmonic_ref[chunk * 2 + odd] * drives[2 * k + odd : 2 * k + odd + 1, :])
            for odd in range(2)
        ]
        left = jnp.concatenate(
            [
                jnp.concatenate([pieces[0][p], pieces[1][p]], axis=1) for p in range(2)
            ],
            axis=0,
        )
        out = dot_nt(left, near_ref[chunk])
        out = out[0:COLS] + out[COLS : 2 * COLS]
        here = carry[0] + out[:, 0:128]
        there = carry[1] + out[:, 128:256]
        high, low = split2(here)
        high_ref[chunk] = high
        low_ref[chunk] = low
        moved = jnp.broadcast_to(shift_ref[pl.ds(chunk, 1), :], (COLS, 128)) > 0
        carry = (jnp.where(moved, there, here), jnp.where(moved, 0.0, there))
    return carry


def place_rows(high, low, node, lanes, left_ref):
    pair = node >> 1
    for a in range(PAIRS):
        mask = jnp.broadcast_to(hot(pair == a), (COLS, 128))
        left_ref[a * 64 : (a + 1) * 64, lanes] = high * mask
        left_ref[(PAIRS + a) * 64 : (PAIRS + a + 1) * 64, lanes] = low * mask


def scatter_rows(hot_ref, left_ref, sum_ref):
    out = dot_nt(left_ref[...], hot_ref[...])
    sum_ref[...] = out[0 : PAIRS * COLS] + out[PAIRS * COLS : 2 * PAIRS * COLS]


def advance(j, now_ref, before_ref, force_ref, sum_ref, mass_ref, modes_ref, next_ref,
            pieces_ref=None):
    order = lax.rem(j, 4) * 64 + iota((COLS, 128), 0)
    live = jnp.where(order < modes_ref[...], STEP_SCALE, 0.0)
    for a in range(NODES):
        rows = slice(a * 64, (a + 1) * 64)
        pair = a // 2
        lanes = slice((a % 2) * 128, (a % 2) * 128 + 128)
        total = force_ref[rows, :] + sum_ref[pair * 64 : (pair + 1) * 64, lanes]
        after = 2.0 * now_ref[rows, :] - before_ref[rows, :] + live * total / mass_ref[a : a + 1, :]
        next_ref[rows, :] = after
        if pieces_ref is not None:
            keep_pieces(after, a, pieces_ref)


INPUTS = 18
VALUES = 11
PADDED = 32 * COLS


def whole_kernel(*refs):
    hbm = refs[:INPUTS]
    out_ref, box_out_ref = refs[INPUTS : INPUTS + 2]
    vmem = refs[INPUTS + 2 : 2 * INPUTS + 2]
    (
        fields, dest_ref, send_ref, node_ref, elem_ref, received, share, shared, harmonic_ref,
        table_ref, force_ref, next_ref, high_ref, low_ref, left_ref, sum_ref,
        edge_ref, edges, partial, sums, drive, drives, ways, returned,
        pieces_ref, hot_ref, square_ref, start_ref, count_ref, meta_ref, shift_ref, local_ref,
        meta_smem, meta_sem, near_ref, order_ref,
        load_sem, send_sem, recv_sem, share_send, share_recv, edge_send, edge_recv,
        sum_send, sum_recv, drive_send, drive_recv, way_send, way_recv,
    ) = refs[2 * INPUTS + 2 :]
    (
        angle_ref, slot_ref, spring_ref, mass_ref, weight_ref, now_ref, before_ref,
        rows_ref, target_ref, lower_ref, upper_ref, value_ref, old_ref, deriv_ref,
        radial_ref, shear_ref, node_mass_ref, modes_ref,
    ) = vmem
    i = lax.axis_index("mer")
    j = lax.axis_index("box")
    above = lax.rem(i + 1, MER)
    below = lax.rem(i + MER - 1, MER)

    def landing(k):
        if k == VALUES:
            return value_ref.at[0 : NODES * COLS]
        return vmem[k]

    loads = [pltpu.make_async_copy(hbm[k], landing(k), load_sem.at[k]) for k in range(INPUTS)]
    for load in loads[:7]:
        load.start()
    barrier = pltpu.get_barrier_semaphore()
    for o in range(1, MER):
        pl.semaphore_signal(
            barrier, inc=1, device_id=(lax.rem(i + o, MER), j), device_id_type=MESH)
    for o in range(1, BOX):
        pl.semaphore_signal(
            barrier, inc=1, device_id=(i, lax.rem(j + o, BOX)), device_id_type=MESH)

    for load in loads[7:]:
        load.start()

    def way(source, target, send, recv, device):
        return pltpu.make_async_remote_copy(
            src_ref=source, dst_ref=target, send_sem=send, recv_sem=recv,
            device_id=device, device_id_type=MESH)

    def to_part(o):
        q = lax.rem(i + o, MER)
        return way(send_ref.at[lax.div(q, 2)], received.at[i], send_sem.at[o], recv_sem.at[o], (q, j))

    def to_share(o):
        q = lax.rem(j + o, BOX)
        return way(share, shared.at[j], share_send.at[o], share_recv.at[o], (i, q))

    def to_sum(step, o):
        q = lax.rem(j + BOX - o, BOX)
        return way(partial.at[step, q], sums.at[step, o],
                   sum_send.at[step, o], sum_recv.at[step, o], (i, q))

    def to_drive(step, o):
        q = lax.rem(j + o, BOX)
        return way(drive.at[step], drives.at[step, j],
                   drive_send.at[step, o], drive_recv.at[step, o], (i, q))

    def to_back(o):
        q = lax.rem(i + o, MER)
        return way(ways.at[lax.div(q, 2)], returned.at[i], way_send.at[o], way_recv.at[o], (q, j))

    def to_edges(step):
        return (
            way(edge_ref.at[step, 2:4], edges.at[step, 0:2],
                edge_send.at[step, 0], edge_recv.at[step, 0], (above, j)),
            way(edge_ref.at[step, 0:2], edges.at[step, 2:4],
                edge_send.at[step, 1], edge_recv.at[step, 1], (below, j)),
        )

    def repeat(first, last, work):
        def body(o, carry):
            work(o)
            return carry

        lax.fori_loop(first, last, body, 0)

    for load in loads[:7]:
        load.wait()
    order_nodes([ref[...] for ref in vmem[:7]], dest_ref, send_ref, fields)
    pl.semaphore_wait(barrier, MER + BOX - 2)
    repeat(1, MER, lambda o: to_part(o).start())
    received[i] = send_ref[lax.div(i, 2)]
    for load in loads[7:]:
        load.wait()
    row_table(rows_ref[...], target_ref[...], (lower_ref[...], upper_ref[...]), node_ref, elem_ref,
              start_ref, count_ref, meta_ref, shift_ref)
    meta = pltpu.make_async_copy(meta_ref, meta_smem, meta_sem.at[0])
    meta.start()
    slot_hots(node_ref, elem_ref, hot_ref)
    square_ref[...] = jnp.zeros_like(square_ref)
    square_ref[0:NODES, 0:NODES] = deriv_ref[...]
    for ref in (value_ref, next_ref):
        ref[NODES * COLS : PADDED, :] = jnp.zeros((PADDED - NODES * COLS, ELEMS), F32)
    for a in range(NODES):
        keep_pieces(value_ref[a * COLS : (a + 1) * COLS, :], a, pieces_ref)
    for lane in (128, 384):
        pieces_ref[(PAIRS - 1) * COLS : PAIRS * COLS, lane : lane + 128] = jnp.zeros(
            (COLS, 128), BF16)
    table_ref[GROUPS : GROUPS + 2] = jnp.zeros((2, COLS, 128), F32)
    meta.wait()

    repeat(1, MER, lambda o: to_part(o).wait_recv())
    half = lax.rem(i, 2)
    own = []
    for f in range(7):
        even = jnp.concatenate([received[2 * r, f : f + 1, :] for r in range(8)], axis=0)
        odd = jnp.concatenate([received[2 * r + 1, f : f + 1, :] for r in range(8)], axis=0)
        own.append(halves(even, odd, half))
    share[0] = own[0]
    share[1] = own[1]
    repeat(1, BOX, lambda o: to_share(o).start())
    shared[j] = share[...]
    spring, mass, weight, box_now, box_before = own[2:]

    def forces(step, ref):
        compute_force(j, ref, square_ref, radial_ref, shear_ref, force_ref)
        edge_forces(force_ref, node_ref, elem_ref, edge_ref.at[step])
        for copy in to_edges(step):
            copy.start()

    def sample_block(step, block):
        partial[step, block] = sample_nodes(table_ref, local_ref, meta_smem, block, harmonic_ref)

    def pulls(step, now):
        sample = partial[step, j]
        for o in range(1, BOX):
            to_sum(step, o).wait_recv()
            sample = sample + sums[step, o]
        pull = spring * (sample - now)
        drive[step] = -weight * pull
        repeat(1, BOX, lambda o: to_drive(step, o).start())
        drives[step, j] = drive[step]
        return pull

    def reactions(step, between):
        def work(block, carry):
            @pl.when(block != j)
            def _():
                to_drive(step, lax.rem(j + BOX - block, BOX)).wait_recv()

            return row_reactions(drives[step, block], block, carry, near_ref, shift_ref,
                                 harmonic_ref, high_ref, low_ref)

        nothing = jnp.zeros((COLS, 128), F32)
        lax.fori_loop(0, BOX, work, (nothing, nothing))
        between()

        def place(t, carry):
            for h in range(4):
                g = t * 4 + h
                source = lax.clamp(0, meta_smem[CHUNKS, g], CHUNKS - 1)
                lanes = pl.ds(pl.multiple_of(t * 512, 512) + h * 128, 128)
                place_rows(high_ref[source], low_ref[source], node_ref[pl.ds(g, 1), :], lanes,
                           left_ref)
            return carry

        lax.fori_loop(0, GROUPS // 4, place, 0)
        for copy in to_edges(step):
            copy.wait_recv()
        for g in range(4):
            ghost = (i == 0) if g < 2 else (i == MER - 1)
            high, low = split2(jnp.where(ghost, 0.0, edges[step, g]))
            k = GROUPS + g
            place_rows(high, low, node_ref[k : k + 1, :], slice(k * 128, (k + 1) * 128), left_ref)
        scatter_rows(hot_ref, left_ref, sum_ref)

    fill_table(value_ref, pieces_ref, hot_ref, node_ref, elem_ref, table_ref)

    def enter(block):
        rows = pl.ds(pl.multiple_of(block * 8, 8), 8)
        places = shared[block, 1].astype(I32)
        filled = jnp.where(places < count_ref[rows, :], 1, 0)
        local_ref[rows, :] = jnp.where(filled > 0, start_ref[rows, :] + places, 0)
        harmonics(j, shared[block, 0], filled, block, harmonic_ref)
        sample_block(0, block)

    enter(j)

    def enter_peer(o):
        to_share(o).wait_recv()
        enter(lax.rem(j + BOX - o, BOX))
        to_sum(0, o).start()

    repeat(1, BOX, enter_peer)
    chunk_hots(local_ref, near_ref)
    pull = pulls(0, box_now)
    forces(0, value_ref)
    box_next = 2.0 * box_now - box_before + STEP_SCALE * pull / mass
    reactions(0, lambda: None)
    advance(j, value_ref, old_ref, force_ref, sum_ref, node_mass_ref, modes_ref, next_ref,
            pieces_ref)

    fill_table(next_ref, pieces_ref, hot_ref, node_ref, elem_ref, table_ref)

    def sample_peer(o):
        sample_block(1, lax.rem(j + BOX - o, BOX))
        to_sum(1, o).start()

    repeat(1, BOX, sample_peer)
    sample_block(1, j)
    order_hots(dest_ref, order_ref)
    pull = pulls(1, box_next)
    box_after = 2.0 * box_next - box_now + STEP_SCALE * pull / mass
    for m in range(8):
        ways[m] = jnp.broadcast_to(box_after[m : m + 1, :], (8, 128))
    returned[i] = ways[lax.div(i, 2)]
    forces(1, next_ref)
    reactions(1, lambda: repeat(1, MER, lambda o: to_back(o).start()))
    advance(j, next_ref, value_ref, force_ref, sum_ref, node_mass_ref, modes_ref, out_ref)

    repeat(1, MER, lambda o: to_back(o).wait_recv())
    even = jnp.concatenate([returned[2 * r, 0:1, :] for r in range(8)], axis=0)
    odd = jnp.concatenate([returned[2 * r + 1, 0:1, :] for r in range(8)], axis=0)
    box = halves(even, odd, half)
    line = jnp.concatenate([box[m : m + 1, :] for m in range(8)], axis=1)
    pieces = jnp.concatenate([piece.astype(F32) for piece in split3(line)], axis=0).astype(BF16)
    for r in range(8):
        out = dot(pieces, order_ref[r])
        box_out_ref[r : r + 1, :] = out[0:1] + (out[1:2] + out[2:3])

    def sent(o):
        to_share(o).wait_send()
        for step in range(2):
            to_sum(step, o).wait_send()
            to_drive(step, o).wait_send()

    repeat(1, BOX, sent)

    def sent_far(o):
        to_part(o).wait_send()
        to_back(o).wait_send()

    repeat(1, MER, sent_far)
    for step in range(2):
        for copy in to_edges(step):
            copy.wait_send()


def hand_over_kernel(final_ref, box_ref, out_ref, box_out_ref, sem):
    copies = [
        pltpu.make_async_copy(final_ref, out_ref, sem.at[0]),
        pltpu.make_async_copy(box_ref, box_out_ref, sem.at[1]),
    ]
    for copy in copies:
        copy.start()
    for copy in copies:
        copy.wait()


def per_device(
    annulus, annulus_prev, derivative, radial_modulus, shear_modulus, node_mass, element_modes,
    upper_rows, lower_rows, coupling_rows, coupling_target, box_field, box_prev, box_angle,
    box_spring, box_mass, box_weight, box_slot,
):
    flat = NODES * COLS
    args = [
        x.reshape(8, 128)
        for x in (box_angle, box_slot, box_spring, box_mass, box_weight, box_field, box_prev)
    ] + [
        coupling_rows.reshape(16, 128), coupling_target.reshape(16, 128),
        lower_rows.reshape(2, 128), upper_rows.reshape(2, 128),
        annulus.reshape(flat, ELEMS), annulus_prev.reshape(flat, ELEMS), derivative,
        radial_modulus, shear_modulus, node_mass, element_modes.reshape(1, ELEMS),
    ]
    vmem = pltpu.VMEM
    scratch = [vmem(x.shape, x.dtype) for x in args]
    scratch[VALUES] = vmem((PADDED, ELEMS), F32)
    scratch += [
        vmem((8, 8, 128), F32),
        vmem((8, 128), I32),
        vmem((8, 8, 128), F32),
        vmem((ALL_GROUPS, 128), I32),
        vmem((ALL_GROUPS, 128), I32),
        vmem((MER, 8, 128), F32),
        vmem((2, 8, 128), F32),
        vmem((BOX, 2, 8, 128), F32),
        vmem((ROWS, COLS, 128), F32),
        vmem((GROUPS + 2, COLS, 128), F32),
        vmem((flat, ELEMS), F32),
        vmem((PADDED, ELEMS), F32),
        vmem((CHUNKS, COLS, 128), BF16),
        vmem((CHUNKS, COLS, 128), BF16),
        vmem((2 * PAIRS * COLS, ALL_GROUPS * 128), BF16),
        vmem((PAIRS * COLS, 256), F32),
        vmem((2, 4, COLS, 128), F32),
        vmem((2, 4, COLS, 128), F32),
        vmem((2, BOX, 8, 128), F32),
        vmem((2, BOX, 8, 128), F32),
        vmem((2, 8, 128), F32),
        vmem((2, BOX, 8, 128), F32),
        vmem((8, 8, 128), F32),
        vmem((MER, 8, 128), F32),
        vmem((PAIRS * COLS, 512), BF16),
        vmem((256, ALL_GROUPS * 128), BF16),
        vmem((128, 128), F32),
        vmem((ROWS, 128), I32),
        vmem((ROWS, 128), I32),
        vmem((CHUNKS + 8, 128), I32),
        vmem((CHUNKS, 128), I32),
        vmem((ROWS, 128), I32),
        pltpu.SMEM((CHUNKS + 8, 128), I32),
        pltpu.SemaphoreType.DMA((1,)),
        vmem((CHUNKS, 256, 256), BF16),
        vmem((8, 1024, 128), BF16),
    ]
    dma = pltpu.SemaphoreType.DMA
    scratch += [dma((INPUTS,))] + [dma((MER,))] * 2 + [dma((BOX,))] * 2 + [dma((2, 2))] * 2
    scratch += [dma((2, BOX))] * 4 + [dma((MER,))] * 2
    any_space = pl.BlockSpec(memory_space=pl.ANY)
    final, box_out = pl.pallas_call(
        whole_kernel,
        out_shape=[jax.ShapeDtypeStruct((flat, ELEMS), F32), jax.ShapeDtypeStruct((8, 128), F32)],
        in_specs=[pl.BlockSpec(memory_space=pltpu.HBM)] * INPUTS,
        out_specs=[pl.BlockSpec(memory_space=pltpu.VMEM)] * 2,
        scratch_shapes=scratch,
        compiler_params=pltpu.CompilerParams(
            vmem_limit_bytes=44 << 20, collective_id=0, has_side_effects=True),
        name="coupled_steps",
    )(*[pltpu.with_memory_space_constraint(x, pltpu.HBM) for x in args])
    final, box_out = pl.pallas_call(
        hand_over_kernel,
        out_shape=[jax.ShapeDtypeStruct((flat, ELEMS), F32), jax.ShapeDtypeStruct((8, 128), F32)],
        in_specs=[pl.BlockSpec(memory_space=pltpu.VMEM)] * 2,
        out_specs=[any_space] * 2,
        scratch_shapes=[dma((2,))],
        compiler_params=pltpu.CompilerParams(vmem_limit_bytes=4 << 20),
        name="hand_over",
    )(final, box_out)
    return final.reshape(NODES, COLS, ELEMS), box_out.reshape(1024)


def solution(mesh):
    mer_box = P(("mer", "box"))
    in_specs = (
        P(None, "box", "mer"), P(None, "box", "mer"), P(),
        P(None, "mer"), P(None, "mer"), P(None, "mer"),
        P("mer"), P("mer"), P("mer"), P("mer"), P("mer", None),
        mer_box, mer_box, mer_box, mer_box, mer_box, mer_box, mer_box,
    )
    return jax.shard_map(
        per_device, mesh=mesh, in_specs=in_specs,
        out_specs=(P(None, "box", "mer"), mer_box), check_vma=False,
    )
```

```python
import jax
import jax.numpy as jnp
from jax import lax
from jax.experimental import pallas as pl
from jax.experimental.pallas import tpu as pltpu
from jax.sharding import PartitionSpec as P

F32 = jnp.float32
BF16 = jnp.bfloat16
I32 = jnp.int32
MESH = pl.DeviceIdType.MESH

MER, BOX = 16, 8
MODES = 256
NODES, COLS, ELEMS = 25, 64, 128
PAIRS = 13
GROUPS = 16
ALL_GROUPS = 20
CHUNKS = 32
ROWS = 64
STEP_SCALE = 0.25


def iota(shape, dim):
    return lax.broadcasted_iota(I32, shape, dim)


def hot(mask):
    return jnp.where(mask, 1.0, 0.0).astype(BF16)


def dot(a, b):
    return jnp.dot(a, b, preferred_element_type=F32)


def dot_nt(a, b):
    return lax.dot_general(a, b, (((1,), (1,)), ((), ())), preferred_element_type=F32)


def split2(x):
    hi = x.astype(BF16)
    return hi, (x - hi.astype(F32)).astype(BF16)


def split3(x):
    hi = x.astype(BF16)
    rest = x - hi.astype(F32)
    mid = rest.astype(BF16)
    return hi, mid, (rest - mid.astype(F32)).astype(BF16)


def take_lanes(x, index):
    return jnp.take_along_axis(x, index, axis=1, mode="promise_in_bounds")


def sincos(x):
    k = jnp.floor(x * 0.6366197723675814 + 0.5)
    r = x - k * 1.5703125
    r = r - k * 4.837512969970703125e-4
    r = r - k * 7.54978995489188216e-8
    z = r * r
    s = ((-1.9515295891e-4 * z + 8.3321608736e-3) * z - 1.6666654611e-1) * z * r + r
    c = ((2.443315711809948e-5 * z - 1.388731625493765e-3) * z + 4.166664568298827e-2) * z * z
    c = c - 0.5 * z + 1.0
    q = k.astype(I32)
    odd = (q & 1) == 1
    sine = jnp.where(odd, c, s)
    cosine = jnp.where(odd, s, c)
    sine = jnp.where((q & 2) == 2, -sine, sine)
    cosine = jnp.where(((q + 1) & 2) == 2, -cosine, cosine)
    return sine, cosine


def before_lane():
    return hot(iota((128, 128), 0) < iota((128, 128), 1))


def order_nodes(sources, dest_ref, send_ref, fields):
    tri = before_lane()
    part = sources[1] & (MER - 1)
    values = [sources[0], (sources[1] >> 4).astype(F32)] + list(sources[2:])
    for r in range(8):
        for f in range(7):
            fields[r, f : f + 1, :] = values[f][r : r + 1, :]
        fields[r, 7:8, :] = jnp.zeros((1, 128), F32)
    base = jnp.zeros((MER, 1), F32)
    total = jnp.zeros((24, 1024), F32)
    for r in range(8):
        mine = part[r : r + 1, :]
        member = jnp.where(iota((MER, 128), 0) == mine, 1.0, 0.0)
        rank = dot(member.astype(BF16), tri) + base
        place = jnp.sum(member * rank, axis=0, keepdims=True).astype(I32)
        base = base + jnp.sum(member, axis=1, keepdims=True)
        dest = mine * 64 + place
        dest_ref[r : r + 1, :] = dest
        order = hot(iota((1024, 128), 0) == dest)
        pieces = jnp.concatenate(split3(fields[r]), axis=0)
        total = total + dot_nt(pieces, order)
    sorted_fields = total[0:8] + (total[8:16] + total[16:24])
    for m in range(8):
        send_ref[m] = sorted_fields[:, m * 128 : (m + 1) * 128]


def pick_rows(shape, source):
    return hot(iota(shape, 1) == source(iota(shape, 0)))


def row_table(rows, target, edges, node_ref, elem_ref, start_ref, count_ref, meta_ref, shift_ref):
    tri = before_lane()
    reader = (target & (BOX - 1)) * MER + (target >> 3)
    node = (rows >> 7).astype(F32)
    elem = (rows & 127).astype(F32)
    readers = iota((128, 128), 0)
    seen = jnp.zeros((128, 128), F32)
    for r in range(16):
        seen = seen + jnp.where(readers == reader[r : r + 1, :], 1.0, 0.0)
    count = jnp.sum(seen, axis=1, keepdims=True)
    wide = jnp.broadcast_to(count, (128, 128)).astype(BF16)
    below = hot(iota((128, 128), 1) < iota((128, 128), 0))
    start = dot(below, wide)
    base = start
    table = jnp.zeros((2 * GROUPS, 128), F32)
    for r in range(16):
        mine = reader[r : r + 1, :]
        member = jnp.where(readers == mine, 1.0, 0.0)
        rank = dot(member.astype(BF16), tri) + base
        place = jnp.sum(member * rank, axis=0, keepdims=True).astype(I32)
        base = base + jnp.sum(member, axis=1, keepdims=True)
        group = iota((GROUPS, 128), 0) == (place >> 7)
        values = jnp.concatenate(
            [
                jnp.where(group, jnp.broadcast_to(node[r : r + 1, :], (GROUPS, 128)), 0.0),
                jnp.where(group, jnp.broadcast_to(elem[r : r + 1, :], (GROUPS, 128)), 0.0),
            ],
            axis=0,
        ).astype(BF16)
        table = table + dot_nt(values, hot(readers == (place & 127)))
    node_ref[0:GROUPS, :] = table[0:GROUPS].astype(I32)
    elem_ref[0:GROUPS, :] = table[GROUPS : 2 * GROUPS].astype(I32)
    for k, edge in enumerate(edges):
        node_ref[GROUPS + 2 * k : GROUPS + 2 * k + 2, :] = edge >> 7
        elem_ref[GROUPS + 2 * k : GROUPS + 2 * k + 2, :] = edge & 127

    high = jnp.floor(start * (1.0 / 16.0))
    parts = [high.astype(BF16), (start - 16.0 * high).astype(BF16)]
    same_half = (iota((128, 128), 0) & 1) == (iota((128, 128), 1) >> 6)

    def halved(x):
        return jnp.where(same_half, x.astype(F32), 0.0).astype(BF16)

    def joined(left, right):
        return (16.0 * dot(left, right[0]) + dot(left, right[1])).astype(I32)

    own = hot((iota((ROWS, 128), 1) >> 1) == iota((ROWS, 128), 0))
    first = joined(pick_rows((ROWS, 128), lambda row: (row >> 1) * 4), parts) >> 7
    start_ref[...] = joined(own, [halved(part) for part in parts]) - 128 * first
    count_ref[...] = dot(own, halved(wide)).astype(I32)
    group = joined(pick_rows((CHUNKS, 128), lambda chunk: chunk * 4), parts) >> 7
    after = joined(pick_rows((CHUNKS, 128), lambda chunk: (chunk + 1) * 4), parts) >> 7
    shift_ref[...] = after - group
    meta_ref[0:CHUNKS, :] = group
    last = jnp.sum(jnp.where(group <= iota((CHUNKS, 128), 1), 1, 0), axis=0, keepdims=True) - 1
    meta_ref[CHUNKS : CHUNKS + 8, :] = jnp.broadcast_to(last, (8, 128))


def halves(even, odd, half):
    low = jnp.where(half == 0, even, pltpu.roll(even, 64, 1))
    high = jnp.where(half == 1, odd, pltpu.roll(odd, 64, 1))
    return jnp.where(iota((8, 128), 1) < 64, low, high)


def harmonics(j, angles, filled, block, harmonic_ref):
    sub = iota((8, 128), 0).astype(F32)
    first = (lax.rem(j, 4) * 64).astype(F32)
    is_sine = j >= 4
    for r in range(8):
        angle = jnp.broadcast_to(angles[r : r + 1, :], (8, 128))
        base_sin, base_cos = sincos(angle * (sub + first))
        step_sin, step_cos = sincos(angle * (sub * 8.0))
        keep = jnp.broadcast_to(filled[r : r + 1, :], (8, 128)) > 0
        a = jnp.where(keep, jnp.where(is_sine, base_sin, base_cos), 0.0)
        b = jnp.where(keep, jnp.where(is_sine, -base_cos, base_sin), 0.0)
        for t in range(8):
            harmonic_ref[block * 8 + r, t * 8 : (t + 1) * 8, :] = (
                a * step_cos[t : t + 1, :] - b * step_sin[t : t + 1, :]
            )


def gather_rows(values_ref, node, elem):
    index = jnp.broadcast_to(elem, (8, 128))
    node = jnp.broadcast_to(node, (8, 128))
    acc = [jnp.zeros((8, 128), F32) for _ in range(8)]
    for a in range(NODES):
        mask = node == a
        for c in range(8):
            taken = take_lanes(values_ref[a * 64 + c * 8 : a * 64 + c * 8 + 8, :], index)
            acc[c] = jnp.where(mask, taken, acc[c])
    return acc


MATRIX_GROUPS, LANE_GROUPS = 6, 2


def keep_pieces(values, a, pieces_ref):
    rows = slice((a // 2) * 64, (a // 2) * 64 + 64)
    lane = (a % 2) * 128
    high, low = split2(values)
    pieces_ref[rows, lane : lane + 128] = high
    pieces_ref[rows, 256 + lane : 384 + lane] = low


def slot_hots(node_ref, elem_ref, hot_ref):
    def body(g, carry):
        lane = (node_ref[pl.ds(g, 1), :] & 1) * 128 + elem_ref[pl.ds(g, 1), :]
        hot_ref[g] = hot(iota((256, 128), 0) == lane)
        return carry

    lax.fori_loop(0, ALL_GROUPS, body, 0)


def fill_table(values_ref, pieces_ref, hot_ref, node_ref, elem_ref, table_ref):
    def body(t, carry):
        first = t * (MATRIX_GROUPS + LANE_GROUPS)
        right = jnp.concatenate([hot_ref[first + k] for k in range(MATRIX_GROUPS)], axis=1)
        out = dot(pieces_ref[...], jnp.concatenate([right, right], axis=0))
        for k in range(LANE_GROUPS):
            g = first + MATRIX_GROUPS + k
            acc = gather_rows(values_ref, node_ref[pl.ds(g, 1), :], elem_ref[pl.ds(g, 1), :])
            for c in range(8):
                table_ref[g, c * 8 : (c + 1) * 8, :] = acc[c]
        for k in range(MATRIX_GROUPS):
            g = first + k
            pair = node_ref[pl.ds(g, 1), :] >> 1
            acc = jnp.zeros((COLS, 128), F32)
            for a in range(PAIRS):
                acc = jnp.where(
                    pair == a, out[a * 64 : (a + 1) * 64, k * 128 : (k + 1) * 128], acc)
            table_ref[g] = acc
        return carry

    lax.fori_loop(0, GROUPS // (MATRIX_GROUPS + LANE_GROUPS), body, 0)


def sample_nodes(table_ref, local_ref, meta_ref, block, harmonic_ref):
    rows = []
    for r in range(8):
        row = block * 8 + r
        group = lax.clamp(0, meta_ref[block * 4 + r // 2, 0], GROUPS)
        local = jnp.broadcast_to(local_ref[pl.ds(row, 1), :], (8, 128))
        index = local & 127
        second = local > 127
        acc = jnp.zeros((8, 128), F32)
        for c in range(8):
            columns = slice(c * 8, (c + 1) * 8)
            taken = jnp.where(
                second,
                take_lanes(table_ref[group + 1, columns, :], index),
                take_lanes(table_ref[group, columns, :], index),
            )
            acc = acc + taken * harmonic_ref[row, columns, :]
        rows.append(jnp.sum(acc, axis=0, keepdims=True))
    return jnp.concatenate(rows, axis=0)


def small_stack(matrix):
    high, low = split2(matrix)
    return jnp.concatenate([high, high, low], axis=1)


def compute_force(j, half, values_ref, deriv_ref, radial_ref, shear_ref, force_ref):
    deriv = deriv_ref[...]
    stack = small_stack(deriv[0:32, 0:32])
    stack_t = small_stack(deriv.T[0:32, 0:32])
    radial = jnp.concatenate([radial_ref[...], jnp.zeros((7, 128), F32)], axis=0)
    radial = jnp.concatenate([radial] * 16, axis=1)
    shear = shear_ref[...]
    first = lax.rem(j, 4) * 64

    def times(left, x):
        high, low = split2(x)
        return dot(left, jnp.concatenate([high, low, high], axis=0))

    def body(k, carry):
        x = jnp.concatenate(
            [values_ref[pl.ds(k * 16 + c, 32, stride=64), :] for c in range(16)], axis=1
        )
        back = times(stack_t, times(stack, x) * radial)
        for c in range(16):
            wave = (first + k * 16 + c).astype(F32) * (2.0 / MODES)
            lanes = slice(c * 128, (c + 1) * 128)
            force_ref[pl.ds(k * 16 + c, NODES, stride=64), :] = (
                -back[0:NODES, lanes] - shear * (wave * wave) * x[0:NODES, lanes]
            )
        return carry

    lax.fori_loop(2 * half, 2 * half + 2, body, 0)


def edge_forces(force_ref, node_ref, elem_ref, edge_ref):
    def body(g, carry):
        acc = gather_rows(
            force_ref, node_ref[pl.ds(GROUPS + g, 1), :], elem_ref[pl.ds(GROUPS + g, 1), :]
        )
        for c in range(8):
            edge_ref[g, c * 8 : (c + 1) * 8, :] = acc[c]
        return carry

    lax.fori_loop(0, 4, body, 0)


def row_reactions(drives, block, carry, local_ref, shift_ref, harmonic_ref, high_ref, low_ref):
    for k in range(4):
        chunk = block * 4 + k
        pieces, hots = [], []
        for odd in range(2):
            r = 2 * k + odd
            pieces.append(split2(harmonic_ref[block * 8 + r] * drives[r : r + 1, :]))
            hots.append(hot(iota((256, 128), 0) == local_ref[pl.ds(block * 8 + r, 1), :]))
        left = jnp.concatenate(
            [
                jnp.concatenate([pieces[0][p], pieces[1][p]], axis=1) for p in range(2)
            ],
            axis=0,
        )
        out = dot_nt(left, jnp.concatenate(hots, axis=1))
        out = out[0:COLS] + out[COLS : 2 * COLS]
        here = carry[0] + out[:, 0:128]
        there = carry[1] + out[:, 128:256]
        high, low = split2(here)
        high_ref[chunk] = high
        low_ref[chunk] = low
        moved = jnp.broadcast_to(shift_ref[pl.ds(chunk, 1), :], (COLS, 128)) > 0
        carry = (jnp.where(moved, there, here), jnp.where(moved, 0.0, there))
    return carry


def scatter_rows(sources, first, node_ref, hot_ref, high_ref, low_ref, left_ref, sum_ref):
    rights = []
    for h in range(4):
        pair = node_ref[pl.ds(first + h, 1), :] >> 1
        high = high_ref[sources[h]]
        low = low_ref[sources[h]]
        for a in range(PAIRS):
            mask = jnp.broadcast_to(hot(pair == a), (COLS, 128))
            rows = slice(a * 64, (a + 1) * 64)
            left_ref[rows, h * 128 : (h + 1) * 128] = high * mask
            left_ref[rows, 512 + h * 128 : 640 + h * 128] = low * mask
        rights.append(hot_ref[first + h])
    sum_ref[...] += dot_nt(left_ref[...], jnp.concatenate(rights + rights, axis=1))


def advance(j, now_ref, before_ref, force_ref, sum_ref, mass_ref, modes_ref, next_ref,
            pieces_ref=None):
    order = lax.rem(j, 4) * 64 + iota((COLS, 128), 0)
    live = order < modes_ref[...]
    scale = STEP_SCALE / mass_ref[...]
    for a in range(NODES):
        rows = slice(a * 64, (a + 1) * 64)
        pair = a // 2
        lanes = slice((a % 2) * 128, (a % 2) * 128 + 128)
        total = force_ref[rows, :] + sum_ref[pair * 64 : (pair + 1) * 64, lanes]
        after = 2.0 * now_ref[rows, :] - before_ref[rows, :]
        after = after + jnp.where(live, scale[a : a + 1, :], 0.0) * total
        next_ref[rows, :] = after
        if pieces_ref is not None:
            keep_pieces(after, a, pieces_ref)


INPUTS = 18
VALUES = 11
PADDED = 32 * COLS


def whole_kernel(*refs):
    hbm = refs[:INPUTS]
    out_ref, box_out_ref = refs[INPUTS : INPUTS + 2]
    vmem = refs[INPUTS + 2 : 2 * INPUTS + 2]
    (
        fields, dest_ref, send_ref, node_ref, elem_ref, received, share, shared, harmonic_ref,
        table_ref, force_ref, next_ref, last_ref, high_ref, low_ref, left_ref, sum_ref,
        edge_ref, edges, partial, sums, drive, drives, ways, returned, box_last,
        pieces_ref, hot_ref, square_ref, start_ref, count_ref, meta_ref, shift_ref, local_ref,
        meta_smem, meta_sem,
        load_sem, send_sem, recv_sem, share_send, share_recv, edge_send, edge_recv,
        sum_send, sum_recv, drive_send, drive_recv, way_send, way_recv, out_sem,
    ) = refs[2 * INPUTS + 2 :]
    (
        angle_ref, slot_ref, spring_ref, mass_ref, weight_ref, now_ref, before_ref,
        rows_ref, target_ref, lower_ref, upper_ref, value_ref, old_ref, deriv_ref,
        radial_ref, shear_ref, node_mass_ref, modes_ref,
    ) = vmem
    i = lax.axis_index("mer")
    j = lax.axis_index("box")
    above = lax.rem(i + 1, MER)
    below = lax.rem(i + MER - 1, MER)

    def landing(k):
        if k == VALUES:
            return value_ref.at[0 : NODES * COLS]
        return vmem[k]

    loads = [pltpu.make_async_copy(hbm[k], landing(k), load_sem.at[k]) for k in range(INPUTS)]
    for load in loads[:7]:
        load.start()
    barrier = pltpu.get_barrier_semaphore()
    for o in range(1, MER):
        pl.semaphore_signal(
            barrier, inc=1, device_id=(lax.rem(i + o, MER), j), device_id_type=MESH)
    for o in range(1, BOX):
        pl.semaphore_signal(
            barrier, inc=1, device_id=(i, lax.rem(j + o, BOX)), device_id_type=MESH)

    for load in loads[7:]:
        load.start()

    def way(source, target, send, recv, device):
        return pltpu.make_async_remote_copy(
            src_ref=source, dst_ref=target, send_sem=send, recv_sem=recv,
            device_id=device, device_id_type=MESH)

    def to_part(o):
        q = lax.rem(i + o, MER)
        return way(send_ref.at[lax.div(q, 2)], received.at[i], send_sem.at[o], recv_sem.at[o], (q, j))

    def to_share(o):
        q = lax.rem(j + o, BOX)
        return way(share, shared.at[j], share_send.at[o], share_recv.at[o], (i, q))

    def to_sum(step, o):
        q = lax.rem(j + BOX - o, BOX)
        return way(partial.at[step, q], sums.at[step, o],
                   sum_send.at[step, o], sum_recv.at[step, o], (i, q))

    def to_drive(step, o):
        q = lax.rem(j + o, BOX)
        return way(drive.at[step], drives.at[step, j],
                   drive_send.at[step, o], drive_recv.at[step, o], (i, q))

    def to_back(o):
        q = lax.rem(i + o, MER)
        return way(ways.at[lax.div(q, 2)], returned.at[i], way_send.at[o], way_recv.at[o], (q, j))

    def to_edges(step):
        return (
            way(edge_ref.at[step, 2:4], edges.at[step, 0:2],
                edge_send.at[step, 0], edge_recv.at[step, 0], (above, j)),
            way(edge_ref.at[step, 0:2], edges.at[step, 2:4],
                edge_send.at[step, 1], edge_recv.at[step, 1], (below, j)),
        )

    def repeat(first, last, work):
        def body(o, carry):
            work(o)
            return carry

        lax.fori_loop(first, last, body, 0)

    for load in loads[:7]:
        load.wait()
    order_nodes([ref[...] for ref in vmem[:7]], dest_ref, send_ref, fields)
    pl.semaphore_wait(barrier, MER + BOX - 2)
    repeat(1, MER, lambda o: to_part(o).start())
    received[i] = send_ref[lax.div(i, 2)]
    for load in loads[7:]:
        load.wait()
    row_table(rows_ref[...], target_ref[...], (lower_ref[...], upper_ref[...]), node_ref, elem_ref,
              start_ref, count_ref, meta_ref, shift_ref)
    meta = pltpu.make_async_copy(meta_ref, meta_smem, meta_sem.at[0])
    meta.start()
    slot_hots(node_ref, elem_ref, hot_ref)
    square_ref[...] = jnp.zeros_like(square_ref)
    square_ref[0:NODES, 0:NODES] = deriv_ref[...]
    for ref in (value_ref, next_ref):
        ref[NODES * COLS : PADDED, :] = jnp.zeros((PADDED - NODES * COLS, ELEMS), F32)
    for a in range(NODES):
        keep_pieces(value_ref[a * COLS : (a + 1) * COLS, :], a, pieces_ref)
    for lane in (128, 384):
        pieces_ref[(PAIRS - 1) * COLS : PAIRS * COLS, lane : lane + 128] = jnp.zeros(
            (COLS, 128), BF16)
    table_ref[GROUPS : GROUPS + 2] = jnp.zeros((2, COLS, 128), F32)
    meta.wait()

    repeat(1, MER, lambda o: to_part(o).wait_recv())
    half = lax.rem(i, 2)
    own = []
    for f in range(7):
        even = jnp.concatenate([received[2 * r, f : f + 1, :] for r in range(8)], axis=0)
        odd = jnp.concatenate([received[2 * r + 1, f : f + 1, :] for r in range(8)], axis=0)
        own.append(halves(even, odd, half))
    share[0] = own[0]
    share[1] = own[1]
    repeat(1, BOX, lambda o: to_share(o).start())
    shared[j] = share[...]
    spring, mass, weight, box_now, box_before = own[2:]

    def first_forces(ref):
        compute_force(j, 0, ref, square_ref, radial_ref, shear_ref, force_ref)

    def forces(step, ref):
        compute_force(j, 1, ref, square_ref, radial_ref, shear_ref, force_ref)
        edge_forces(force_ref, node_ref, elem_ref, edge_ref.at[step])
        for copy in to_edges(step):
            copy.start()

    def sample_block(step, block):
        partial[step, block] = sample_nodes(table_ref, local_ref, meta_smem, block, harmonic_ref)

    def pulls(step, now):
        sample = partial[step, j]
        for o in range(1, BOX):
            to_sum(step, o).wait_recv()
            sample = sample + sums[step, o]
        pull = spring * (sample - now)
        drive[step] = -weight * pull
        repeat(1, BOX, lambda o: to_drive(step, o).start())
        drives[step, j] = drive[step]
        return pull

    def reactions(step):
        sum_ref[...] = jnp.zeros_like(sum_ref)

        def work(k, carry):
            for block in (2 * k, 2 * k + 1):
                @pl.when(block != j)
                def _():
                    to_drive(step, lax.rem(j + BOX - block, BOX)).wait_recv()

            for block in (2 * k, 2 * k + 1):
                carry = row_reactions(drives[step, block], block, carry, local_ref, shift_ref,
                                      harmonic_ref, high_ref, low_ref)
            return carry

        nothing = jnp.zeros((COLS, 128), F32)
        lax.fori_loop(0, BOX // 2, work, (nothing, nothing))

        def scatter(t, carry):
            sources = [
                lax.clamp(0, meta_smem[CHUNKS, t * 4 + h], CHUNKS - 1) for h in range(4)
            ]
            scatter_rows(sources, t * 4, node_ref, hot_ref, high_ref, low_ref, left_ref, sum_ref)
            return carry

        lax.fori_loop(0, GROUPS // 4, scatter, 0)
        for copy in to_edges(step):
            copy.wait_recv()
        for g in range(4):
            ghost = (i == 0) if g < 2 else (i == MER - 1)
            high, low = split2(jnp.where(ghost, 0.0, edges[step, g]))
            high_ref[CHUNKS + g] = high
            low_ref[CHUNKS + g] = low
        scatter_rows([CHUNKS + h for h in range(4)], GROUPS, node_ref, hot_ref, high_ref,
                     low_ref, left_ref, sum_ref)

    fill_table(value_ref, pieces_ref, hot_ref, node_ref, elem_ref, table_ref)

    def enter(block):
        rows = pl.ds(pl.multiple_of(block * 8, 8), 8)
        places = shared[block, 1].astype(I32)
        filled = jnp.where(places < count_ref[rows, :], 1, 0)
        local_ref[rows, :] = jnp.where(filled > 0, start_ref[rows, :] + places, 0)
        harmonics(j, shared[block, 0], filled, block, harmonic_ref)
        sample_block(0, block)

    enter(j)

    def enter_peer(o):
        to_share(o).wait_recv()
        enter(lax.rem(j + BOX - o, BOX))
        to_sum(0, o).start()

    repeat(1, BOX, enter_peer)
    first_forces(value_ref)
    pull = pulls(0, box_now)
    forces(0, value_ref)
    box_next = 2.0 * box_now - box_before + STEP_SCALE * pull / mass
    reactions(0)
    advance(j, value_ref, old_ref, force_ref, sum_ref, node_mass_ref, modes_ref, next_ref,
            pieces_ref)

    fill_table(next_ref, pieces_ref, hot_ref, node_ref, elem_ref, table_ref)

    def sample_peer(o):
        sample_block(1, lax.rem(j + BOX - o, BOX))
        to_sum(1, o).start()

    repeat(1, BOX, sample_peer)
    sample_block(1, j)
    first_forces(next_ref)
    pull = pulls(1, box_next)
    box_after = 2.0 * box_next - box_now + STEP_SCALE * pull / mass
    for m in range(8):
        ways[m] = jnp.broadcast_to(box_after[m : m + 1, :], (8, 128))
    repeat(1, MER, lambda o: to_back(o).start())
    returned[i] = ways[lax.div(i, 2)]
    forces(1, next_ref)
    reactions(1)
    advance(j, next_ref, value_ref, force_ref, sum_ref, node_mass_ref, modes_ref, out_ref)

    repeat(1, MER, lambda o: to_back(o).wait_recv())
    even = jnp.concatenate([returned[2 * r, 0:1, :] for r in range(8)], axis=0)
    odd = jnp.concatenate([returned[2 * r + 1, 0:1, :] for r in range(8)], axis=0)
    box = halves(even, odd, half)
    line = jnp.concatenate([box[m : m + 1, :] for m in range(8)], axis=1)
    pieces = jnp.concatenate([piece.astype(F32) for piece in split3(line)], axis=0).astype(BF16)
    for r in range(8):
        out = dot(pieces, hot(iota((1024, 128), 0) == dest_ref[r : r + 1, :]))
        box_last[r : r + 1, :] = out[0:1] + (out[1:2] + out[2:3])
    box_out_ref[...] = box_last[...]

    def sent(o):
        to_share(o).wait_send()
        for step in range(2):
            to_sum(step, o).wait_send()
            to_drive(step, o).wait_send()

    repeat(1, BOX, sent)

    def sent_far(o):
        to_part(o).wait_send()
        to_back(o).wait_send()

    repeat(1, MER, sent_far)
    for step in range(2):
        for copy in to_edges(step):
            copy.wait_send()


def hand_over_kernel(final_ref, box_ref, out_ref, box_out_ref, sem):
    copies = [
        pltpu.make_async_copy(final_ref, out_ref, sem.at[0]),
        pltpu.make_async_copy(box_ref, box_out_ref, sem.at[1]),
    ]
    for copy in copies:
        copy.start()
    for copy in copies:
        copy.wait()


def per_device(
    annulus, annulus_prev, derivative, radial_modulus, shear_modulus, node_mass, element_modes,
    upper_rows, lower_rows, coupling_rows, coupling_target, box_field, box_prev, box_angle,
    box_spring, box_mass, box_weight, box_slot,
):
    flat = NODES * COLS
    args = [
        x.reshape(8, 128)
        for x in (box_angle, box_slot, box_spring, box_mass, box_weight, box_field, box_prev)
    ] + [
        coupling_rows.reshape(16, 128), coupling_target.reshape(16, 128),
        lower_rows.reshape(2, 128), upper_rows.reshape(2, 128),
        annulus.reshape(flat, ELEMS), annulus_prev.reshape(flat, ELEMS), derivative,
        radial_modulus, shear_modulus, node_mass, element_modes.reshape(1, ELEMS),
    ]
    vmem = pltpu.VMEM
    scratch = [vmem(x.shape, x.dtype) for x in args]
    scratch[VALUES] = vmem((PADDED, ELEMS), F32)
    scratch += [
        vmem((8, 8, 128), F32),
        vmem((8, 128), I32),
        vmem((8, 8, 128), F32),
        vmem((ALL_GROUPS, 128), I32),
        vmem((ALL_GROUPS, 128), I32),
        vmem((MER, 8, 128), F32),
        vmem((2, 8, 128), F32),
        vmem((BOX, 2, 8, 128), F32),
        vmem((ROWS, COLS, 128), F32),
        vmem((GROUPS + 2, COLS, 128), F32),
        vmem((flat, ELEMS), F32),
        vmem((PADDED, ELEMS), F32),
        vmem((flat, ELEMS), F32),
        vmem((CHUNKS + 4, COLS, 128), BF16),
        vmem((CHUNKS + 4, COLS, 128), BF16),
        vmem((PAIRS * COLS, 1024), BF16),
        vmem((PAIRS * COLS, 256), F32),
        vmem((2, 4, COLS, 128), F32),
        vmem((2, 4, COLS, 128), F32),
        vmem((2, BOX, 8, 128), F32),
        vmem((2, BOX, 8, 128), F32),
        vmem((2, 8, 128), F32),
        vmem((2, BOX, 8, 128), F32),
        vmem((8, 8, 128), F32),
        vmem((MER, 8, 128), F32),
        vmem((8, 128), F32),
        vmem((PAIRS * COLS, 512), BF16),
        vmem((ALL_GROUPS, 256, 128), BF16),
        vmem((128, 128), F32),
        vmem((ROWS, 128), I32),
        vmem((ROWS, 128), I32),
        vmem((CHUNKS + 8, 128), I32),
        vmem((CHUNKS, 128), I32),
        vmem((ROWS, 128), I32),
        pltpu.SMEM((CHUNKS + 8, 128), I32),
        pltpu.SemaphoreType.DMA((1,)),
    ]
    dma = pltpu.SemaphoreType.DMA
    scratch += [dma((INPUTS,))] + [dma((MER,))] * 2 + [dma((BOX,))] * 2 + [dma((2, 2))] * 2
    scratch += [dma((2, BOX))] * 4 + [dma((MER,))] * 2 + [dma((2,))]
    any_space = pl.BlockSpec(memory_space=pl.ANY)
    final, box_out = pl.pallas_call(
        whole_kernel,
        out_shape=[jax.ShapeDtypeStruct((flat, ELEMS), F32), jax.ShapeDtypeStruct((8, 128), F32)],
        in_specs=[pl.BlockSpec(memory_space=pltpu.HBM)] * INPUTS,
        out_specs=[pl.BlockSpec(memory_space=pltpu.VMEM)] * 2,
        scratch_shapes=scratch,
        compiler_params=pltpu.CompilerParams(
            vmem_limit_bytes=44 << 20, collective_id=0, has_side_effects=True),
        name="coupled_steps",
    )(*[pltpu.with_memory_space_constraint(x, pltpu.HBM) for x in args])
    final, box_out = pl.pallas_call(
        hand_over_kernel,
        out_shape=[jax.ShapeDtypeStruct((flat, ELEMS), F32), jax.ShapeDtypeStruct((8, 128), F32)],
        in_specs=[pl.BlockSpec(memory_space=pltpu.VMEM)] * 2,
        out_specs=[any_space] * 2,
        scratch_shapes=[dma((2,))],
        compiler_params=pltpu.CompilerParams(vmem_limit_bytes=4 << 20),
        name="hand_over",
    )(final, box_out)
    return final.reshape(NODES, COLS, ELEMS), box_out.reshape(1024)


def solution(mesh):
    mer_box = P(("mer", "box"))
    in_specs = (
        P(None, "box", "mer"), P(None, "box", "mer"), P(),
        P(None, "mer"), P(None, "mer"), P(None, "mer"),
        P("mer"), P("mer"), P("mer"), P("mer"), P("mer", None),
        mer_box, mer_box, mer_box, mer_box, mer_box, mer_box, mer_box,
    )
    return jax.shard_map(
        per_device, mesh=mesh, in_specs=in_specs,
        out_specs=(P(None, "box", "mer"), mer_box), check_vma=False,
    )
```

```python
import jax
import jax.numpy as jnp
from jax import lax
from jax.experimental import pallas as pl
from jax.experimental.pallas import tpu as pltpu
from jax.sharding import PartitionSpec as P

F32 = jnp.float32
BF16 = jnp.bfloat16
I32 = jnp.int32
MESH = pl.DeviceIdType.MESH

MER, BOX = 16, 8
MODES = 256
NODES, COLS, ELEMS = 25, 64, 128
PAIRS = 13
GROUPS = 16
ALL_GROUPS = 20
CHUNKS = 32
ROWS = 64
STEP_SCALE = 0.25


def iota(shape, dim):
    return lax.broadcasted_iota(I32, shape, dim)


def hot(mask):
    return jnp.where(mask, 1.0, 0.0).astype(BF16)


def dot(a, b):
    return jnp.dot(a, b, preferred_element_type=F32)


def dot_nt(a, b):
    return lax.dot_general(a, b, (((1,), (1,)), ((), ())), preferred_element_type=F32)


def split2(x):
    hi = x.astype(BF16)
    return hi, (x - hi.astype(F32)).astype(BF16)


def split3(x):
    hi = x.astype(BF16)
    rest = x - hi.astype(F32)
    mid = rest.astype(BF16)
    return hi, mid, (rest - mid.astype(F32)).astype(BF16)


def take_lanes(x, index):
    return jnp.take_along_axis(x, index, axis=1, mode="promise_in_bounds")


def sincos(x):
    k = jnp.floor(x * 0.6366197723675814 + 0.5)
    r = x - k * 1.5703125
    r = r - k * 4.837512969970703125e-4
    r = r - k * 7.54978995489188216e-8
    z = r * r
    s = ((-1.9515295891e-4 * z + 8.3321608736e-3) * z - 1.6666654611e-1) * z * r + r
    c = ((2.443315711809948e-5 * z - 1.388731625493765e-3) * z + 4.166664568298827e-2) * z * z
    c = c - 0.5 * z + 1.0
    q = k.astype(I32)
    odd = (q & 1) == 1
    sine = jnp.where(odd, c, s)
    cosine = jnp.where(odd, s, c)
    sine = jnp.where((q & 2) == 2, -sine, sine)
    cosine = jnp.where(((q + 1) & 2) == 2, -cosine, cosine)
    return sine, cosine


def before_lane():
    return hot(iota((128, 128), 0) < iota((128, 128), 1))


def order_nodes(sources, dest_ref, send_ref, fields):
    tri = before_lane()
    part = sources[1] & (MER - 1)
    values = [sources[0], (sources[1] >> 4).astype(F32)] + list(sources[2:])
    for r in range(8):
        for f in range(7):
            fields[r, f : f + 1, :] = values[f][r : r + 1, :]
        fields[r, 7:8, :] = jnp.zeros((1, 128), F32)
    base = jnp.zeros((MER, 1), F32)
    total = jnp.zeros((24, 1024), F32)
    for r in range(8):
        mine = part[r : r + 1, :]
        member = jnp.where(iota((MER, 128), 0) == mine, 1.0, 0.0)
        rank = dot(member.astype(BF16), tri) + base
        place = jnp.sum(member * rank, axis=0, keepdims=True).astype(I32)
        base = base + jnp.sum(member, axis=1, keepdims=True)
        dest = mine * 64 + place
        dest_ref[r : r + 1, :] = dest
        order = hot(iota((1024, 128), 0) == dest)
        pieces = jnp.concatenate(split3(fields[r]), axis=0)
        total = total + dot_nt(pieces, order)
    sorted_fields = total[0:8] + (total[8:16] + total[16:24])
    for m in range(8):
        send_ref[m] = sorted_fields[:, m * 128 : (m + 1) * 128]


def pick_rows(shape, source):
    return hot(iota(shape, 1) == source(iota(shape, 0)))


def row_table(rows, target, edges, node_ref, elem_ref, start_ref, count_ref, meta_ref, shift_ref):
    tri = before_lane()
    reader = (target & (BOX - 1)) * MER + (target >> 3)
    node = (rows >> 7).astype(F32)
    elem = (rows & 127).astype(F32)
    readers = iota((128, 128), 0)
    seen = jnp.zeros((128, 128), F32)
    for r in range(16):
        seen = seen + jnp.where(readers == reader[r : r + 1, :], 1.0, 0.0)
    count = jnp.sum(seen, axis=1, keepdims=True)
    wide = jnp.broadcast_to(count, (128, 128)).astype(BF16)
    below = hot(iota((128, 128), 1) < iota((128, 128), 0))
    start = dot(below, wide)
    base = start
    table = jnp.zeros((2 * GROUPS, 128), F32)
    for r in range(16):
        mine = reader[r : r + 1, :]
        member = jnp.where(readers == mine, 1.0, 0.0)
        rank = dot(member.astype(BF16), tri) + base
        place = jnp.sum(member * rank, axis=0, keepdims=True).astype(I32)
        base = base + jnp.sum(member, axis=1, keepdims=True)
        group = iota((GROUPS, 128), 0) == (place >> 7)
        values = jnp.concatenate(
            [
                jnp.where(group, jnp.broadcast_to(node[r : r + 1, :], (GROUPS, 128)), 0.0),
                jnp.where(group, jnp.broadcast_to(elem[r : r + 1, :], (GROUPS, 128)), 0.0),
            ],
            axis=0,
        ).astype(BF16)
        table = table + dot_nt(values, hot(readers == (place & 127)))
    node_ref[0:GROUPS, :] = table[0:GROUPS].astype(I32)
    elem_ref[0:GROUPS, :] = table[GROUPS : 2 * GROUPS].astype(I32)
    for k, edge in enumerate(edges):
        node_ref[GROUPS + 2 * k : GROUPS + 2 * k + 2, :] = edge >> 7
        elem_ref[GROUPS + 2 * k : GROUPS + 2 * k + 2, :] = edge & 127

    high = jnp.floor(start * (1.0 / 16.0))
    parts = [high.astype(BF16), (start - 16.0 * high).astype(BF16)]
    same_half = (iota((128, 128), 0) & 1) == (iota((128, 128), 1) >> 6)

    def halved(x):
        return jnp.where(same_half, x.astype(F32), 0.0).astype(BF16)

    def joined(left, right):
        return (16.0 * dot(left, right[0]) + dot(left, right[1])).astype(I32)

    own = hot((iota((ROWS, 128), 1) >> 1) == iota((ROWS, 128), 0))
    first = joined(pick_rows((ROWS, 128), lambda row: (row >> 1) * 4), parts) >> 7
    start_ref[...] = joined(own, [halved(part) for part in parts]) - 128 * first
    count_ref[...] = dot(own, halved(wide)).astype(I32)
    group = joined(pick_rows((CHUNKS, 128), lambda chunk: chunk * 4), parts) >> 7
    after = joined(pick_rows((CHUNKS, 128), lambda chunk: (chunk + 1) * 4), parts) >> 7
    shift_ref[...] = after - group
    meta_ref[0:CHUNKS, :] = group
    last = jnp.sum(jnp.where(group <= iota((CHUNKS, 128), 1), 1, 0), axis=0, keepdims=True) - 1
    meta_ref[CHUNKS : CHUNKS + 8, :] = jnp.broadcast_to(last, (8, 128))


def halves(even, odd, half):
    low = jnp.where(half == 0, even, pltpu.roll(even, 64, 1))
    high = jnp.where(half == 1, odd, pltpu.roll(odd, 64, 1))
    return jnp.where(iota((8, 128), 1) < 64, low, high)


def harmonics(j, angles, filled, block, harmonic_ref):
    sub = iota((8, 128), 0).astype(F32)
    first = (lax.rem(j, 4) * 64).astype(F32)
    is_sine = j >= 4
    for r in range(8):
        angle = jnp.broadcast_to(angles[r : r + 1, :], (8, 128))
        base_sin, base_cos = sincos(angle * (sub + first))
        step_sin, step_cos = sincos(angle * (sub * 8.0))
        keep = jnp.broadcast_to(filled[r : r + 1, :], (8, 128)) > 0
        a = jnp.where(keep, jnp.where(is_sine, base_sin, base_cos), 0.0)
        b = jnp.where(keep, jnp.where(is_sine, -base_cos, base_sin), 0.0)
        for t in range(8):
            harmonic_ref[block * 8 + r, t * 8 : (t + 1) * 8, :] = (
                a * step_cos[t : t + 1, :] - b * step_sin[t : t + 1, :]
            )


def gather_rows(values_ref, node, elem):
    index = jnp.broadcast_to(elem, (8, 128))
    node = jnp.broadcast_to(node, (8, 128))
    acc = [jnp.zeros((8, 128), F32) for _ in range(8)]
    for a in range(NODES):
        mask = node == a
        for c in range(8):
            taken = take_lanes(values_ref[a * 64 + c * 8 : a * 64 + c * 8 + 8, :], index)
            acc[c] = jnp.where(mask, taken, acc[c])
    return acc


MATRIX_GROUPS, LANE_GROUPS = 6, 2


def keep_pieces(values, a, pieces_ref):
    rows = slice((a // 2) * 64, (a // 2) * 64 + 64)
    lane = (a % 2) * 128
    high, low = split2(values)
    pieces_ref[rows, lane : lane + 128] = high
    pieces_ref[rows, 256 + lane : 384 + lane] = low


def slot_hots(node_ref, elem_ref, hot_ref):
    def body(g, carry):
        lane = (node_ref[pl.ds(g, 1), :] & 1) * 128 + elem_ref[pl.ds(g, 1), :]
        hot_ref[g] = hot(iota((256, 128), 0) == lane)
        return carry

    lax.fori_loop(0, ALL_GROUPS, body, 0)


def fill_table(values_ref, pieces_ref, hot_ref, node_ref, elem_ref, table_ref):
    def body(t, carry):
        first = t * (MATRIX_GROUPS + LANE_GROUPS)
        right = jnp.concatenate([hot_ref[first + k] for k in range(MATRIX_GROUPS)], axis=1)
        out = dot(pieces_ref[...], jnp.concatenate([right, right], axis=0))
        for k in range(LANE_GROUPS):
            g = first + MATRIX_GROUPS + k
            acc = gather_rows(values_ref, node_ref[pl.ds(g, 1), :], elem_ref[pl.ds(g, 1), :])
            for c in range(8):
                table_ref[g, c * 8 : (c + 1) * 8, :] = acc[c]
        for k in range(MATRIX_GROUPS):
            g = first + k
            pair = node_ref[pl.ds(g, 1), :] >> 1
            acc = jnp.zeros((COLS, 128), F32)
            for a in range(PAIRS):
                acc = jnp.where(
                    pair == a, out[a * 64 : (a + 1) * 64, k * 128 : (k + 1) * 128], acc)
            table_ref[g] = acc
        return carry

    lax.fori_loop(0, GROUPS // (MATRIX_GROUPS + LANE_GROUPS), body, 0)


def sample_nodes(table_ref, local_ref, meta_ref, block, harmonic_ref):
    rows = []
    for r in range(8):
        row = block * 8 + r
        group = lax.clamp(0, meta_ref[block * 4 + r // 2, 0], GROUPS)
        local = jnp.broadcast_to(local_ref[pl.ds(row, 1), :], (8, 128))
        index = local & 127
        second = local > 127
        acc = jnp.zeros((8, 128), F32)
        for c in range(8):
            columns = slice(c * 8, (c + 1) * 8)
            taken = jnp.where(
                second,
                take_lanes(table_ref[group + 1, columns, :], index),
                take_lanes(table_ref[group, columns, :], index),
            )
            acc = acc + taken * harmonic_ref[row, columns, :]
        rows.append(jnp.sum(acc, axis=0, keepdims=True))
    return jnp.concatenate(rows, axis=0)


def small_stack(matrix):
    high, low = split2(matrix)
    return jnp.concatenate([high, high, low], axis=1)


def compute_force(j, half, values_ref, deriv_ref, radial_ref, shear_ref, force_ref):
    deriv = deriv_ref[...]
    stack = small_stack(deriv[0:32, 0:32])
    stack_t = small_stack(deriv.T[0:32, 0:32])
    radial = jnp.concatenate([radial_ref[...], jnp.zeros((7, 128), F32)], axis=0)
    radial = jnp.concatenate([radial] * 16, axis=1)
    shear = shear_ref[...]
    first = lax.rem(j, 4) * 64

    def times(left, x):
        high, low = split2(x)
        return dot(left, jnp.concatenate([high, low, high], axis=0))

    def body(k, carry):
        x = jnp.concatenate(
            [values_ref[pl.ds(k * 16 + c, 32, stride=64), :] for c in range(16)], axis=1
        )
        back = times(stack_t, times(stack, x) * radial)
        for c in range(16):
            wave = (first + k * 16 + c).astype(F32) * (2.0 / MODES)
            lanes = slice(c * 128, (c + 1) * 128)
            force_ref[pl.ds(k * 16 + c, NODES, stride=64), :] = (
                -back[0:NODES, lanes] - shear * (wave * wave) * x[0:NODES, lanes]
            )
        return carry

    lax.fori_loop(2 * half, 2 * half + 2, body, 0)


def edge_forces(force_ref, node_ref, elem_ref, edge_ref):
    def body(g, carry):
        acc = gather_rows(
            force_ref, node_ref[pl.ds(GROUPS + g, 1), :], elem_ref[pl.ds(GROUPS + g, 1), :]
        )
        for c in range(8):
            edge_ref[g, c * 8 : (c + 1) * 8, :] = acc[c]
        return carry

    lax.fori_loop(0, 4, body, 0)


def row_reactions(drives, block, carry, local_ref, shift_ref, harmonic_ref, high_ref, low_ref):
    for k in range(4):
        chunk = block * 4 + k
        pieces, hots = [], []
        for odd in range(2):
            r = 2 * k + odd
            pieces.append(split2(harmonic_ref[block * 8 + r] * drives[r : r + 1, :]))
            hots.append(hot(iota((256, 128), 0) == local_ref[pl.ds(block * 8 + r, 1), :]))
        left = jnp.concatenate(
            [
                jnp.concatenate([pieces[0][p], pieces[1][p]], axis=1) for p in range(2)
            ],
            axis=0,
        )
        out = dot_nt(left, jnp.concatenate(hots, axis=1))
        out = out[0:COLS] + out[COLS : 2 * COLS]
        here = carry[0] + out[:, 0:128]
        there = carry[1] + out[:, 128:256]
        high, low = split2(here)
        high_ref[chunk] = high
        low_ref[chunk] = low
        moved = jnp.broadcast_to(shift_ref[pl.ds(chunk, 1), :], (COLS, 128)) > 0
        carry = (jnp.where(moved, there, here), jnp.where(moved, 0.0, there))
    return carry


def scatter_rows(sources, first, node_ref, hot_ref, high_ref, low_ref, left_ref, sum_ref):
    rights = []
    for h in range(4):
        pair = node_ref[pl.ds(first + h, 1), :] >> 1
        high = high_ref[sources[h]]
        low = low_ref[sources[h]]
        for a in range(PAIRS):
            mask = jnp.broadcast_to(hot(pair == a), (COLS, 128))
            rows = slice(a * 64, (a + 1) * 64)
            left_ref[rows, h * 128 : (h + 1) * 128] = high * mask
            left_ref[rows, 512 + h * 128 : 640 + h * 128] = low * mask
        rights.append(hot_ref[first + h])
    sum_ref[...] += dot_nt(left_ref[...], jnp.concatenate(rights + rights, axis=1))


def advance(j, now_ref, before_ref, force_ref, sum_ref, mass_ref, modes_ref, next_ref,
            pieces_ref=None):
    order = lax.rem(j, 4) * 64 + iota((COLS, 128), 0)
    live = order < modes_ref[...]
    scale = STEP_SCALE / mass_ref[...]
    for a in range(NODES):
        rows = slice(a * 64, (a + 1) * 64)
        pair = a // 2
        lanes = slice((a % 2) * 128, (a % 2) * 128 + 128)
        total = force_ref[rows, :] + sum_ref[pair * 64 : (pair + 1) * 64, lanes]
        after = 2.0 * now_ref[rows, :] - before_ref[rows, :]
        after = after + jnp.where(live, scale[a : a + 1, :], 0.0) * total
        next_ref[rows, :] = after
        if pieces_ref is not None:
            keep_pieces(after, a, pieces_ref)


INPUTS = 18
VALUES = 11
PADDED = 32 * COLS


def whole_kernel(*refs):
    hbm = refs[:INPUTS]
    out_ref, box_out_ref = refs[INPUTS : INPUTS + 2]
    vmem = refs[INPUTS + 2 : 2 * INPUTS + 2]
    (
        fields, dest_ref, send_ref, node_ref, elem_ref, received, share, shared, harmonic_ref,
        table_ref, force_ref, next_ref, last_ref, high_ref, low_ref, left_ref, sum_ref,
        edge_ref, edges, partial, sums, drive, drives, ways, returned, box_last,
        pieces_ref, hot_ref, square_ref, start_ref, count_ref, meta_ref, shift_ref, local_ref,
        meta_smem, meta_sem,
        load_sem, send_sem, recv_sem, share_send, share_recv, edge_send, edge_recv,
        sum_send, sum_recv, drive_send, drive_recv, way_send, way_recv, out_sem,
    ) = refs[2 * INPUTS + 2 :]
    (
        angle_ref, slot_ref, spring_ref, mass_ref, weight_ref, now_ref, before_ref,
        rows_ref, target_ref, lower_ref, upper_ref, value_ref, old_ref, deriv_ref,
        radial_ref, shear_ref, node_mass_ref, modes_ref,
    ) = vmem
    i = lax.axis_index("mer")
    j = lax.axis_index("box")
    above = lax.rem(i + 1, MER)
    below = lax.rem(i + MER - 1, MER)

    def landing(k):
        if k == VALUES:
            return value_ref.at[0 : NODES * COLS]
        return vmem[k]

    loads = [pltpu.make_async_copy(hbm[k], landing(k), load_sem.at[k]) for k in range(INPUTS)]
    for load in loads[:7]:
        load.start()
    barrier = pltpu.get_barrier_semaphore()
    for o in range(1, MER):
        pl.semaphore_signal(
            barrier, inc=1, device_id=(lax.rem(i + o, MER), j), device_id_type=MESH)
    for o in range(1, BOX):
        pl.semaphore_signal(
            barrier, inc=1, device_id=(i, lax.rem(j + o, BOX)), device_id_type=MESH)

    for load in loads[7:]:
        load.start()

    def way(source, target, send, recv, device):
        return pltpu.make_async_remote_copy(
            src_ref=source, dst_ref=target, send_sem=send, recv_sem=recv,
            device_id=device, device_id_type=MESH)

    def to_part(o):
        q = lax.rem(i + o, MER)
        return way(send_ref.at[lax.div(q, 2)], received.at[i], send_sem.at[o], recv_sem.at[o], (q, j))

    def to_share(o):
        q = lax.rem(j + o, BOX)
        return way(share, shared.at[j], share_send.at[o], share_recv.at[o], (i, q))

    def to_sum(step, o):
        q = lax.rem(j + BOX - o, BOX)
        return way(partial.at[step, q], sums.at[step, o],
                   sum_send.at[step, o], sum_recv.at[step, o], (i, q))

    def to_drive(step, o):
        q = lax.rem(j + o, BOX)
        return way(drive.at[step], drives.at[step, j],
                   drive_send.at[step, o], drive_recv.at[step, o], (i, q))

    def to_back(o):
        q = lax.rem(i + o, MER)
        return way(ways.at[lax.div(q, 2)], returned.at[i], way_send.at[o], way_recv.at[o], (q, j))

    def to_edges(step):
        return (
            way(edge_ref.at[step, 2:4], edges.at[step, 0:2],
                edge_send.at[step, 0], edge_recv.at[step, 0], (above, j)),
            way(edge_ref.at[step, 0:2], edges.at[step, 2:4],
                edge_send.at[step, 1], edge_recv.at[step, 1], (below, j)),
        )

    def repeat(first, last, work):
        def body(o, carry):
            work(o)
            return carry

        lax.fori_loop(first, last, body, 0)

    for load in loads[:7]:
        load.wait()
    order_nodes([ref[...] for ref in vmem[:7]], dest_ref, send_ref, fields)
    pl.semaphore_wait(barrier, MER + BOX - 2)
    repeat(1, MER, lambda o: to_part(o).start())
    received[i] = send_ref[lax.div(i, 2)]
    for load in loads[7:]:
        load.wait()
    row_table(rows_ref[...], target_ref[...], (lower_ref[...], upper_ref[...]), node_ref, elem_ref,
              start_ref, count_ref, meta_ref, shift_ref)
    meta = pltpu.make_async_copy(meta_ref, meta_smem, meta_sem.at[0])
    meta.start()
    slot_hots(node_ref, elem_ref, hot_ref)
    square_ref[...] = jnp.zeros_like(square_ref)
    square_ref[0:NODES, 0:NODES] = deriv_ref[...]
    for ref in (value_ref, next_ref):
        ref[NODES * COLS : PADDED, :] = jnp.zeros((PADDED - NODES * COLS, ELEMS), F32)
    for a in range(NODES):
        keep_pieces(value_ref[a * COLS : (a + 1) * COLS, :], a, pieces_ref)
    for lane in (128, 384):
        pieces_ref[(PAIRS - 1) * COLS : PAIRS * COLS, lane : lane + 128] = jnp.zeros(
            (COLS, 128), BF16)
    table_ref[GROUPS : GROUPS + 2] = jnp.zeros((2, COLS, 128), F32)
    meta.wait()

    repeat(1, MER, lambda o: to_part(o).wait_recv())
    half = lax.rem(i, 2)
    own = []
    for f in range(7):
        even = jnp.concatenate([received[2 * r, f : f + 1, :] for r in range(8)], axis=0)
        odd = jnp.concatenate([received[2 * r + 1, f : f + 1, :] for r in range(8)], axis=0)
        own.append(halves(even, odd, half))
    share[0] = own[0]
    share[1] = own[1]
    repeat(1, BOX, lambda o: to_share(o).start())
    shared[j] = share[...]
    spring, mass, weight, box_now, box_before = own[2:]

    def first_forces(ref):
        compute_force(j, 0, ref, square_ref, radial_ref, shear_ref, force_ref)

    def forces(step, ref):
        compute_force(j, 1, ref, square_ref, radial_ref, shear_ref, force_ref)
        edge_forces(force_ref, node_ref, elem_ref, edge_ref.at[step])
        for copy in to_edges(step):
            copy.start()

    def sample_block(step, block):
        partial[step, block] = sample_nodes(table_ref, local_ref, meta_smem, block, harmonic_ref)

    def pulls(step, now):
        sample = partial[step, j]
        for o in range(1, BOX):
            to_sum(step, o).wait_recv()
            sample = sample + sums[step, o]
        pull = spring * (sample - now)
        drive[step] = -weight * pull
        repeat(1, BOX, lambda o: to_drive(step, o).start())
        drives[step, j] = drive[step]
        return pull

    def reactions(step):
        sum_ref[...] = jnp.zeros_like(sum_ref)

        def work(k, carry):
            for block in (2 * k, 2 * k + 1):
                @pl.when(block != j)
                def _():
                    to_drive(step, lax.rem(j + BOX - block, BOX)).wait_recv()

            for block in (2 * k, 2 * k + 1):
                carry = row_reactions(drives[step, block], block, carry, local_ref, shift_ref,
                                      harmonic_ref, high_ref, low_ref)
            return carry

        nothing = jnp.zeros((COLS, 128), F32)
        lax.fori_loop(0, BOX // 2, work, (nothing, nothing))

        def scatter(t, carry):
            sources = [
                lax.clamp(0, meta_smem[CHUNKS, t * 4 + h], CHUNKS - 1) for h in range(4)
            ]
            scatter_rows(sources, t * 4, node_ref, hot_ref, high_ref, low_ref, left_ref, sum_ref)
            return carry

        lax.fori_loop(0, GROUPS // 4, scatter, 0)
        for copy in to_edges(step):
            copy.wait_recv()
        for g in range(4):
            ghost = (i == 0) if g < 2 else (i == MER - 1)
            high, low = split2(jnp.where(ghost, 0.0, edges[step, g]))
            high_ref[CHUNKS + g] = high
            low_ref[CHUNKS + g] = low
        scatter_rows([CHUNKS + h for h in range(4)], GROUPS, node_ref, hot_ref, high_ref,
                     low_ref, left_ref, sum_ref)

    fill_table(value_ref, pieces_ref, hot_ref, node_ref, elem_ref, table_ref)

    def enter(block):
        rows = pl.ds(pl.multiple_of(block * 8, 8), 8)
        places = shared[block, 1].astype(I32)
        filled = jnp.where(places < count_ref[rows, :], 1, 0)
        local_ref[rows, :] = jnp.where(filled > 0, start_ref[rows, :] + places, 0)
        harmonics(j, shared[block, 0], filled, block, harmonic_ref)
        sample_block(0, block)

    enter(j)

    def enter_peer(o):
        to_share(o).wait_recv()
        enter(lax.rem(j + BOX - o, BOX))
        to_sum(0, o).start()

    repeat(1, BOX, enter_peer)
    first_forces(value_ref)
    pull = pulls(0, box_now)
    forces(0, value_ref)
    box_next = 2.0 * box_now - box_before + STEP_SCALE * pull / mass
    reactions(0)
    advance(j, value_ref, old_ref, force_ref, sum_ref, node_mass_ref, modes_ref, next_ref,
            pieces_ref)

    fill_table(next_ref, pieces_ref, hot_ref, node_ref, elem_ref, table_ref)

    def sample_peer(o):
        sample_block(1, lax.rem(j + BOX - o, BOX))
        to_sum(1, o).start()

    repeat(1, BOX, sample_peer)
    sample_block(1, j)
    first_forces(next_ref)
    pull = pulls(1, box_next)
    box_after = 2.0 * box_next - box_now + STEP_SCALE * pull / mass
    for m in range(8):
        ways[m] = jnp.broadcast_to(box_after[m : m + 1, :], (8, 128))
    forces(1, next_ref)
    repeat(1, MER, lambda o: to_back(o).start())
    returned[i] = ways[lax.div(i, 2)]
    reactions(1)
    advance(j, next_ref, value_ref, force_ref, sum_ref, node_mass_ref, modes_ref, out_ref)

    repeat(1, MER, lambda o: to_back(o).wait_recv())
    even = jnp.concatenate([returned[2 * r, 0:1, :] for r in range(8)], axis=0)
    odd = jnp.concatenate([returned[2 * r + 1, 0:1, :] for r in range(8)], axis=0)
    box = halves(even, odd, half)
    line = jnp.concatenate([box[m : m + 1, :] for m in range(8)], axis=1)
    pieces = jnp.concatenate([piece.astype(F32) for piece in split3(line)], axis=0).astype(BF16)
    for r in range(8):
        out = dot(pieces, hot(iota((1024, 128), 0) == dest_ref[r : r + 1, :]))
        box_last[r : r + 1, :] = out[0:1] + (out[1:2] + out[2:3])
    box_out_ref[...] = box_last[...]

    def sent(o):
        to_share(o).wait_send()
        for step in range(2):
            to_sum(step, o).wait_send()
            to_drive(step, o).wait_send()

    repeat(1, BOX, sent)

    def sent_far(o):
        to_part(o).wait_send()
        to_back(o).wait_send()

    repeat(1, MER, sent_far)
    for step in range(2):
        for copy in to_edges(step):
            copy.wait_send()


def hand_over_kernel(final_ref, box_ref, out_ref, box_out_ref, sem):
    copies = [
        pltpu.make_async_copy(final_ref, out_ref, sem.at[0]),
        pltpu.make_async_copy(box_ref, box_out_ref, sem.at[1]),
    ]
    for copy in copies:
        copy.start()
    for copy in copies:
        copy.wait()


def per_device(
    annulus, annulus_prev, derivative, radial_modulus, shear_modulus, node_mass, element_modes,
    upper_rows, lower_rows, coupling_rows, coupling_target, box_field, box_prev, box_angle,
    box_spring, box_mass, box_weight, box_slot,
):
    flat = NODES * COLS
    args = [
        x.reshape(8, 128)
        for x in (box_angle, box_slot, box_spring, box_mass, box_weight, box_field, box_prev)
    ] + [
        coupling_rows.reshape(16, 128), coupling_target.reshape(16, 128),
        lower_rows.reshape(2, 128), upper_rows.reshape(2, 128),
        annulus.reshape(flat, ELEMS), annulus_prev.reshape(flat, ELEMS), derivative,
        radial_modulus, shear_modulus, node_mass, element_modes.reshape(1, ELEMS),
    ]
    vmem = pltpu.VMEM
    scratch = [vmem(x.shape, x.dtype) for x in args]
    scratch[VALUES] = vmem((PADDED, ELEMS), F32)
    scratch += [
        vmem((8, 8, 128), F32),
        vmem((8, 128), I32),
        vmem((8, 8, 128), F32),
        vmem((ALL_GROUPS, 128), I32),
        vmem((ALL_GROUPS, 128), I32),
        vmem((MER, 8, 128), F32),
        vmem((2, 8, 128), F32),
        vmem((BOX, 2, 8, 128), F32),
        vmem((ROWS, COLS, 128), F32),
        vmem((GROUPS + 2, COLS, 128), F32),
        vmem((flat, ELEMS), F32),
        vmem((PADDED, ELEMS), F32),
        vmem((flat, ELEMS), F32),
        vmem((CHUNKS + 4, COLS, 128), BF16),
        vmem((CHUNKS + 4, COLS, 128), BF16),
        vmem((PAIRS * COLS, 1024), BF16),
        vmem((PAIRS * COLS, 256), F32),
        vmem((2, 4, COLS, 128), F32),
        vmem((2, 4, COLS, 128), F32),
        vmem((2, BOX, 8, 128), F32),
        vmem((2, BOX, 8, 128), F32),
        vmem((2, 8, 128), F32),
        vmem((2, BOX, 8, 128), F32),
        vmem((8, 8, 128), F32),
        vmem((MER, 8, 128), F32),
        vmem((8, 128), F32),
        vmem((PAIRS * COLS, 512), BF16),
        vmem((ALL_GROUPS, 256, 128), BF16),
        vmem((128, 128), F32),
        vmem((ROWS, 128), I32),
        vmem((ROWS, 128), I32),
        vmem((CHUNKS + 8, 128), I32),
        vmem((CHUNKS, 128), I32),
        vmem((ROWS, 128), I32),
        pltpu.SMEM((CHUNKS + 8, 128), I32),
        pltpu.SemaphoreType.DMA((1,)),
    ]
    dma = pltpu.SemaphoreType.DMA
    scratch += [dma((INPUTS,))] + [dma((MER,))] * 2 + [dma((BOX,))] * 2 + [dma((2, 2))] * 2
    scratch += [dma((2, BOX))] * 4 + [dma((MER,))] * 2 + [dma((2,))]
    any_space = pl.BlockSpec(memory_space=pl.ANY)
    final, box_out = pl.pallas_call(
        whole_kernel,
        out_shape=[jax.ShapeDtypeStruct((flat, ELEMS), F32), jax.ShapeDtypeStruct((8, 128), F32)],
        in_specs=[pl.BlockSpec(memory_space=pltpu.HBM)] * INPUTS,
        out_specs=[pl.BlockSpec(memory_space=pltpu.VMEM)] * 2,
        scratch_shapes=scratch,
        compiler_params=pltpu.CompilerParams(
            vmem_limit_bytes=44 << 20, collective_id=0, has_side_effects=True),
        name="coupled_steps",
    )(*[pltpu.with_memory_space_constraint(x, pltpu.HBM) for x in args])
    final, box_out = pl.pallas_call(
        hand_over_kernel,
        out_shape=[jax.ShapeDtypeStruct((flat, ELEMS), F32), jax.ShapeDtypeStruct((8, 128), F32)],
        in_specs=[pl.BlockSpec(memory_space=pltpu.VMEM)] * 2,
        out_specs=[any_space] * 2,
        scratch_shapes=[dma((2,))],
        compiler_params=pltpu.CompilerParams(vmem_limit_bytes=4 << 20),
        name="hand_over",
    )(final, box_out)
    return final.reshape(NODES, COLS, ELEMS), box_out.reshape(1024)


def solution(mesh):
    mer_box = P(("mer", "box"))
    in_specs = (
        P(None, "box", "mer"), P(None, "box", "mer"), P(),
        P(None, "mer"), P(None, "mer"), P(None, "mer"),
        P("mer"), P("mer"), P("mer"), P("mer"), P("mer", None),
        mer_box, mer_box, mer_box, mer_box, mer_box, mer_box, mer_box,
    )
    return jax.shard_map(
        per_device, mesh=mesh, in_specs=in_specs,
        out_specs=(P(None, "box", "mer"), mer_box), check_vma=False,
    )
```
